32 devices in a mesh: ctx: 8 (over z, x), wsh: 4 (over y, core).
Axes of the slice: x: 2, y: 2, z: 4, core: 2. Of those that a mesh axis runs over, the one named last changes fastest.
Arguments:
- tokens: bfloat16 [4, 4096, 512], P('wsh', 'ctx'), may hold values from -6 to 6
- segments: int32 [4, 4096], P('wsh', 'ctx'), may hold values from 0 to 7, as said below
- deal_order: int32 [32], replicated, may hold values from 0 to 31, as said below
- cotangent: bfloat16 [4, 4096, 512], P('wsh', 'ctx'), may hold values from -6 to 6
- proj_weight: bfloat16 [512, 2176], P('wsh'), may hold values from -0.25 to 0.25
- value_weight: bfloat16 [512, 1024], P('wsh'), may hold values from -0.25 to 0.25
- merge_weight: bfloat16 [1024, 512], P('wsh'), may hold values from -0.375 to 0.375
- ffn_up: bfloat16 [512, 1024], P('wsh'), may hold values from -0.25 to 0.25
- ffn_down: bfloat16 [1024, 512], P('wsh'), may hold values from -0.1875 to 0.1875
- norm_gain: bfloat16 [512], P('wsh'), may hold values from 0.5 to 1.5
- ffn_gain: bfloat16 [512], P('wsh'), may hold values from 0.5 to 1.5
- skip_gain: bfloat16 [512], P('wsh'), may hold values from -3 to 3
- ema_decay: bfloat16 [512, 16], P('wsh'), may hold values from 3.5 to 12
- ema_input: bfloat16 [512, 16], P('wsh'), may hold values from -5 to 5
- ema_output: bfloat16 [512, 16], P('wsh'), may hold values from -1.5 to 1.5
- query_key: bfloat16 [128, 3], P('wsh'), may hold values from -8 to 8
Outputs:
- output: bfloat16 [4, 4096, 512], P('wsh', 'ctx')
- input_grad: bfloat16 [4, 4096, 512], P('wsh', 'ctx')
- grad_proj: float32 [512, 2176], P('wsh')
- grad_value: float32 [512, 1024], P('wsh')
- grad_merge: float32 [1024, 512], P('wsh')
- grad_up: float32 [512, 1024], P('wsh')
- grad_down: float32 [1024, 512], P('wsh')
- grad_norm: float32 [512], P('wsh')
- grad_ffn_gain: float32 [512], P('wsh')
- grad_skip: float32 [512], P('wsh')
- grad_decay: float32 [512, 16], P('wsh')
- grad_ema_input: float32 [512, 16], P('wsh')
- grad_ema_output: float32 [512, 16], P('wsh')
- grad_query_key: float32 [128, 3], P('wsh')
The draws below stay inside these ranges and needn't reach their ends.
Inputs may be any that keep to these rules, and one draw needn't show every extreme that they name: `deal_order`: a permutation, the same for every sequence. `segments`: in each sequence, read in sequence order, the ids never fall and rise by one at each document start, the first token has id 0 and the last token has the largest id.
All inputs are finite; a program needn't handle non-finite values.
Results may differ from the reference program's by a relative error of at most 0.04.
Values may be sent and summed in bfloat16 or wider, within the bound.
No kernel may reach another device: no remote copies, remote signals or barrier semaphores. Data moves between devices by JAX's collectives and lax.ppermute only.
A program may use at most 256 MiB of HBM per device.

```python
import jax
import jax.numpy as jnp
from jax import lax

D = 512
Z = 128
VALUE_WIDTH = 1024
NDIM = 16
BLOCK_TOKENS = 128
FF = 1024
BLOCK_COUNT = 32
LEN = 4096
SEQS = 4


def dealing_of(key):
    return jax.random.permutation(jax.random.fold_in(key, 31), BLOCK_COUNT).astype(jnp.int32)


def label_rows(key):
    doc_count = max(2, LEN // 512)
    first_key, second_key = jax.random.split(jax.random.fold_in(key, 37))
    factor = jax.random.randint(first_key, (SEQS, doc_count), 16, 32)
    powers = jax.random.randint(second_key, (SEQS, doc_count), 0, 5)
    weights = factor * jnp.left_shift(jnp.ones_like(powers), powers)
    running = jnp.cumsum(weights, axis=1)
    totals = running[:, -1:]
    offsets = jnp.arange(1, doc_count, dtype=jnp.int32)[None, :]
    ends = running[:, :-1] * (LEN - doc_count) // totals + offsets
    places = jnp.arange(LEN, dtype=jnp.int32)
    doc_ids = jax.vmap(lambda bound_row: jnp.searchsorted(bound_row, places, side='right'))(ends)
    return doc_ids.astype(jnp.int32)


def draw_deal_order(key, part):
    return dealing_of(key)


def draw_segments(key, part):
    dealing = dealing_of(key)
    doc_ids = label_rows(key)
    return doc_ids.reshape(SEQS, BLOCK_COUNT, BLOCK_TOKENS)[:, dealing, :].reshape(SEQS, LEN)


def block_scale(key, extent, shards, least, high):
    loudness = 1.0
    for axis_at, blocks in shards:
        draws = jax.random.uniform(jax.random.fold_in(jax.random.fold_in(key, 6), axis_at), (blocks,), jnp.float32, least / len(shards), high / len(shards))
        loudness = loudness * jnp.repeat(jnp.exp(draws), extent[axis_at] // blocks).reshape((-1,) + (1,) * (len(extent) - 1 - axis_at))
    return loudness


def scatter_about(stream_key, shape, scale, limit, cuts=(), kind=jnp.bfloat16):
    gain = block_scale(stream_key, shape, cuts, -0.22, 0.18) if cuts else 1.0
    drawn = jax.random.normal(stream_key, shape, jnp.float32) * scale * gain
    return jnp.minimum(jnp.maximum(drawn, -limit), limit).astype(kind)


def setup_inputs(seed: int = 0) -> dict:
    splits = jax.random.split(jax.random.key(seed), 17)
    return {
        "tokens": scatter_about(splits[0], (SEQS, LEN, D), 1.0, 6.0, ((0, 4), (1, 8))),
        "segments": draw_segments(jax.random.fold_in(splits[16], 71), 0),
        "deal_order": draw_deal_order(jax.random.fold_in(splits[16], 71), 0),
        "cotangent": scatter_about(splits[3], (SEQS, LEN, D), 1.0, 6.0, ((0, 4), (1, 8))),
        "proj_weight": scatter_about(splits[4], (D, Z + VALUE_WIDTH + 2 * D), D ** -0.5, 0.25, ((0, 4),)),
        "value_weight": scatter_about(splits[5], (D, VALUE_WIDTH), D ** -0.5, 0.25, ((0, 4),)),
        "merge_weight": scatter_about(splits[6], (VALUE_WIDTH, D), (VALUE_WIDTH // 4) ** -0.5, 0.375, ((0, 4),)),
        "ffn_up": scatter_about(splits[7], (D, FF), D ** -0.5, 0.25, ((0, 4),)),
        "ffn_down": scatter_about(splits[8], (FF, D), FF ** -0.5, 0.1875, ((0, 4),)),
        "norm_gain": jnp.clip(1.0 + 0.1 * jax.random.normal(splits[9], (D,), jnp.float32), 0.5, 1.5).astype(jnp.bfloat16),
        "ffn_gain": jnp.clip(1.0 + 0.1 * jax.random.normal(splits[10], (D,), jnp.float32), 0.5, 1.5).astype(jnp.bfloat16),
        "skip_gain": scatter_about(splits[11], (D,), 0.5, 3.0, ((0, 4),)),
        "ema_decay": jnp.clip(3.5 + 8.5 * jax.random.uniform(splits[12], (D, NDIM), jnp.float32) ** block_scale(splits[12], (D, NDIM), ((0, 4),), -0.2, 0.2), 3.5, 12.0).astype(jnp.bfloat16),
        "ema_input": scatter_about(splits[13], (D, NDIM), 1.0, 5.0, ((0, 4),)),
        "ema_output": scatter_about(splits[14], (D, NDIM), 0.25, 1.5, ((0, 4),)),
        "query_key": scatter_about(splits[15], (Z, 3), 2.0, 8.0, ((0, 4),)),
    }


@jax.custom_vjp
def reduced_precision(v):
    return lax.optimization_barrier(v.astype(jnp.bfloat16)).astype(jnp.float32)

@jax.custom_vjp
def reduced_backward(v):
    return v

def low_keep(v):
    return (reduced_precision(v), None)

def low_pass(kept, grad):
    return (grad,)

def back_keep(v):
    return (v, None)

def back_low(kept, grad):
    return (reduced_precision(grad),)
reduced_precision.defvjp(low_keep, low_pass)
reduced_backward.defvjp(back_keep, back_low)

def product(left_op, right_op):
    return jnp.dot(left_op, right_op, precision=lax.Precision.HIGHEST)

def swish_unit(value_rows):
    return value_rows * jax.nn.sigmoid(value_rows)

def layer_norm(value_rows, gain_vec):
    centred = value_rows - lax.optimization_barrier(jnp.mean(value_rows, axis=-1, keepdims=True))
    spread = lax.optimization_barrier(jnp.mean(centred * centred, axis=-1, keepdims=True))
    return centred * lax.rsqrt(spread + 1e-05) * gain_vec

def combine(earlier, later):
    return (earlier[0] * later[0], later[0] * earlier[1] + later[1])

def ema_block(carried, normed, continuing, decay_rates, drives, readout):
    step_rates = continuing[:, None, None] * decay_rates[None]
    push_terms = normed[:, None, :] * drives[None]
    acc_rate, acc_push = lax.associative_scan(combine, (step_rates, push_terms), axis=0)
    ema_states = acc_rate * carried[None] + acc_push
    return (ema_states[-1], lax.optimization_barrier(jnp.sum(ema_states * readout[None], axis=1)))

def forward_one(token_rows, labels, proj_weight, value_weight, merge_weight, ffn_up, ffn_down, norm_gain, ffn_gain, skip_gain, ema_decay, ema_input, ema_output, query_key):
    sequence_length = token_rows.shape[0]
    normed = layer_norm(token_rows, norm_gain)
    normed_low = reduced_precision(normed)
    earlier = jnp.concatenate([labels[:1] - 1, labels[:-1]])
    continuing = (labels == earlier).astype(jnp.float32)
    decay_rates = jax.nn.sigmoid(ema_decay.T)
    drives = jnp.sqrt(jax.nn.sigmoid(-ema_decay.T) * (1.0 + decay_rates)) * ema_input.T
    readout = ema_output.T

    def step_fn(carried, pieces):
        return ema_block(carried, pieces[0], pieces[1], decay_rates, drives, readout)
    zero_state = jnp.zeros((NDIM, D), jnp.float32)
    _, ema_mix = lax.scan(jax.checkpoint(step_fn), zero_state, (normed.reshape(BLOCK_COUNT, BLOCK_TOKENS, D), continuing.reshape(BLOCK_COUNT, BLOCK_TOKENS)))
    active = swish_unit(ema_mix.reshape(sequence_length, D) + skip_gain * normed)
    projected = reduced_backward(product(reduced_precision(active), proj_weight))
    gate_up = jax.nn.sigmoid(projected[:, :D])
    shared = swish_unit(projected[:, D:D + Z])
    reset_gate = swish_unit(projected[:, D + Z:D + Z + VALUE_WIDTH])
    hidden_x = projected[:, D + Z + VALUE_WIDTH:]
    value_rows = reduced_precision(swish_unit(reduced_backward(product(normed_low, value_weight))))
    queries = reduced_precision(shared * query_key[:, 0] + query_key[:, 1])
    keys_all = reduced_precision(shared * query_key[:, 2])
    block_labels = labels.reshape(BLOCK_COUNT, BLOCK_TOKENS)
    causal = jnp.arange(BLOCK_TOKENS)[:, None] >= jnp.arange(BLOCK_TOKENS)[None, :]
    allowed = causal[None] & (block_labels[:, :, None] == block_labels[:, None, :])
    raw_scores = reduced_backward(jnp.einsum('nqz,nkz->nqk', queries.reshape(BLOCK_COUNT, BLOCK_TOKENS, Z), keys_all.reshape(BLOCK_COUNT, BLOCK_TOKENS, Z), precision=lax.Precision.HIGHEST))
    scores = jnp.where(allowed, raw_scores * Z ** (-0.5), -1e+30)
    row_peak = lax.optimization_barrier(jnp.max(scores, axis=-1, keepdims=True))
    exp_scores = jnp.exp(scores - row_peak)
    attention_weights = exp_scores / lax.optimization_barrier(jnp.sum(exp_scores, axis=-1, keepdims=True))
    attention_output = reduced_backward(jnp.einsum('lfz,lzw->lfw', reduced_precision(attention_weights), value_rows.reshape(BLOCK_COUNT, BLOCK_TOKENS, VALUE_WIDTH), precision=lax.Precision.HIGHEST)).reshape(sequence_length, VALUE_WIDTH)
    merged = reduced_backward(product(reduced_precision(reset_gate * attention_output), merge_weight))
    hidden = swish_unit(hidden_x + merged)
    residual = token_rows + gate_up * (hidden - token_rows)
    ffn_inner = reduced_precision(swish_unit(reduced_backward(product(reduced_precision(layer_norm(residual, ffn_gain)), ffn_up))))
    return residual + reduced_backward(product(ffn_inner, ffn_down))

def reference(tokens, segments, deal_order, cotangent, proj_weight, value_weight, merge_weight, ffn_up, ffn_down, norm_gain, ffn_gain, skip_gain, ema_decay, ema_input, ema_output, query_key):
    positions = jnp.arange(BLOCK_COUNT, dtype=jnp.int32)
    inverse = jnp.zeros((BLOCK_COUNT,), jnp.int32).at[deal_order].set(positions)

    def to_sequence(tensor):
        blocks_view = tensor.reshape((SEQS, BLOCK_COUNT, BLOCK_TOKENS) + tensor.shape[2:])
        return blocks_view[:, inverse].reshape(tensor.shape)

    def to_dealt(tensor):
        blocks_view = tensor.reshape((SEQS, BLOCK_COUNT, BLOCK_TOKENS) + tensor.shape[2:])
        return blocks_view[:, deal_order].reshape(tensor.shape)
    labels = to_sequence(segments)
    floats = (to_sequence(tokens.astype(jnp.float32)), proj_weight.astype(jnp.float32), value_weight.astype(jnp.float32), merge_weight.astype(jnp.float32), ffn_up.astype(jnp.float32), ffn_down.astype(jnp.float32), norm_gain.astype(jnp.float32), ffn_gain.astype(jnp.float32), skip_gain.astype(jnp.float32), ema_decay.astype(jnp.float32), ema_input.astype(jnp.float32), ema_output.astype(jnp.float32), query_key.astype(jnp.float32))

    def whole_fn(token_rows, *weights):
        return lax.map(lambda seq_pair: forward_one(seq_pair[0], seq_pair[1], *weights), (token_rows, labels))
    result, pull_back = jax.vjp(whole_fn, *floats)
    gradients = pull_back(to_sequence(cotangent.astype(jnp.float32)))
    return (to_dealt(result).astype(jnp.bfloat16), to_dealt(gradients[0]).astype(jnp.bfloat16), gradients[1], gradients[2], gradients[3], gradients[4], gradients[5], gradients[6], gradients[7], gradients[8], gradients[9], gradients[10], gradients[11], gradients[12])
```

```python
import functools

import jax
import jax.numpy as jnp
from jax import lax
from jax.experimental import pallas as pl
from jax.experimental.pallas import tpu as pltpu
from jax.sharding import PartitionSpec as P

D = 512
Z = 128
VALUE_WIDTH = 1024
NDIM = 16
BLOCK_TOKENS = 128
FF = 1024
LANES = 128
GROUPS = D // LANES
PARTS = 8
F32 = jnp.float32
BF16 = jnp.bfloat16
EPS = 1e-05
SMALL_ROWS = 56


def swish_unit(v):
    return v * jax.nn.sigmoid(v)


def swish_slope(v):
    s = jax.nn.sigmoid(v)
    return s * (1.0 + v * (1.0 - s))


def decay_tables(par_ref):
    decay = par_ref[0:NDIM, :].astype(F32)
    rate = jax.nn.sigmoid(decay)
    width = jnp.sqrt(jax.nn.sigmoid(-decay) * (1.0 + rate))
    return decay, rate, width


def power_of_rate(decay, count):
    return jnp.exp(-count * jnp.log1p(jnp.exp(-decay)))


def spread(table, j, g):
    return jnp.broadcast_to(table[j : j + 1, g * LANES : (g + 1) * LANES], (PARTS, LANES))


def put_runs(ref, value, run):
    stride = ref.shape[-2] // PARTS
    if len(ref.shape) == 2:
        for h in range(PARTS):
            ref[h * stride : h * stride + run, :] = value[h * run : (h + 1) * run, :]
    else:
        for g in range(GROUPS):
            for h in range(PARTS):
                ref[g, h * stride : h * stride + run, :] = value[
                    h * run : (h + 1) * run, g * LANES : (g + 1) * LANES
                ]


def get_runs(ref, run):
    stride = ref.shape[-2] // PARTS
    return jnp.concatenate(
        [
            jnp.concatenate([ref[g, h * stride : h * stride + run, :] for h in range(PARTS)], axis=0)
            for g in range(GROUPS)
        ],
        axis=1,
    )


def at_step(ref, t, g=None):
    stride = ref.shape[-2] // PARTS
    if g is None:
        return ref[pl.ds(t, PARTS, stride=stride), :]
    return ref[g, pl.ds(t, PARTS, stride=stride), :]


def set_step(ref, t, g, value):
    stride = ref.shape[-2] // PARTS
    ref[g, pl.ds(t, PARTS, stride=stride), :] = value


def column(ref, i):
    return jnp.broadcast_to(ref[:, i : i + 1], (ref.shape[0], LANES))


def front_kernel(run, tok_ref, par_ref, msk_ref, nrm_ref, mix_ref, end_ref, sum_ref, far_ref, xs, os, cont, head):
    x = tok_ref[...].astype(F32)
    centred = x - jnp.mean(x, axis=-1, keepdims=True)
    var = jnp.mean(centred * centred, axis=-1, keepdims=True)
    normed = centred * lax.rsqrt(var + EPS) * par_ref[48:49, :].astype(F32)
    nrm_ref[...] = normed
    put_runs(xs, normed, run)
    put_runs(cont, column(msk_ref, 0), run)
    put_runs(head, column(msk_ref, 1), run)
    decay, rate, width = decay_tables(par_ref)
    gain = par_ref[32:48, :].astype(F32) * width * par_ref[16:32, :].astype(F32)
    far_ref[...] = power_of_rate(decay, BLOCK_TOKENS)
    rate_run = power_of_rate(decay, run)
    head_end = at_step(head, run - 1)
    for g in range(GROUPS):
        rates = [spread(rate, j, g) for j in range(NDIM)]
        gains = [spread(gain, j, g) for j in range(NDIM)]

        def step(t, states, g=g, rates=rates, gains=gains):
            x_t = at_step(xs, t, g)
            c_t = at_step(cont, t)
            new = [(c_t * rates[j]) * states[j] + x_t for j in range(NDIM)]
            acc = gains[0] * new[0]
            for j in range(1, NDIM):
                acc = acc + gains[j] * new[j]
            set_step(os, t, g, acc)
            return tuple(new)

        zero = tuple(jnp.zeros((PARTS, LANES), F32) for _ in range(NDIM))
        ends = lax.fori_loop(0, run, step, zero, unroll=4)
        for j in range(NDIM):
            end_ref[j, :, g * LANES : (g + 1) * LANES] = ends[j]
            sum_ref[j, :, g * LANES : (g + 1) * LANES] = ends[j] + head_end * spread(
                rate_run, j, g
            ) * pltpu.roll(ends[j], 1, 0)
    mix_ref[...] = get_runs(os, run)


def scan_kernel(blocks, count, order_ref, got_ref, far_ref, out_ref, place):
    rows = far_ref.shape[0]

    def note(p, carry):
        place[order_ref[p]] = p
        return carry

    lax.fori_loop(0, count, note, 0)

    def step(k, carry):
        state, last_before = carry
        pos = place[k]
        dev, b = pos // blocks, pos % blocks
        got = got_ref[dev, b].astype(F32)
        first, last = got[rows : rows + 1, :], got[rows + 1 : rows + 2, :]
        state = jnp.where(first == last_before, state, 0.0)
        out_ref[dev, b] = state.astype(BF16)
        state = jnp.where(first == last, far_ref[...] * state, 0.0) + got[:rows, :]
        return state, last

    lax.fori_loop(0, count, step, (jnp.zeros((rows, LANES), F32), jnp.full((1, LANES), -1.0, F32)))


def back_scan_kernel(blocks, count, order_ref, got_ref, bnd_ref, far_ref, out_ref, place):
    rows = far_ref.shape[0]

    def note(p, carry):
        place[order_ref[p]] = p
        return carry

    lax.fori_loop(0, count, note, 0)

    def step(i, carry):
        state, first_after = carry
        pos = place[count - 1 - i]
        dev, b = pos // blocks, pos % blocks
        bnd = bnd_ref[dev, b].astype(F32)
        first, last = bnd[rows : rows + 1, :], bnd[rows + 1 : rows + 2, :]
        state = jnp.where(last == first_after, state, 0.0)
        out_ref[dev, b] = state.astype(BF16)
        state = jnp.where(first == last, far_ref[...] * state, 0.0) + got_ref[dev, b].astype(F32)
        return state, first

    lax.fori_loop(0, count, step, (jnp.zeros((rows, LANES), F32), jnp.full((1, LANES), -1.0, F32)))


def carry_kernel(run, mix_ref, nrm_ref, ent_ref, end_ref, par_ref, msk_ref, pre_ref, act_ref, low_ref, ein_ref, os, head):
    put_runs(head, column(msk_ref, 1), run)
    decay, rate, width = decay_tables(par_ref)
    gain = par_ref[32:48, :].astype(F32) * width * par_ref[16:32, :].astype(F32)
    rate_run = power_of_rate(decay, run)
    head_end = at_step(head, run - 1)
    per_block = BLOCK_TOKENS // run
    lead = lax.broadcasted_iota(jnp.int32, (PARTS, LANES), 0) % per_block == 0
    for g in range(GROUPS):
        gl = slice(g * LANES, (g + 1) * LANES)
        rates = [spread(rate, j, g) for j in range(NDIM)]
        start = []
        for j in range(NDIM):
            ent = ent_ref[j, :, gl]
            inner = pltpu.roll(end_ref[j, :, gl], 1, 0) + pltpu.roll(head_end, 1, 0) * spread(rate_run, j, g) * ent
            ent = jnp.where(lead, ent, inner)
            ein_ref[j, :, gl] = ent
            start.append(ent * spread(gain, j, g))

        def step(t, states, g=g, rates=rates):
            new = [rates[j] * states[j] for j in range(NDIM)]
            acc = new[0]
            for j in range(1, NDIM):
                acc = acc + new[j]
            set_step(os, t, g, acc * at_step(head, t))
            return tuple(new)

        lax.fori_loop(0, run, step, tuple(start), unroll=4)
    normed = nrm_ref[...]
    pre = mix_ref[...] + get_runs(os, run) + par_ref[50:51, :].astype(F32) * normed
    pre_ref[...] = pre
    act_ref[...] = swish_unit(pre).astype(BF16)
    low_ref[...] = normed.astype(BF16)


def adjoint_kernel(run, gact_ref, pre_ref, nrm_ref, ein_ref, par_ref, msk_ref, gn_ref, lead_ref, sum_ref, u_ref, v_ref, ve_ref, gs_ref, xs, gs, os, cont, head):
    normed = nrm_ref[...]
    g_mix = gact_ref[...] * swish_slope(pre_ref[...])
    gs_ref[...] = jnp.sum(g_mix * normed, axis=0, keepdims=True)
    put_runs(xs, normed, run)
    put_runs(gs, g_mix, run)
    put_runs(cont, column(msk_ref, 0), run)
    put_runs(head, column(msk_ref, 1), run)
    decay, rate, width = decay_tables(par_ref)
    gain = par_ref[32:48, :].astype(F32) * width * par_ref[16:32, :].astype(F32)
    rate_run = power_of_rate(decay, run)
    head_end = at_step(head, run - 1)
    zero = jnp.zeros((PARTS, LANES), F32)
    for g in range(GROUPS):
        gl = slice(g * LANES, (g + 1) * LANES)
        rates = [spread(rate, j, g) for j in range(NDIM)]
        gains = [spread(gain, j, g) for j in range(NDIM)]

        def back(i, carries, g=g, rates=rates, gains=gains):
            t = run - 1 - i
            g_t = at_step(gs, t, g)
            c_t = at_step(cont, t)
            new = []
            acc = None
            for j in range(NDIM):
                b = g_t + carries[j]
                term = gains[j] * b
                acc = term if acc is None else acc + term
                new.append((c_t * rates[j]) * b)
            set_step(os, t, g, acc)
            return tuple(new)

        ends = lax.fori_loop(0, run, back, (zero,) * NDIM, unroll=4)
        for j in range(NDIM):
            lead_ref[j, :, gl] = ends[j]
            sum_ref[j, :, gl] = ends[j] + head_end * spread(rate_run, j, g) * pltpu.roll(ends[j], PARTS - 1, 0)
        half = NDIM // 2
        for first in (0, half):
            picks = range(first, first + half)

            def ahead(t, carry, g=g, picks=picks, rates=rates):
                us, vs, uacc, vacc = carry
                g_t = at_step(gs, t, g)
                x_t = at_step(xs, t, g)
                c_t = at_step(cont, t)
                nu, nv, nua, nva = [], [], [], []
                for i, j in enumerate(picks):
                    r = c_t * rates[j]
                    v = r * vs[i] + c_t * us[i]
                    u = r * us[i] + x_t
                    nu.append(u)
                    nv.append(v)
                    nua.append(uacc[i] + g_t * u)
                    nva.append(vacc[i] + g_t * v)
                return tuple(nu), tuple(nv), tuple(nua), tuple(nva)

            us = tuple(ein_ref[j, :, gl] for j in picks)
            zeros = (zero,) * half
            us, vs, uacc, vacc = lax.fori_loop(0, run, ahead, (us, zeros, zeros, zeros), unroll=2)
            for i, j in enumerate(picks):
                u_ref[j, :, gl] = uacc[i]
                v_ref[j, :, gl] = vacc[i]
                ve_ref[j, :, gl] = vs[i]
    gn_ref[...] = get_runs(os, run) + par_ref[50:51, :].astype(F32) * g_mix


def finish_kernel(run, gn_ref, gnv_ref, que_ref, lead_ref, u_ref, v_ref, ve_ref, tok_ref, dir_ref, par_ref, msk_ref, ig_ref, gain_ref, ema_ref, os, tail, head):
    put_runs(head, column(msk_ref, 1), run)
    put_runs(tail, column(msk_ref, 2), run)
    decay, rate, width = decay_tables(par_ref)
    drive_in = par_ref[16:32, :].astype(F32)
    readout = par_ref[32:48, :].astype(F32)
    drive = width * drive_in
    gain = readout * drive
    rate_run = power_of_rate(decay, run)
    head_end = at_step(head, run - 1)
    per_block = BLOCK_TOKENS // run
    final = lax.broadcasted_iota(jnp.int32, (PARTS, LANES), 0) % per_block == per_block - 1
    u_rows, v_rows = [], []
    for g in range(GROUPS):
        gl = slice(g * LANES, (g + 1) * LANES)
        rates = [spread(rate, j, g) for j in range(NDIM)]
        start = []
        u_list, v_list = [], []
        for j in range(NDIM):
            que = que_ref[j, :, gl]
            inner = pltpu.roll(lead_ref[j, :, gl], PARTS - 1, 0) + pltpu.roll(head_end, PARTS - 1, 0) * spread(
                rate_run, j, g
            ) * que
            que = jnp.where(final, que, inner)
            start.append(que * spread(gain, j, g))
            u_list.append(jnp.sum(u_ref[j, :, gl], axis=0, keepdims=True))
            v_list.append(jnp.sum(v_ref[j, :, gl] + que * ve_ref[j, :, gl], axis=0, keepdims=True))
        u_rows.append(jnp.concatenate(u_list, axis=0))
        v_rows.append(jnp.concatenate(v_list, axis=0))

        def step(i, states, g=g, rates=rates):
            t = run - 1 - i
            acc = states[0]
            for j in range(1, NDIM):
                acc = acc + states[j]
            set_step(os, t, g, acc * at_step(tail, t))
            return tuple(rates[j] * states[j] for j in range(NDIM))

        lax.fori_loop(0, run, step, tuple(start), unroll=4)
    u_all = jnp.concatenate(u_rows, axis=1)
    v_all = jnp.concatenate(v_rows, axis=1)
    ema_ref[0:16, :] = (
        readout * drive * v_all * rate * (1.0 - rate)
        - readout * u_all * drive_in * rate * rate * (1.0 - rate) / width
    )
    ema_ref[16:32, :] = readout * u_all * width
    ema_ref[32:48, :] = drive * u_all
    g_normed = gn_ref[...] + gnv_ref[...] + get_runs(os, run)
    x = tok_ref[...].astype(F32)
    centred = x - jnp.mean(x, axis=-1, keepdims=True)
    var = jnp.mean(centred * centred, axis=-1, keepdims=True)
    inv = lax.rsqrt(var + EPS)
    n = centred * inv
    gain_ref[...] = jnp.sum(g_normed * n, axis=0, keepdims=True)
    h = g_normed * par_ref[48:49, :].astype(F32)
    back = inv * (h - jnp.mean(h, axis=-1, keepdims=True) - n * jnp.mean(h * n, axis=-1, keepdims=True))
    ig_ref[...] = (dir_ref[...] + back).astype(BF16)


def shaped(shape, dtype=F32):
    return jax.ShapeDtypeStruct(shape, dtype)


def swap(value, axis, bit):
    size = lax.axis_size(axis)
    return lax.ppermute(value, axis, [(i, i ^ bit) for i in range(size)])


def bits_of(size):
    out, bit = [], 1
    while bit < size:
        out.append(bit)
        bit *= 2
    return out


def gather_weight(shard, me, size):
    pieces = {0: shard[None]}
    for bit in reversed(bits_of(size)):
        keys = sorted(pieces)
        got = swap(jnp.concatenate([pieces[k] for k in keys], axis=0), "wsh", bit)
        for i, k in enumerate(keys):
            pieces[k | bit] = got[i : i + 1]
    stacked = jnp.concatenate([pieces[k] for k in range(size)], axis=0)
    rows = [lax.dynamic_index_in_dim(stacked, me ^ s, 0, keepdims=False) for s in range(size)]
    return jnp.concatenate(rows, axis=0)


def reduce_shares(share, me_w, me_c):
    size_w, size_c = lax.axis_size("wsh"), lax.axis_size("ctx")
    low = share.astype(BF16)
    pieces = [lax.dynamic_index_in_dim(low, me_w ^ p, 0, keepdims=True) for p in range(size_w)]
    pieces = jnp.concatenate(pieces, axis=0)
    for bit in bits_of(size_w):
        pieces = pieces.reshape((-1, 2) + pieces.shape[1:])
        got = swap(pieces[:, 1], "wsh", bit)
        pieces = (pieces[:, 0].astype(F32) + got.astype(F32)).astype(BF16)
    mine = pieces[0]
    rows, cols = mine.shape
    parts = mine.reshape(size_c, rows // size_c, cols)
    pieces = jnp.concatenate(
        [lax.dynamic_index_in_dim(parts, me_c ^ q, 0, keepdims=True) for q in range(size_c)], axis=0
    )
    for bit in bits_of(size_c):
        pieces = pieces.reshape((-1, 2) + pieces.shape[1:])
        got = swap(pieces[:, 1], "ctx", bit)
        pieces = (pieces[:, 0].astype(F32) + got.astype(F32)).astype(BF16)
    for bit in reversed(bits_of(size_c)):
        got = swap(pieces, "ctx", bit)
        pieces = jnp.stack([pieces, got], axis=1).reshape((-1,) + pieces.shape[1:])
    out = [lax.dynamic_index_in_dim(pieces, me_c ^ r, 0, keepdims=False) for r in range(size_c)]
    return jnp.concatenate(out, axis=0).astype(F32)


def body(
    tokens,
    segments,
    deal_order,
    cotangent,
    proj_weight,
    value_weight,
    merge_weight,
    ffn_up,
    ffn_down,
    norm_gain,
    ffn_gain,
    skip_gain,
    ema_decay,
    ema_input,
    ema_output,
    query_key,
):
    size_w, size_c = lax.axis_size("wsh"), lax.axis_size("ctx")
    me_w, me_c = lax.axis_index("wsh"), lax.axis_index("ctx")
    part = D // size_w
    zpart = Z // size_w
    small = jnp.concatenate(
        [
            ema_decay.T,
            ema_input.T,
            ema_output.T,
            norm_gain[None],
            ffn_gain[None],
            skip_gain[None],
            jnp.pad(query_key.T, ((0, 0), (0, part - zpart))),
            jnp.zeros((SMALL_ROWS - 3 * NDIM - 6, part), BF16),
        ],
        axis=0,
    )
    small_all = lax.all_gather(small, "wsh", axis=0, tiled=False)
    par = jnp.transpose(small_all, (1, 0, 2)).reshape(SMALL_ROWS, D)
    qk_table = jnp.transpose(small_all[:, 51:54, :zpart], (0, 2, 1)).reshape(Z, 3).astype(F32)
    ffn_gain_full = par[49].astype(F32)

    proj_full = gather_weight(proj_weight, me_w, size_w)
    value_full = gather_weight(value_weight, me_w, size_w)
    merge_full = gather_weight(merge_weight, me_w, size_w)
    up_full = gather_weight(ffn_up, me_w, size_w)
    down_full = gather_weight(ffn_down, me_w, size_w)

    row_count = tokens.shape[1]
    blocks = row_count // BLOCK_TOKENS
    run = row_count // PARTS
    per_block = BLOCK_TOKENS // run
    labels = segments[0].reshape(blocks, BLOCK_TOKENS)
    runs = labels.reshape(blocks, per_block, run)
    before = jnp.concatenate([labels[:, :1], labels[:, :-1]], axis=1)
    entry = before.reshape(blocks, per_block, run)[:, :, :1]
    masks = jnp.stack(
        [
            (labels == before).reshape(-1),
            (runs == entry).reshape(-1),
            (runs == runs[:, :, -1:]).reshape(-1),
            jnp.zeros((row_count,), bool),
        ],
        axis=1,
    ).astype(F32)

    pad_run = run + 1
    runs_scratch = pltpu.VMEM((GROUPS, PARTS * pad_run, LANES), F32)
    mask_scratch = pltpu.VMEM((PARTS * pad_run, LANES), F32)
    state_shape = shaped((NDIM, PARTS, D))
    normed, mix_local, ends, sums, far = pl.pallas_call(
        functools.partial(front_kernel, run),
        out_shape=(shaped((row_count, D)), shaped((row_count, D)), state_shape, state_shape, shaped((NDIM, D))),
        scratch_shapes=[runs_scratch, runs_scratch, mask_scratch, mask_scratch],
        name="front",
    )(tokens[0], par, masks)

    rows = NDIM * GROUPS // size_c
    pads = max(8 - 2, 0) if rows % 8 == 0 else 6

    def to_slices(state):
        flat = jnp.transpose(state.reshape(NDIM, blocks, GROUPS, LANES), (0, 2, 1, 3))
        return jnp.transpose(flat.reshape(size_c, rows, blocks, LANES), (0, 2, 1, 3))

    def from_slices(got):
        flat = jnp.transpose(got, (0, 2, 1, 3)).reshape(NDIM, GROUPS, blocks, LANES)
        state = jnp.transpose(flat, (0, 2, 1, 3)).reshape(NDIM, blocks, 1, D).astype(F32)
        return jnp.broadcast_to(state, (NDIM, blocks, per_block, D)).reshape(NDIM, PARTS, D)

    far_rows = lax.dynamic_slice_in_dim(far.reshape(NDIM * GROUPS, LANES), me_c * rows, rows)
    block_ends = sums.reshape(NDIM, blocks, per_block, D)[:, :, -1]
    bounds = jnp.stack([labels[:, 0], labels[:, -1]], axis=1).astype(BF16)
    bounds = jnp.broadcast_to(bounds[None, :, :, None], (size_c, blocks, 2, LANES))
    payload = jnp.concatenate(
        [to_slices(block_ends).astype(BF16), bounds, jnp.zeros((size_c, blocks, pads, LANES), BF16)], axis=2
    )
    got = lax.all_to_all(payload, "ctx", 0, 0, tiled=True)
    count = deal_order.shape[0]
    vm = pl.BlockSpec(memory_space=pltpu.VMEM)
    sm = pl.BlockSpec(memory_space=pltpu.SMEM)
    entries = pl.pallas_call(
        functools.partial(scan_kernel, blocks, count),
        out_shape=shaped((size_c, blocks, rows, LANES), BF16),
        in_specs=[sm, vm, vm],
        scratch_shapes=[pltpu.SMEM((count,), jnp.int32)],
        name="scan",
    )(deal_order, got, far_rows)
    entry_states = from_slices(lax.all_to_all(entries, "ctx", 0, 0, tiled=True))

    pre_active, active_low, normed_low, entered = pl.pallas_call(
        functools.partial(carry_kernel, run),
        out_shape=(
            shaped((row_count, D)),
            shaped((row_count, D), BF16),
            shaped((row_count, D), BF16),
            state_shape,
        ),
        scratch_shapes=[runs_scratch, mask_scratch],
        name="carry",
    )(mix_local, normed, entry_states, ends, par, masks)

    token_rows = tokens[0].astype(F32)
    causal = jnp.arange(BLOCK_TOKENS)[:, None] >= jnp.arange(BLOCK_TOKENS)[None, :]
    projected = jnp.dot(active_low, proj_full, preferred_element_type=F32)
    value_pre = jnp.dot(normed_low, value_full, preferred_element_type=F32)

    def heads_fn(projected, value_pre, qk_table):
        gate_up = jax.nn.sigmoid(projected[:, :D])
        shared = swish_unit(projected[:, D : D + Z])
        reset_gate = swish_unit(projected[:, D + Z : D + Z + VALUE_WIDTH])
        hidden_x = projected[:, D + Z + VALUE_WIDTH :]
        queries = shared * qk_table[:, 0] + qk_table[:, 1]
        keys_all = shared * qk_table[:, 2]
        return (gate_up, reset_gate, hidden_x, queries, keys_all, swish_unit(value_pre))

    (gate_up, reset_gate, hidden_x, queries, keys_all, value_rows), heads_back = jax.vjp(
        heads_fn, projected, value_pre, qk_table
    )
    query_low = queries.astype(BF16).reshape(blocks, BLOCK_TOKENS, Z)
    key_low = keys_all.astype(BF16).reshape(blocks, BLOCK_TOKENS, Z)
    value_low = value_rows.astype(BF16).reshape(blocks, BLOCK_TOKENS, VALUE_WIDTH)
    allowed = causal[None] & (labels[:, :, None] == labels[:, None, :])
    score_scale = Z ** (-0.5)
    raw = jnp.einsum("nqz,nkz->nqk", query_low, key_low, preferred_element_type=F32)
    scores = jnp.where(allowed, raw * score_scale, -1e30)
    peak = jnp.max(scores, axis=-1, keepdims=True)
    exps = jnp.exp(scores - peak)
    probs = exps / jnp.sum(exps, axis=-1, keepdims=True)
    probs_low = probs.astype(BF16)
    attended = jnp.einsum("lfz,lzw->lfw", probs_low, value_low, preferred_element_type=F32).reshape(
        row_count, VALUE_WIDTH
    )
    merged_low = (reset_gate * attended).astype(BF16)
    merged = jnp.dot(merged_low, merge_full, preferred_element_type=F32)

    def layer_norm(value, gain_vec):
        centred = value - jnp.mean(value, axis=-1, keepdims=True)
        var = jnp.mean(centred * centred, axis=-1, keepdims=True)
        return centred * lax.rsqrt(var + EPS) * gain_vec

    def mix_out(token_rows, gate_up, hidden_x, merged, gain_vec):
        hidden = swish_unit(hidden_x + merged)
        residual = token_rows + gate_up * (hidden - token_rows)
        return (residual, layer_norm(residual, gain_vec))

    (residual, normed_two), out_back = jax.vjp(mix_out, token_rows, gate_up, hidden_x, merged, ffn_gain_full)
    two_low = normed_two.astype(BF16)
    up_pre = jnp.dot(two_low, up_full, preferred_element_type=F32)
    inner = swish_unit(up_pre).astype(BF16)
    output = (residual + jnp.dot(inner, down_full, preferred_element_type=F32)).astype(BF16)[None]
    grad_out = cotangent[0]
    grad_down = jnp.dot(inner.T, grad_out, preferred_element_type=F32)
    grad_inner = jnp.dot(grad_out, down_full.T, preferred_element_type=F32)
    grad_up_pre = (grad_inner * swish_slope(up_pre)).astype(BF16)
    grad_up = jnp.dot(two_low.T, grad_up_pre, preferred_element_type=F32)
    grad_two = jnp.dot(grad_up_pre, up_full.T, preferred_element_type=F32)
    grad_rows, grad_gate, grad_hidden_x, grad_merged, grad_ffn_gain = out_back((grad_out.astype(F32), grad_two))
    grad_merged_low = grad_merged.astype(BF16)
    grad_merge = jnp.dot(merged_low.T, grad_merged_low, preferred_element_type=F32)
    grad_product = jnp.dot(grad_merged_low, merge_full.T, preferred_element_type=F32)
    grad_reset = grad_product * attended
    grad_att = (grad_product * reset_gate).astype(BF16).reshape(blocks, BLOCK_TOKENS, VALUE_WIDTH)
    grad_probs = jnp.einsum("yho,yeo->yhe", grad_att, value_low, preferred_element_type=F32)
    grad_values = jnp.einsum("ral,raf->rlf", probs_low, grad_att, preferred_element_type=F32).reshape(
        row_count, VALUE_WIDTH
    )
    grad_scores = probs * (grad_probs - jnp.sum(grad_probs * probs, axis=-1, keepdims=True))
    grad_raw = (grad_scores * score_scale).astype(BF16)
    grad_queries = jnp.einsum("nqk,nkz->nqz", grad_raw, key_low, preferred_element_type=F32).reshape(row_count, Z)
    grad_keys = jnp.einsum("nqk,nqz->nkz", grad_raw, query_low, preferred_element_type=F32).reshape(row_count, Z)
    grad_projected, grad_value_pre, grad_query_key = heads_back(
        (grad_gate, grad_reset, grad_hidden_x, grad_queries, grad_keys, grad_values)
    )
    grad_projected_low = grad_projected.astype(BF16)
    grad_proj = jnp.dot(active_low.T, grad_projected_low, preferred_element_type=F32)
    grad_active = jnp.dot(grad_projected_low, proj_full.T, preferred_element_type=F32)
    grad_value_low = grad_value_pre.astype(BF16)
    grad_value = jnp.dot(normed_low.T, grad_value_low, preferred_element_type=F32)
    grad_normed_value = jnp.dot(grad_value_low, value_full.T, preferred_element_type=F32)

    gn_local, leads, lead_sums, u_part, v_part, v_end, grad_skip = pl.pallas_call(
        functools.partial(adjoint_kernel, run),
        out_shape=(shaped((row_count, D)),) + (state_shape,) * 5 + (shaped((1, D)),),
        scratch_shapes=[runs_scratch] * 3 + [mask_scratch] * 2,
        name="adjoint",
    )(grad_active, pre_active, normed, entered, par, masks)
    block_leads = lead_sums.reshape(NDIM, blocks, per_block, D)[:, :, 0]
    got_back = lax.all_to_all(to_slices(block_leads).astype(BF16), "ctx", 0, 0, tiled=True)
    queues = pl.pallas_call(
        functools.partial(back_scan_kernel, blocks, count),
        out_shape=shaped((size_c, blocks, rows, LANES), BF16),
        in_specs=[sm, vm, vm, vm],
        scratch_shapes=[pltpu.SMEM((count,), jnp.int32)],
        name="back_scan",
    )(deal_order, got_back, got, far_rows)
    queue_states = from_slices(lax.all_to_all(queues, "ctx", 0, 0, tiled=True))
    input_grad, grad_norm, grad_ema = pl.pallas_call(
        functools.partial(finish_kernel, run),
        out_shape=(shaped((row_count, D), BF16), shaped((1, D)), shaped((3 * NDIM, D))),
        scratch_shapes=[runs_scratch, mask_scratch, mask_scratch],
        name="finish",
    )(gn_local, grad_normed_value, queue_states, leads, u_part, v_part, v_end, tokens[0], grad_rows, par, masks)

    def rows_of(grad):
        return grad.reshape((size_w, grad.shape[0] // size_w) + grad.shape[1:])

    ffn_share = jnp.concatenate([rows_of(grad_down).reshape(size_w, part, -1), rows_of(grad_up)], axis=2)
    merge_share = rows_of(grad_merge).reshape(size_w, part, -1)
    proj_share = jnp.concatenate([rows_of(grad_value), rows_of(grad_proj)], axis=2)
    ffn_total = reduce_shares(ffn_share, me_w, me_c)
    merge_total = reduce_shares(merge_share, me_w, me_c)
    proj_total = reduce_shares(proj_share, me_w, me_c)
    small_grads = jnp.concatenate(
        [
            grad_ema,
            grad_norm,
            grad_ffn_gain[None],
            grad_skip,
            jnp.pad(
                grad_query_key.T.reshape(3, size_w, zpart), ((0, 0), (0, 0), (0, part - zpart))
            ).reshape(3, D),
            jnp.zeros((64 - 54, D), F32),
        ],
        axis=0,
    )
    small_share = jnp.transpose(small_grads.reshape(64, size_w, part), (1, 0, 2))
    small_total = reduce_shares(small_share, me_w, me_c)
    depth = merge_weight.shape[0]
    return (
        output,
        input_grad[None],
        proj_total[:, FF:],
        proj_total[:, :FF],
        merge_total.reshape(depth, D),
        ffn_total[:, FF:],
        ffn_total[:, :FF].reshape(depth, D),
        small_total[48],
        small_total[49],
        small_total[50],
        small_total[0:16].T,
        small_total[16:32].T,
        small_total[32:48].T,
        small_total[51:54, :zpart].T,
    )


def solution(mesh):
    rows, flat = P("wsh", None), P("wsh")
    sequence = P("wsh", "ctx", None)
    placed = (sequence, P("wsh", "ctx"), P(), sequence) + (rows,) * 5 + (flat,) * 3 + (rows,) * 4
    return jax.shard_map(
        body,
        mesh=mesh,
        in_specs=placed,
        out_specs=(sequence, sequence) + (rows,) * 5 + (flat,) * 3 + (rows,) * 4,
        check_vma=False,
    )
```

```python
import functools

import jax
import jax.numpy as jnp
from jax import lax
from jax.experimental import pallas as pl
from jax.experimental.pallas import tpu as pltpu
from jax.sharding import PartitionSpec as P

D = 512
Z = 128
VALUE_WIDTH = 1024
NDIM = 16
BLOCK_TOKENS = 128
FF = 1024
PROJ = 2 * D + Z + VALUE_WIDTH
LANES = 128
GROUPS = D // LANES
STATES = NDIM * GROUPS
PARTS = 8
F32 = jnp.float32
BF16 = jnp.bfloat16
EPS = 1e-05
SMALL_ROWS = 56
SCALE = Z ** (-0.5)
VM = pl.BlockSpec(memory_space=pltpu.VMEM)
SM = pl.BlockSpec(memory_space=pltpu.SMEM)
HBM = pl.BlockSpec(memory_space=pltpu.HBM)


sigmoid = jax.nn.sigmoid


def swish_unit(v):
    return v * sigmoid(v)


def swish_slope(v):
    s = sigmoid(v)
    return s * (1.0 + v * (1.0 - s))


def shaped(shape, dtype=F32):
    return jax.ShapeDtypeStruct(shape, dtype)


def dot(a, b):
    return jnp.dot(a, b, preferred_element_type=F32)


def dot_nt(a, b):
    return lax.dot_general(a, b, (((1,), (1,)), ((), ())), preferred_element_type=F32)


def tree_sum(terms):
    terms = list(terms)
    while len(terms) > 1:
        terms = [terms[i] + terms[i + 1] if i + 1 < len(terms) else terms[i] for i in range(0, len(terms), 2)]
    return terms[0]


def decay_tables(par_ref):
    decay = par_ref[0:NDIM, :]
    rate = sigmoid(decay)
    width = jnp.sqrt(sigmoid(-decay) * (1.0 + rate))
    return decay, rate, width


def power_of_rate(decay, count):
    return jnp.exp(-count * jnp.log1p(jnp.exp(-decay)))


def spread(table, j, g):
    return jnp.broadcast_to(table[j : j + 1, g * LANES : (g + 1) * LANES], (PARTS, LANES))


def state_rows(j, g):
    return pl.ds((j * GROUPS + g) * PARTS, PARTS)


def put_runs(ref, value, run):
    stride = ref.shape[-2] // PARTS
    if len(ref.shape) == 2:
        for h in range(PARTS):
            ref[h * stride : h * stride + run, :] = value[h * run : (h + 1) * run, :]
    else:
        for g in range(GROUPS):
            for h in range(PARTS):
                ref[g, h * stride : h * stride + run, :] = value[
                    h * run : (h + 1) * run, g * LANES : (g + 1) * LANES
                ]


def get_runs(ref, run):
    stride = ref.shape[-2] // PARTS
    return jnp.concatenate(
        [
            jnp.concatenate([ref[g, h * stride : h * stride + run, :] for h in range(PARTS)], axis=0)
            for g in range(GROUPS)
        ],
        axis=1,
    )


def at_step(ref, t, g=None):
    stride = ref.shape[-2] // PARTS
    if g is None:
        return ref[pl.ds(t, PARTS, stride=stride), :]
    return ref[g, pl.ds(t, PARTS, stride=stride), :]


def set_step(ref, t, g, value):
    stride = ref.shape[-2] // PARTS
    ref[g, pl.ds(t, PARTS, stride=stride), :] = value


def column(ref, i):
    return jnp.broadcast_to(ref[:, i : i + 1], (ref.shape[0], LANES))


class Mover:
    def __init__(self, sems):
        self.sems = sems
        self.used = 0

    def start(self, *pairs):
        copies = []
        for src, dst in pairs:
            copies.append(pltpu.make_async_copy(src, dst, self.sems.at[self.used]))
            self.used += 1
        for copy in copies:
            copy.start()
        return copies


def wait_all(copies):
    for copy in copies:
        copy.wait()


WEIGHTS = (("proj", PROJ, False), ("value", VALUE_WIDTH, False), ("merge", D, True), ("up", FF, False), ("down", D, True))
TRAVEL = ((0,), (1, 2), (3, 4))


def travel_cols(i):
    return WEIGHTS[i][1] * (2 if WEIGHTS[i][2] else 1)


def spans_of(weight, base, count, shard_rows):
    _, cols, tall = WEIGHTS[weight]
    if not tall:
        return [(base, 0, cols)]
    return [(base, 0, cols), (base + shard_rows // 2, cols, 2 * cols)]


def pack_kernel(me_ref, dec_ref, inp_ref, rdo_ref, ng_ref, fg_ref, sg_ref, qk_ref, *refs):
    shards = refs[:5]
    out_ref = refs[5]
    halves = refs[6 : 6 + len(TRAVEL)]
    sems = refs[-1]
    move = Mover(sems)
    side = me_ref[1] & 1
    copies = []
    for group, half in zip(TRAVEL, halves):
        at = 0
        count = half.shape[0]
        for w in group:
            shard_rows = shards[w].shape[0]
            for base, start, stop in spans_of(w, pl.multiple_of(side * count, count), count, shard_rows):
                copies += move.start((shards[w].at[pl.ds(base, count), :], half.at[:, at + start : at + stop]))
            at += travel_cols(w)
    part = out_ref.shape[1]
    rows = qk_ref.shape[1]
    out_ref[...] = jnp.zeros_like(out_ref)
    out_ref[0:NDIM, :] = dec_ref[...]
    out_ref[NDIM : 2 * NDIM, :] = inp_ref[...]
    out_ref[2 * NDIM : 3 * NDIM, :] = rdo_ref[...]
    gains = jnp.concatenate([ng_ref[...], fg_ref[...], sg_ref[...]], axis=0).astype(F32)
    qk = qk_ref[...].astype(F32)
    if rows < part:
        qk = jnp.concatenate([qk, jnp.zeros((3, part - rows), F32)], axis=1)
    out_ref[3 * NDIM : SMALL_ROWS, :] = jnp.concatenate([gains, qk, jnp.zeros((2, part), F32)], axis=0).astype(BF16)
    wait_all(copies)


def build_masks(seg_ref, run, blocks, cont, head, tail=None, labels=None):
    seg = seg_ref[...].astype(F32)
    rows = [seg[:, b * BLOCK_TOKENS : (b + 1) * BLOCK_TOKENS] for b in range(blocks)]
    turned = jnp.concatenate(rows + [rows[0]] * (8 - blocks), axis=0).T
    per_block = PARTS // blocks
    stride = head.shape[0] // PARTS
    top = lax.broadcasted_iota(jnp.int32, (BLOCK_TOKENS, LANES), 0) == 0
    for b in range(blocks):
        col = jnp.broadcast_to(turned[:, b : b + 1], (BLOCK_TOKENS, LANES))
        if labels is not None:
            labels[b * BLOCK_TOKENS : (b + 1) * BLOCK_TOKENS, :] = col
        joined = jnp.where(top | (col == pltpu.roll(col, 1, 0)), 1.0, 0.0)
        for r in range(per_block):
            first = r * run
            part = col[first : first + run, :]
            entry = col[max(first - 1, 0) : max(first - 1, 0) + 1, :]
            last = col[first + run - 1 : first + run, :]
            at = (b * per_block + r) * stride
            cont[at : at + run, :] = joined[first : first + run, :]
            head[at : at + run, :] = jnp.where(part == entry, 1.0, 0.0)
            if tail is not None:
                tail[at : at + run, :] = jnp.where(part == last, 1.0, 0.0)


def normalise(x, gain):
    centred = x - jnp.mean(x, axis=-1, keepdims=True)
    inv = lax.rsqrt(jnp.mean(centred * centred, axis=-1, keepdims=True) + EPS)
    return centred * inv, inv, centred * inv * gain


def front_kernel(keys, run, blocks, *refs):
    n = len(keys)
    me_ref, tok_ref, seg_ref = refs[:3]
    small_refs = refs[3 : 3 + n]
    par_ref, qk_ref, end_ref, pay_ref, far_ref = refs[3 + n : 8 + n]
    xs, cont, head, sums, small = refs[8 + n :]
    me = me_ref[0]
    size_w = small.shape[0]
    zpart = Z // size_w
    for ref, ks in zip(small_refs, keys):
        for i, k in enumerate(ks):
            small[me ^ k] = ref[i].astype(F32)
    par_ref[...] = jnp.concatenate([small[w] for w in range(size_w)], axis=1)
    qk_ref[0:3, :] = jnp.concatenate(
        [small[w, 3 * NDIM + 3 : 3 * NDIM + 6, 0:zpart] for w in range(size_w)], axis=1
    )
    qk_ref[3:8, :] = jnp.zeros((5, Z), F32)
    put_runs(xs, normalise(tok_ref[...].astype(F32), par_ref[48:49, :])[2], run)
    build_masks(seg_ref, run, blocks, cont, head)
    decay, rate, _ = decay_tables(par_ref)
    far = power_of_rate(decay, BLOCK_TOKENS)
    rate_run = power_of_rate(decay, run)
    head_end = at_step(head, run - 1)
    for g in range(GROUPS):
        rates = [spread(rate, j, g) for j in range(NDIM)]
        for j in range(NDIM):
            far_ref[j * GROUPS + g : j * GROUPS + g + 1, :] = far[j : j + 1, g * LANES : (g + 1) * LANES]

        def step(t, states, g=g, rates=rates):
            x_t = at_step(xs, t, g)
            c_t = at_step(cont, t)
            return tuple((c_t * rates[j]) * states[j] + x_t for j in range(NDIM))

        zero = tuple(jnp.zeros((PARTS, LANES), F32) for _ in range(NDIM))
        ends = lax.fori_loop(0, run, step, zero, unroll=4)
        for j in range(NDIM):
            end_ref[state_rows(j, g), :] = ends[j]
            sums[state_rows(j, g), :] = ends[j] + head_end * spread(rate_run, j, g) * pltpu.roll(ends[j], 1, 0)
    per_block = PARTS // blocks
    seg = seg_ref[...].astype(F32)
    for b in range(blocks):
        ends = [seg[:, b * BLOCK_TOKENS : b * BLOCK_TOKENS + 1], seg[:, (b + 1) * BLOCK_TOKENS - 1 : (b + 1) * BLOCK_TOKENS]]
        bounds = jnp.concatenate([jnp.broadcast_to(e, (1, LANES)) for e in ends] + [jnp.zeros((6, LANES), F32)], axis=0)
        mine = jnp.concatenate([sums[pl.ds((b + 1) * per_block - 1, STATES, stride=PARTS), :], bounds], axis=0)
        for c in range(pay_ref.shape[0]):
            pay_ref[c, b] = mine.astype(BF16)


def local_kernel(run, blocks, tok_ref, seg_ref, par_ref, nrm_ref, mix_ref, cont, head, tail, lab_ref, xs, os):
    normed = normalise(tok_ref[...].astype(F32), par_ref[48:49, :])[2]
    nrm_ref[...] = normed
    put_runs(xs, normed, run)
    for ref in (cont, head, tail):
        ref[...] = jnp.zeros_like(ref)
    build_masks(seg_ref, run, blocks, cont, head, tail, lab_ref)
    _, rate, width = decay_tables(par_ref)
    gain = par_ref[32:48, :] * width * par_ref[16:32, :]
    for g in range(GROUPS):
        rates = [spread(rate, j, g) for j in range(NDIM)]
        gains = [spread(gain, j, g) for j in range(NDIM)]

        def step(t, states, g=g, rates=rates, gains=gains):
            x_t = at_step(xs, t, g)
            c_t = at_step(cont, t)
            new = [(c_t * rates[j]) * states[j] + x_t for j in range(NDIM)]
            set_step(os, t, g, tree_sum([gains[j] * new[j] for j in range(NDIM)]))
            return tuple(new)

        zero = tuple(jnp.zeros((PARTS, LANES), F32) for _ in range(NDIM))
        lax.fori_loop(0, run, step, zero, unroll=4)
    mix_ref[...] = get_runs(os, run)


def scan_states(me_ref, order_ref, got_ref, bnd_ref, far_ref, table, place, blocks, forward):
    count = place.shape[0]
    per_block = PARTS // blocks
    mine = me_ref[1]

    def note(p, carry):
        place[order_ref[p]] = p
        return carry

    lax.fori_loop(0, count, note, 0)

    def step(i, carry):
        state, label = carry
        pos = place[i if forward else count - 1 - i]
        dev, b = pos // blocks, pos % blocks
        got = got_ref[dev, b].astype(F32)
        bnd = bnd_ref[dev, b, STATES : STATES + 2, :].astype(F32)
        first, last = bnd[0:1, :], bnd[1:2, :]
        state = jnp.where((first if forward else last) == label, state, 0.0)

        @pl.when(dev == mine)
        def _():
            for r in range(per_block):
                table[pl.ds(b * per_block + r, STATES, stride=PARTS), :] = state

        state = jnp.where(first == last, far_ref[...] * state, 0.0) + got[0:STATES, :]
        return state, (last if forward else first)

    lax.fori_loop(0, count, step, (jnp.zeros((STATES, LANES), F32), jnp.full((1, LANES), -1.0, F32)))


def weight_copies(move, weight, sources, side, me, target, part):
    _, cols, tall = WEIGHTS[weight]
    copies = []
    for ref, column, key, half in sources:
        tall_by = 2 if tall else 1
        base = (me ^ key) * (part * tall_by)
        if half is None:
            copies += move.start((ref, target.at[pl.ds(pl.multiple_of(base, part), part * tall_by), :]))
            continue
        count = part // 2
        base = base + (side if half == 0 else 1 - side) * count
        for s in range(tall_by):
            rows = pl.ds(pl.multiple_of(base + s * part, count), count)
            copies += move.start((ref.at[:, column + s * cols : column + (s + 1) * cols], target.at[rows, :]))
    return copies


def sources_of(weight, own, own_other, travelled, keys):
    group = next(i for i, g in enumerate(TRAVEL) if weight in g)
    column = sum(travel_cols(w) for w in TRAVEL[group] if w < weight)
    out = [(own, 0, 0, None), (own_other, 0, 1, None)]
    near, far, near_other, far_other = travelled[group]
    for i, k in enumerate(keys):
        out += [(near.at[i], column, k, 0), (far.at[i], column, k, 1)]
        out += [(near_other.at[i], column, k | 1, 0), (far_other.at[i], column, k | 1, 1)]
    return out


def shard_transpose(value, me, size_w, target):
    width = value.shape[1] // size_w
    turned = value[...].T
    for shard in range(size_w):
        p = me ^ shard
        at = ((p & 1) * (size_w // 2) + (p >> 1)) * width
        target[pl.ds(pl.multiple_of(at, width), width), :] = turned[shard * width : (shard + 1) * width, :]


def store_shares(res, size_w, keep_ref, send_ref, col, tall=False):
    half = size_w // 2
    width = res.shape[1]
    steps = 2 if tall else 1
    rows = res.shape[0] // (steps * size_w)
    for i in range(size_w):
        target = keep_ref if i < half else send_ref
        for s in range(steps):
            block = res[(steps * i + s) * rows : (steps * i + s + 1) * rows, :]
            target[i % half, :, col + s * width : col + (s + 1) * width] = block.astype(BF16)


def layer_kernel(wkeys, run, blocks, size_w, *refs):
    me_ref, order_ref, got_ref, far_ref, end_ref, par_ref, qk_ref, head, lab_ref, seg_ref = refs[:10]
    mix_h, nrm_h, tok_h, cot_h = refs[10:14]
    own, own_other = refs[14:19], refs[19:24]
    travelled = [refs[24 + 4 * i : 28 + 4 * i] for i in range(len(TRAVEL))]
    refs = refs[24 + 4 * len(TRAVEL) :]
    ein_ref, fgain_ref = refs[:2]
    outs = refs[2:20]
    places = refs[20:38]
    (mix, nrm, tok, cot, os, table, wp, wv, wm, wu, wd, hid, gat, two, inner, ups, turned, place, sems) = refs[38:]
    (out_s, keep, send, pre_s, act, low, mlow, gcol, dir_s, rg, ra, val, vsl, prob, q_s, k_s, ssl, sh) = places
    move = Mover(sems)
    pending = []

    def flush(*which):
        for i in which:
            pending.extend(move.start((places[i], outs[i])))

    me = me_ref[0]
    side = me_ref[1] & 1
    part = D // size_w
    fetched = move.start((mix_h, mix), (nrm_h, nrm), (tok_h, tok), (cot_h, cot))
    loads = []
    for w, target in enumerate((wp, wv, wm, wu, wd)):
        loads.append(
            weight_copies(move, w, sources_of(w, own[w], own_other[w], travelled, wkeys), side, me, target, part)
        )

    scan_states(me_ref, order_ref, got_ref, got_ref, far_ref, table, place, blocks, True)
    decay, rate, width = decay_tables(par_ref)
    gain = par_ref[32:48, :] * width * par_ref[16:32, :]
    rate_run = power_of_rate(decay, run)
    head_end = at_step(head, run - 1)
    head_before = pltpu.roll(head_end, 1, 0)
    per_block = PARTS // blocks
    lead = lax.broadcasted_iota(jnp.int32, (PARTS, LANES), 0) % per_block == 0
    for g in range(GROUPS):
        rates = [spread(rate, j, g) for j in range(NDIM)]
        start = []
        for j in range(NDIM):
            ent = table[state_rows(j, g), :]
            inward = pltpu.roll(end_ref[state_rows(j, g), :], 1, 0) + head_before * spread(rate_run, j, g) * ent
            ent = jnp.where(lead, ent, inward)
            ein_ref[state_rows(j, g), :] = ent
            start.append(ent * spread(gain, j, g))

        def step(t, states, g=g, rates=rates):
            new = [rates[j] * states[j] for j in range(NDIM)]
            set_step(os, t, g, tree_sum(new) * at_step(head, t))
            return tuple(new)

        lax.fori_loop(0, run, step, tuple(start), unroll=4)
    wait_all(fetched)
    normed = nrm[...]
    pre = mix[...] + get_runs(os, run) + par_ref[50:51, :] * normed
    pre_s[...] = pre
    act[...] = swish_unit(pre).astype(BF16)
    low[...] = normed.astype(BF16)
    flush(3, 4, 5)

    wait_all(loads[0])
    gates = dot(act[...], wp[:, 0 : D + Z])
    gat[...] = sigmoid(gates[:, 0:D])
    shared_in = gates[:, D : D + Z]
    shared = swish_unit(shared_in)
    sh[...] = shared
    ssl[...] = swish_slope(shared_in)
    q_s[...] = (shared * qk_ref[0:1, :] + qk_ref[1:2, :]).astype(BF16)
    k_s[...] = (shared * qk_ref[2:3, :]).astype(BF16)
    hid[...] = dot(act[...], wp[:, D + Z + VALUE_WIDTH :])
    wait_all(loads[1])
    v = dot(low[...], wv[...])
    s = sigmoid(v)
    val[...] = (v * s).astype(BF16)
    vsl[...] = (s * (1.0 + v * (1.0 - s))).astype(BF16)
    causal = lax.broadcasted_iota(jnp.int32, (BLOCK_TOKENS, BLOCK_TOKENS), 0) >= lax.broadcasted_iota(
        jnp.int32, (BLOCK_TOKENS, BLOCK_TOKENS), 1
    )
    seg = seg_ref[...].astype(F32)
    for b in range(blocks):
        rows = slice(b * BLOCK_TOKENS, (b + 1) * BLOCK_TOKENS)
        allowed = causal & (lab_ref[rows, :] == seg[:, rows])
        scores = jnp.where(allowed, dot_nt(q_s[rows, :], k_s[rows, :]) * SCALE, -1e30)
        exps = jnp.exp(scores - jnp.max(scores, axis=-1, keepdims=True))
        prob[rows, :] = exps / jnp.sum(exps, axis=-1, keepdims=True)
    flush(11, 12, 13, 14, 15, 16, 17)
    r = dot(act[...], wp[:, D + Z : D + Z + VALUE_WIDTH])
    s = sigmoid(r)
    gate = r * s
    rg[...] = gate.astype(BF16)
    slope = s * (1.0 + r * (1.0 - s))
    att = jnp.concatenate(
        [
            dot(
                prob[b * BLOCK_TOKENS : (b + 1) * BLOCK_TOKENS, :].astype(BF16),
                val[b * BLOCK_TOKENS : (b + 1) * BLOCK_TOKENS, :],
            )
            for b in range(blocks)
        ],
        axis=0,
    )
    ra[...] = (slope * att).astype(BF16)
    mlow[...] = (gate * att).astype(BF16)
    flush(6, 9, 10)
    wait_all(loads[2])
    hm = hid[...] + dot(mlow[...], wm[...])
    hid[...] = hm
    x = tok[...].astype(F32)
    residual = x + gat[...] * (swish_unit(hm) - x)
    n, inv, normed_two = normalise(residual, par_ref[49:50, :])
    two[...] = normed_two.astype(BF16)

    wait_all(loads[3])
    u = dot(two[...], wu[...])
    s = sigmoid(u)
    inner[...] = (u * s).astype(BF16)
    slope = s * (1.0 + u * (1.0 - s))
    wait_all(loads[4])
    ups[...] = (dot_nt(cot[...], wd[...]) * slope).astype(BF16)
    shard_transpose(inner, me, size_w, turned)
    store_shares(dot(turned[...], cot[...]), size_w, keep, send, 0, True)
    shard_transpose(two, me, size_w, turned.at[0:D])
    store_shares(dot(turned[0:D, :], ups[...]), size_w, keep, send, 2 * D)
    flush(1, 2)
    out_s[...] = (residual + dot(inner[...], wd[...])).astype(BF16)
    flush(0)
    g_two = dot_nt(ups[...], wu[...])
    fgain_ref[...] = jnp.sum(g_two * n, axis=0, keepdims=True)
    h = g_two * par_ref[49:50, :]
    g_res = cot[...].astype(F32) + inv * (
        h - jnp.mean(h, axis=-1, keepdims=True) - n * jnp.mean(h * n, axis=-1, keepdims=True)
    )
    gate = gat[...]
    s = sigmoid(hm)
    gcol[:, 0:D] = (g_res * (hm * s - x) * gate * (1.0 - gate)).astype(BF16)
    gcol[:, D : 2 * D] = (g_res * gate * (s * (1.0 + hm * (1.0 - s)))).astype(BF16)
    dir_s[...] = g_res * (1.0 - gate)
    flush(7, 8)
    wait_all(pending)


def back_kernel(wkeys, blocks, size_w, *refs):
    me_ref, qk_ref = refs[:2]
    inputs = refs[2:13]
    own, own_other = refs[13], refs[14]
    travelled = refs[15:19]
    refs = refs[19:]
    gqk_ref = refs[0]
    outs = refs[1:5]
    held = refs[5:16]
    keep, send, gproj, gval = refs[16:20]
    wm, gatt, turned, sems = refs[20:]
    gcol, rg, ra, val, prob, k_s, q_s, sh, ssl, vsl, act = held
    move = Mover(sems)
    me = me_ref[0]
    side = me_ref[1] & 1
    part = D // size_w
    fetched = {0: move.start((inputs[0], held[0]))}
    loads = weight_copies(move, 2, sources_of(2, own, own_other, (None, travelled), wkeys), side, me, wm, part)
    for i in range(1, 11):
        fetched[i] = move.start((inputs[i], held[i]))

    def need(*which):
        for i in which:
            wait_all(fetched[i])

    need(0)
    wait_all(loads)
    gp = dot_nt(gcol[:, D : 2 * D], wm[...])
    need(1, 2)
    gatt[...] = (gp * rg[...].astype(F32)).astype(BF16)
    gproj[:, D + Z : D + Z + VALUE_WIDTH] = (gp * ra[...].astype(F32)).astype(BF16)
    gproj[:, 0:D] = gcol[:, 0:D]
    gproj[:, D + Z + VALUE_WIDTH :] = gcol[:, D : 2 * D]
    need(3, 4, 5, 6, 7, 8, 9)
    sums = [jnp.zeros((1, Z), F32)] * 3
    for b in range(blocks):
        rows = slice(b * BLOCK_TOKENS, (b + 1) * BLOCK_TOKENS)
        p = prob[rows, :]
        g_att = gatt[rows, :]
        g_probs = dot_nt(g_att, val[rows, :])
        g_values = dot(p.T.astype(BF16), g_att)
        gval[rows, :] = (g_values * vsl[rows, :].astype(F32)).astype(BF16)
        g_scores = p * (g_probs - jnp.sum(g_probs * p, axis=-1, keepdims=True))
        g_raw = g_scores * SCALE
        g_q = dot(g_raw.astype(BF16), k_s[rows, :])
        g_k = dot(g_raw.T.astype(BF16), q_s[rows, :])
        shared = sh[rows, :]
        for i, term in enumerate((g_q * shared, g_q, g_k * shared)):
            sums[i] = sums[i] + jnp.sum(term, axis=0, keepdims=True)
        g_shared = g_q * qk_ref[0:1, :] + g_k * qk_ref[2:3, :]
        gproj[rows, D : D + Z] = (g_shared * ssl[rows, :]).astype(BF16)
    gqk_ref[...] = jnp.concatenate(sums + [jnp.zeros((5, Z), F32)], axis=0)
    pending = move.start((gproj, outs[2]), (gval, outs[3]))
    need(10)
    shard_transpose(act, me, size_w, turned)
    split = D + Z + D
    store_shares(dot(turned[...], gproj[:, 0:split]), size_w, keep, send, 0)
    store_shares(dot(turned[...], gproj[:, split:]), size_w, keep, send, split)
    pending += move.start((send, outs[1]), (keep, outs[0]))
    wait_all(pending)


def back_rest_kernel(wkeys, size_w, *refs):
    me_ref = refs[0]
    inputs = refs[1:6]
    own, own_other = refs[6:8], refs[8:10]
    travelled = [refs[10:14], refs[14:18]]
    refs = refs[18:]
    outs = refs[0:4]
    held = refs[4:9]
    keep, send, gact, gnv = refs[9:13]
    wp, wv, turned, sems = refs[13:]
    mlow, gcol, low, gval, gproj = held
    move = Mover(sems)
    me = me_ref[0]
    side = me_ref[1] & 1
    part = D // size_w
    fetched = [move.start((inputs[i], held[i])) for i in range(5)]
    loads = [
        weight_copies(move, w, sources_of(w, own[w], own_other[w], travelled, wkeys), side, me, target, part)
        for w, target in enumerate((wp, wv))
    ]
    wait_all(fetched[0] + fetched[1])
    shard_transpose(mlow, me, size_w, turned)
    store_shares(dot(turned[...], gcol[:, D : 2 * D]), size_w, keep, send, 0, True)
    wait_all(fetched[2] + fetched[3])
    shard_transpose(low, me, size_w, turned.at[0:D])
    store_shares(dot(turned[0:D, :], gval[...]), size_w, keep, send, 2 * D)
    pending = move.start((send, outs[1]), (keep, outs[0]))
    wait_all(fetched[4] + loads[0])
    gact[...] = dot_nt(gproj[...], wp[...])
    pending += move.start((gact, outs[2]))
    wait_all(loads[1])
    gnv[...] = dot_nt(gval[...], wv[...])
    pending += move.start((gnv, outs[3]))
    wait_all(pending)


def adjoint_kernel(run, blocks, gact_ref, pre_ref, nrm_ref, ein_ref, par_ref, cont, head, gn_ref, lead_ref, pay_ref, u_ref, v_ref, ve_ref, gs_ref, xs, gs, os, sums):
    normed = nrm_ref[...]
    g_mix = gact_ref[...] * swish_slope(pre_ref[...])
    gs_ref[...] = jnp.sum(g_mix * normed, axis=0, keepdims=True)
    put_runs(xs, normed, run)
    put_runs(gs, g_mix, run)
    decay, rate, width = decay_tables(par_ref)
    gain = par_ref[32:48, :] * width * par_ref[16:32, :]
    rate_run = power_of_rate(decay, run)
    head_end = at_step(head, run - 1)
    zero = jnp.zeros((PARTS, LANES), F32)
    for g in range(GROUPS):
        rates = [spread(rate, j, g) for j in range(NDIM)]
        gains = [spread(gain, j, g) for j in range(NDIM)]

        def back(i, carries, g=g, rates=rates, gains=gains):
            t = run - 1 - i
            g_t = at_step(gs, t, g)
            c_t = at_step(cont, t)
            bs = [g_t + carries[j] for j in range(NDIM)]
            set_step(os, t, g, tree_sum([gains[j] * bs[j] for j in range(NDIM)]))
            return tuple((c_t * rates[j]) * bs[j] for j in range(NDIM))

        ends = lax.fori_loop(0, run, back, (zero,) * NDIM, unroll=4)
        for j in range(NDIM):
            lead_ref[state_rows(j, g), :] = ends[j]
            sums[state_rows(j, g), :] = ends[j] + head_end * spread(rate_run, j, g) * pltpu.roll(ends[j], PARTS - 1, 0)
        half = NDIM // 2
        for first in (0, half):
            picks = range(first, first + half)

            def ahead(t, carry, g=g, picks=picks, rates=rates):
                us, vs, uacc, vacc = carry
                g_t = at_step(gs, t, g)
                x_t = at_step(xs, t, g)
                c_t = at_step(cont, t)
                nu, nv, nua, nva = [], [], [], []
                for i, j in enumerate(picks):
                    r = c_t * rates[j]
                    v = r * vs[i] + c_t * us[i]
                    u = r * us[i] + x_t
                    nu.append(u)
                    nv.append(v)
                    nua.append(uacc[i] + g_t * u)
                    nva.append(vacc[i] + g_t * v)
                return tuple(nu), tuple(nv), tuple(nua), tuple(nva)

            us = tuple(ein_ref[state_rows(j, g), :] for j in picks)
            zeros = (zero,) * half
            us, vs, uacc, vacc = lax.fori_loop(0, run, ahead, (us, zeros, zeros, zeros), unroll=4)
            for i, j in enumerate(picks):
                u_ref[state_rows(j, g), :] = uacc[i]
                v_ref[state_rows(j, g), :] = vacc[i]
                ve_ref[state_rows(j, g), :] = vs[i]
    gn_ref[...] = get_runs(os, run) + par_ref[50:51, :] * g_mix
    per_block = PARTS // blocks
    for b in range(blocks):
        mine = sums[pl.ds(b * per_block, STATES, stride=PARTS), :].astype(BF16)
        for c in range(pay_ref.shape[0]):
            pay_ref[c, b] = mine


def finish_kernel(run, blocks, me_ref, order_ref, got_ref, bnd_ref, far_ref, gn_ref, gnv_ref, lead_ref, u_ref, v_ref, ve_ref, tok_ref, dir_ref, par_ref, head, tail, gs_ref, fg_ref, gqk_ref, ig_ref, small_ref, os, table, place):
    scan_states(me_ref, order_ref, got_ref, bnd_ref, far_ref, table, place, blocks, False)
    decay, rate, width = decay_tables(par_ref)
    drive_in = par_ref[16:32, :]
    readout = par_ref[32:48, :]
    drive = width * drive_in
    gain = readout * drive
    rate_run = power_of_rate(decay, run)
    head_after = pltpu.roll(at_step(head, run - 1), PARTS - 1, 0)
    per_block = PARTS // blocks
    final = lax.broadcasted_iota(jnp.int32, (PARTS, LANES), 0) % per_block == per_block - 1
    u_rows, v_rows = [], []
    for g in range(GROUPS):
        rates = [spread(rate, j, g) for j in range(NDIM)]
        start = []
        u_list, v_list = [], []
        for j in range(NDIM):
            at = state_rows(j, g)
            que = table[at, :]
            inward = pltpu.roll(lead_ref[at, :], PARTS - 1, 0) + head_after * spread(rate_run, j, g) * que
            que = jnp.where(final, que, inward)
            start.append(que * spread(gain, j, g))
            u_list.append(jnp.sum(u_ref[at, :], axis=0, keepdims=True))
            v_list.append(jnp.sum(v_ref[at, :] + que * ve_ref[at, :], axis=0, keepdims=True))
        u_rows.append(jnp.concatenate(u_list, axis=0))
        v_rows.append(jnp.concatenate(v_list, axis=0))

        def step(i, states, g=g, rates=rates):
            t = run - 1 - i
            set_step(os, t, g, tree_sum(states) * at_step(tail, t))
            return tuple(rates[j] * states[j] for j in range(NDIM))

        lax.fori_loop(0, run, step, tuple(start), unroll=4)
    u_all = jnp.concatenate(u_rows, axis=1)
    v_all = jnp.concatenate(v_rows, axis=1)
    g_normed = gn_ref[...] + gnv_ref[...] + get_runs(os, run)
    x = tok_ref[...].astype(F32)
    centred = x - jnp.mean(x, axis=-1, keepdims=True)
    var = jnp.mean(centred * centred, axis=-1, keepdims=True)
    inv = lax.rsqrt(var + EPS)
    n = centred * inv
    h = g_normed * par_ref[48:49, :]
    back = inv * (h - jnp.mean(h, axis=-1, keepdims=True) - n * jnp.mean(h * n, axis=-1, keepdims=True))
    ig_ref[...] = (dir_ref[...] + back).astype(BF16)
    size_w = 2 * small_ref.shape[1]
    half = size_w // 2
    part = small_ref.shape[3]
    zpart = Z // size_w
    me = me_ref[0]
    grads = jnp.concatenate(
        [
            readout * drive * v_all * rate * (1.0 - rate)
            - readout * u_all * drive_in * rate * rate * (1.0 - rate) / width,
            readout * u_all * width,
            drive * u_all,
            jnp.sum(g_normed * n, axis=0, keepdims=True),
            fg_ref[...],
            gs_ref[...],
            jnp.zeros((5, D), F32),
        ],
        axis=0,
    )
    for w in range(size_w):
        p = me ^ w
        qk = gqk_ref[0:8, w * zpart : (w + 1) * zpart]
        if zpart < part:
            qk = jnp.concatenate([qk, jnp.zeros((8, part - zpart), F32)], axis=1)
        both = jnp.concatenate([grads[:, w * part : (w + 1) * part], qk], axis=0)
        small_ref[p & 1, p >> 1] = both.astype(BF16)


def swap(value, axis, bit):
    size = lax.axis_size(axis)
    return lax.ppermute(value, axis, [(i, i ^ bit) for i in range(size)])


def bits_of(size):
    out, bit = [], 1
    while bit < size:
        out.append(bit)
        bit *= 2
    return out


def tie(*values):
    return lax.optimization_barrier(values)


class Share:
    def __init__(self, terms, rows):
        self.terms = terms
        self.rows = rows

    def value(self):
        total = None
        for array, first in self.terms:
            if array.shape[0] != self.rows:
                array = lax.dynamic_slice_in_dim(array, first, self.rows, 0)
            array = array.astype(F32)
            total = array if total is None else total + array
        return total.astype(BF16)

    def halve(self, bit_on):
        count = self.rows // 2
        stay = Share([(a, f + bit_on * count) for a, f in self.terms], count)
        go = Share([(a, f + (1 - bit_on) * count) for a, f in self.terms], count)
        return stay, go

    def plus(self, array):
        return Share(self.terms + [(array, 0)], self.rows)


def stack_values(shares):
    return jnp.stack([share.value() for share in shares])


def far_keys(size):
    keys = []
    for bit in reversed(bits_of(size)[1:]):
        keys += [k | bit for k in [0] + keys]
    return keys


def reverse_bits(value, count):
    out = 0
    for i in range(count):
        out = out | (((value >> i) & 1) << (count - 1 - i))
    return out


def place_kernel(keys, nbits, spans, *refs):
    n = len(keys)
    me = refs[0][1]
    pieces = refs[1 : 1 + n]
    outs = refs[1 + n :]
    for ref, ks in zip(pieces, keys):
        rows = ref.shape[1]
        for i, k in enumerate(ks):
            base = reverse_bits(me ^ k, nbits) * rows
            for out, (start, tall) in zip(outs, spans):
                width = out.shape[1]
                for s in range(2 if tall else 1):
                    at = pl.ds(pl.multiple_of(base + s * (out.shape[0] // 2), rows), rows)
                    out[at, :] = ref[i, :, start + s * width : start + (s + 1) * width].astype(F32)


def place(levels, keys, nbits, where, spans, shapes, name):
    rows = levels[0].shape[1]
    if rows % 8:
        return place_by_gather(levels, keys, nbits, where, spans, shapes)
    return pl.pallas_call(
        functools.partial(place_kernel, keys, nbits, spans),
        out_shape=tuple(shaped(s) for s in shapes),
        in_specs=[SM] + [VM] * len(levels),
        name=name,
    )(where, *levels)


def place_by_gather(levels, keys, nbits, where, spans, shapes):
    flat = [k for level in keys for k in level]
    index = jnp.array([flat.index(k) for k in range(len(flat))], jnp.int32)
    order = index[where[1] ^ jnp.array([reverse_bits(i, nbits) for i in range(len(flat))], jnp.int32)]
    block = jnp.concatenate(levels, axis=0)[order].astype(F32)
    block = block.reshape(-1, block.shape[-1])
    outs = []
    for (start, tall), (rows, width) in zip(spans, shapes):
        columns = [block[:, start + s * width : start + (s + 1) * width] for s in range(2 if tall else 1)]
        outs.append(jnp.concatenate(columns, axis=0))
    return tuple(outs)


def body(
    tokens,
    segments,
    deal_order,
    cotangent,
    proj_weight,
    value_weight,
    merge_weight,
    ffn_up,
    ffn_down,
    norm_gain,
    ffn_gain,
    skip_gain,
    ema_decay,
    ema_input,
    ema_output,
    query_key,
):
    size_w, size_c = lax.axis_size("wsh"), lax.axis_size("ctx")
    me_w, me_c = lax.axis_index("wsh"), lax.axis_index("ctx")
    where = jnp.stack([me_w, me_c]).astype(jnp.int32)
    wbits, cbits = bits_of(size_w), bits_of(size_c)
    nbits = len(cbits)
    part = D // size_w
    zpart = Z // size_w
    half = size_w // 2
    rc = tokens.shape[1]
    blocks = rc // BLOCK_TOKENS
    run = rc // PARTS
    count = deal_order.shape[0]
    shards = (proj_weight, value_weight, merge_weight, ffn_up, ffn_down)
    group_cols = [sum(travel_cols(w) for w in group) for group in TRAVEL]
    big = pltpu.CompilerParams(vmem_limit_bytes=60 * 1024 * 1024)

    def cost(us):
        return pl.CostEstimate(flops=int(us * 1e9), bytes_accessed=int(us * 3e6), transcendentals=0)

    packed = pl.pallas_call(
        pack_kernel,
        out_shape=(shaped((SMALL_ROWS, part), BF16),) + tuple(shaped((part // 2, c), BF16) for c in group_cols),
        in_specs=[SM] + [VM] * 7 + [HBM] * 5,
        scratch_shapes=[pltpu.SemaphoreType.DMA((16,))],
        name="pack",
    )(
        where,
        ema_decay.T,
        ema_input.T,
        ema_output.T,
        norm_gain[None],
        ffn_gain[None],
        skip_gain[None],
        query_key.T,
        *shards,
    )
    small, travel = packed[0], packed[1:]

    def far_pieces(block):
        have = []
        for bit in reversed(wbits[1:]):
            sent = jnp.concatenate([block[None]] + have, axis=0) if have else block[None]
            have.append(swap(sent, "wsh", bit))
        return have[0] if len(have) == 1 else jnp.concatenate(have, axis=0)

    wkeys = far_keys(size_w)
    small_near = swap(small[None], "wsh", 1)
    tied = tie(small_near, *travel)
    small_near, travel = tied[0], tied[1:]
    small_far = far_pieces(small)
    near = [far_pieces(block) for block in travel]
    small_last = swap(small_far, "wsh", 1)
    skeys = [[0], [1], wkeys, [k | 1 for k in wkeys]]

    pad_run = run + 1
    runs_scratch = pltpu.VMEM((GROUPS, PARTS * pad_run, LANES), F32)
    mask_shape = shaped((PARTS * pad_run, LANES))
    mask_scratch = pltpu.VMEM((PARTS * pad_run, LANES), F32)
    table_scratch = pltpu.VMEM((STATES * PARTS, LANES), F32)
    table = shaped((STATES * PARTS, LANES))
    par, qk, ends, payload, far = pl.pallas_call(
        functools.partial(front_kernel, skeys, run, blocks),
        out_shape=(
            shaped((SMALL_ROWS, D)),
            shaped((8, Z)),
            table,
            shaped((size_c, blocks, STATES + 8, LANES), BF16),
            shaped((STATES, LANES)),
        ),
        in_specs=[SM] + [VM] * 6,
        scratch_shapes=[
            runs_scratch,
            mask_scratch,
            mask_scratch,
            table_scratch,
            pltpu.VMEM((size_w, SMALL_ROWS, part), F32),
        ],
        cost_estimate=cost(4),
        name="front",
    )(where, tokens[0], segments, small[None], small_near, small_far, small_last)
    got = lax.all_to_all(payload, "ctx", 0, 0, tiled=True)
    normed, mix_local, cont, head, tail, label_cols = pl.pallas_call(
        functools.partial(local_kernel, run, blocks),
        out_shape=(shaped((rc, D)), shaped((rc, D)), mask_shape, mask_shape, mask_shape, shaped((rc, LANES))),
        scratch_shapes=[runs_scratch, runs_scratch],
        cost_estimate=cost(6),
        name="local",
    )(tokens[0], segments, par)

    tied = tie(payload, *near)
    near = tied[1:]
    across = [swap(piece, "ctx", 1) for piece in near]
    tied = tie(mix_local, *near, *across, *shards)
    mix_local, near, across = tied[0], tied[1 : 1 + len(TRAVEL)], tied[1 + len(TRAVEL) : 1 + 2 * len(TRAVEL)]
    own_other = [swap(shard, "wsh", 1) for shard in tied[1 + 2 * len(TRAVEL) :]]
    travelled = [(a, b, swap(a, "wsh", 1), swap(b, "wsh", 1)) for a, b in zip(near, across)]

    saved = (
        shaped((rc, D), BF16),
        shaped((half, part, 2 * D + FF), BF16),
        shaped((half, part, 2 * D + FF), BF16),
        shaped((rc, D)),
        shaped((rc, D), BF16),
        shaped((rc, D), BF16),
        shaped((rc, VALUE_WIDTH), BF16),
        shaped((rc, 2 * D), BF16),
        shaped((rc, D)),
        shaped((rc, VALUE_WIDTH), BF16),
        shaped((rc, VALUE_WIDTH), BF16),
        shaped((rc, VALUE_WIDTH), BF16),
        shaped((rc, VALUE_WIDTH), BF16),
        shaped((rc, BLOCK_TOKENS)),
        shaped((rc, Z), BF16),
        shaped((rc, Z), BF16),
        shaped((rc, Z)),
        shaped((rc, Z)),
    )

    def vmem_of(shapes):
        return [pltpu.VMEM(s.shape, s.dtype) for s in shapes]

    copies_each = 2 + 4 * len(wkeys)
    results = pl.pallas_call(
        functools.partial(layer_kernel, wkeys, run, blocks, size_w),
        out_shape=(table, shaped((1, D))) + saved,
        in_specs=[SM, SM] + [VM] * 8 + [HBM] * (4 + 10 + 4 * len(TRAVEL)),
        out_specs=(VM, VM) + (HBM,) * len(saved),
        scratch_shapes=vmem_of(saved)
        + [
            pltpu.VMEM((rc, D), F32),
            pltpu.VMEM((rc, D), F32),
            pltpu.VMEM((rc, D), BF16),
            pltpu.VMEM((rc, D), BF16),
            runs_scratch,
            table_scratch,
            pltpu.VMEM((D, PROJ), BF16),
            pltpu.VMEM((D, VALUE_WIDTH), BF16),
            pltpu.VMEM((VALUE_WIDTH, D), BF16),
            pltpu.VMEM((D, FF), BF16),
            pltpu.VMEM((FF, D), BF16),
            pltpu.VMEM((rc, D), F32),
            pltpu.VMEM((rc, D), F32),
            pltpu.VMEM((rc, D), BF16),
            pltpu.VMEM((rc, FF), BF16),
            pltpu.VMEM((rc, FF), BF16),
            pltpu.VMEM((FF, rc), BF16),
            pltpu.SMEM((count,), jnp.int32),
            pltpu.SemaphoreType.DMA((4 + len(saved) + 7 * copies_each,)),
        ],
        compiler_params=big,
        cost_estimate=cost(17),
        name="layer",
    )(
        where,
        deal_order,
        got,
        far,
        ends,
        par,
        qk,
        head,
        label_cols,
        segments,
        mix_local,
        normed,
        tokens[0],
        cotangent[0],
        *shards,
        *own_other,
        *[piece for group in travelled for piece in group],
    )
    ein, grad_ffn_gain = results[:2]
    (
        output,
        ffn_keep,
        ffn_send,
        pre_active,
        active_low,
        normed_low,
        merged_low,
        gcols,
        direct,
        reset_gate,
        reset_slope,
        values,
        value_slope,
        probs,
        queries,
        keys_low,
        shared_slope,
        shared,
    ) = results[2:]

    def bit_of(index, i):
        return (index >> i) & 1

    def shares_of(keep, got):
        return [Share([(keep[i], 0), (got[i], 0)], keep.shape[1]) for i in range(half)]

    def plus_all(shares, got):
        return [share.plus(got[i]) for i, share in enumerate(shares)]

    def widen(levels, keys, bit):
        block = levels[0] if len(levels) == 1 else jnp.concatenate(levels, axis=0)
        return levels + [swap(block, "ctx", bit)], keys + [[k | bit for level in keys for k in level]]

    f_shares = shares_of(ffn_keep, swap(ffn_send, "wsh", 1))
    f_go = stack_values(f_shares[1::2])
    f_shares = f_shares[0::2]
    f_go, gcols = tie(f_go, gcols)
    f_got = swap(f_go, "wsh", 2)
    copies_weight = 2 * copies_each
    gproj_shape, gval_shape = shaped((rc, PROJ), BF16), shaped((rc, VALUE_WIDTH), BF16)
    back_in = (
        gcols,
        reset_gate,
        reset_slope,
        values,
        probs,
        keys_low,
        queries,
        shared,
        shared_slope,
        value_slope,
        active_low,
    )
    p_shapes = (shaped((half, part, PROJ), BF16),) * 2 + (gproj_shape, gval_shape)
    grad_qk, p_keep, p_send, gproj, gval = pl.pallas_call(
        functools.partial(back_kernel, wkeys, blocks, size_w),
        out_shape=(shaped((8, Z)),) + p_shapes,
        in_specs=[SM, VM] + [HBM] * (11 + 2 + 4),
        out_specs=(VM,) + (HBM,) * 4,
        scratch_shapes=vmem_of(back_in)
        + vmem_of(p_shapes)
        + [
            pltpu.VMEM((VALUE_WIDTH, D), BF16),
            pltpu.VMEM((rc, VALUE_WIDTH), BF16),
            pltpu.VMEM((D, rc), BF16),
            pltpu.SemaphoreType.DMA((15 + copies_weight,)),
        ],
        compiler_params=big,
        cost_estimate=cost(9),
        name="back",
    )(where, qk, *back_in, merge_weight, own_other[2], *travelled[1])
    p_got = swap(p_send, "wsh", 1)
    tied = tie(gproj, p_send, f_got)
    gproj, f_got = tied[0], tied[2]
    rest_in = (merged_low, gcols, normed_low, gval, gproj)
    q_cols = 2 * D + VALUE_WIDTH
    q_shapes = (shaped((half, part, q_cols), BF16),) * 2 + (shaped((rc, D)),) * 2
    q_keep, q_send, grad_active, grad_normed_value = pl.pallas_call(
        functools.partial(back_rest_kernel, wkeys, size_w),
        out_shape=q_shapes,
        in_specs=[SM] + [HBM] * (5 + 4 + 8),
        out_specs=(HBM,) * 4,
        scratch_shapes=vmem_of(rest_in)
        + vmem_of(q_shapes)
        + [
            pltpu.VMEM((D, PROJ), BF16),
            pltpu.VMEM((D, VALUE_WIDTH), BF16),
            pltpu.VMEM((VALUE_WIDTH, rc), BF16),
            pltpu.SemaphoreType.DMA((9 + copies_weight,)),
        ],
        compiler_params=big,
        cost_estimate=cost(7),
        name="back_rest",
    )(where, *rest_in, *shards[:2], *own_other[:2], *travelled[0], *travelled[1])

    side = bit_of(me_c, 0)
    p_shares = shares_of(p_keep, p_got)
    p_go = stack_values(p_shares[1::2])
    p_shares = p_shares[0::2]
    f_shares = plus_all(f_shares, f_got)
    for bit in wbits[2:]:
        f_got = swap(stack_values(f_shares[1::2]), "wsh", bit)
        f_shares = plus_all(f_shares[0::2], f_got)
    f_share, f_away = f_shares[0].halve(side)
    f_go = f_away.value()
    p_go, f_go, q_send = tie(p_go, f_go, q_send)
    p_got = swap(p_go, "wsh", 2)
    q_got = swap(q_send, "wsh", 1)
    f_got = swap(f_go, "ctx", 1)
    both = [share.halve(side) for share in shares_of(q_keep, q_got)]
    q_shares = [stay for stay, _ in both]
    q_go = stack_values([away for _, away in both])
    q_go, grad_active = tie(q_go, grad_active)
    q_got = swap(q_go, "ctx", 1)

    gn_local, leads, payload_back, u_part, v_part, v_end, grad_skip = pl.pallas_call(
        functools.partial(adjoint_kernel, run, blocks),
        out_shape=(
            shaped((rc, D)),
            table,
            shaped((size_c, blocks, STATES, LANES), BF16),
            table,
            table,
            table,
            shaped((1, D)),
        ),
        scratch_shapes=[runs_scratch] * 3 + [table_scratch],
        cost_estimate=cost(14),
        name="adjoint",
    )(grad_active, pre_active, normed, ein, par, cont, head)

    p_got, q_got, f_got, payload_back = tie(p_got, q_got, f_got, payload_back)
    p_shares = plus_all(p_shares, p_got)
    q_shares = plus_all(q_shares, q_got)
    for bit in wbits[2:]:
        p_got = swap(stack_values(p_shares[1::2]), "wsh", bit)
        q_got = swap(stack_values(q_shares[1::2]), "wsh", bit // 2)
        p_shares, q_shares = plus_all(p_shares[0::2], p_got), plus_all(q_shares[0::2], q_got)
    p_share, p_away = p_shares[0].halve(side)
    p_go = p_away.value()
    q_go = q_shares[1].value()
    q_share = q_shares[0]
    f_share, f_away = f_share.plus(f_got).halve(bit_of(me_c, 1))
    f_go = f_away.value()
    p_go, q_go, f_go, payload_back = tie(p_go, q_go, f_go, payload_back)
    p_got = swap(p_go, "ctx", 1)
    q_got = swap(q_go, "wsh", wbits[-1])
    f_got = swap(f_go, "ctx", 2)
    got_back = lax.all_to_all(payload_back, "ctx", 0, 0, tiled=True)

    p_got, q_got, f_got, got_back = tie(p_got, q_got, f_got, got_back)
    p_share, q_share, f_share = p_share.plus(p_got), q_share.plus(q_got), f_share.plus(f_got)

    def rest_step(i):
        p_stay, p_away = p_share.halve(bit_of(me_c, i))
        q_stay, q_away = q_share.halve(bit_of(me_c, i))
        return p_stay, q_stay, jnp.concatenate([p_away.value(), q_away.value()], axis=1)

    p_share, q_share, r_go = rest_step(1)
    f_share, f_away = f_share.halve(bit_of(me_c, 2))
    r_go, f_go, got_back = tie(r_go, f_away.value(), got_back)
    r_got = swap(r_go, "ctx", 2)
    f_got = swap(f_go, "ctx", 4)
    input_grad, small_share = pl.pallas_call(
        functools.partial(finish_kernel, run, blocks),
        out_shape=(shaped((rc, D), BF16), shaped((2, half, SMALL_ROWS + 8, part), BF16)),
        in_specs=[SM, SM] + [VM] * 17,
        scratch_shapes=[runs_scratch, table_scratch, pltpu.SMEM((count,), jnp.int32)],
        cost_estimate=cost(7),
        name="finish",
    )(
        where,
        deal_order,
        got_back,
        got,
        far,
        gn_local,
        grad_normed_value,
        leads,
        u_part,
        v_part,
        v_end,
        tokens[0],
        direct,
        par,
        head,
        tail,
        grad_skip,
        grad_ffn_gain,
        grad_qk,
    )
    r_got, f_got, small_share = tie(r_got, f_got, small_share)
    p_share, q_share = p_share.plus(r_got[:, :PROJ]), q_share.plus(r_got[:, PROJ:])
    f_share = f_share.plus(f_got)
    for i, bit in enumerate(cbits[3:]):
        f_share, f_away = f_share.halve(bit_of(me_c, 3 + i))
        f_share = f_share.plus(swap(f_away.value(), "ctx", bit))
    f_levels, f_keys = [f_share.value()[None]], [[0]]
    for i, bit in enumerate(cbits[2:]):
        p_share, q_share, r_go = rest_step(2 + i)
        if i == 0:
            r_go, f_own, small_share = tie(r_go, f_levels[0], small_share)
            f_levels = [f_own]
            f_levels, f_keys = widen(f_levels, f_keys, cbits[-1])
        r_got = swap(r_go, "ctx", bit)
        p_share, q_share = p_share.plus(r_got[:, :PROJ]), q_share.plus(r_got[:, PROJ:])
        if i == 0:
            s_shares = shares_of(small_share[0], swap(small_share[1], "wsh", 1))
            for wbit in wbits[1:]:
                s_got = swap(stack_values(s_shares[1::2]), "wsh", wbit)
                s_shares = plus_all(s_shares[0::2], s_got)
    r_own = jnp.concatenate([p_share.value(), q_share.value()], axis=1)
    r_own, f_last, small_mine = tie(r_own, f_levels[-1], s_shares[0].value())
    f_levels = f_levels[:-1] + [f_last]
    r_levels, r_keys = widen([r_own[None]], [[0]], cbits[-1])
    for bit in reversed(cbits[1:-1]):
        f_levels, f_keys = widen(f_levels, f_keys, bit)
    r_last, f_last = tie(r_levels[-1], f_levels[-1])
    r_levels = r_levels[:-1] + [r_last]
    f_levels = f_levels[:-1] + [f_last]
    for bit in reversed(cbits[1:-1]):
        r_levels, r_keys = widen(r_levels, r_keys, bit)
    f_levels, f_keys = widen(f_levels, f_keys, 1)
    r_last, f_last, small_mine = tie(r_levels[-1], f_levels[-1], small_mine)
    r_levels = r_levels[:-1] + [r_last]
    f_levels = f_levels[:-1] + [f_last]
    r_levels, r_keys = widen(r_levels, r_keys, 1)
    everyone = lax.all_to_all(
        jnp.broadcast_to(small_mine[None], (size_c,) + small_mine.shape), "ctx", 0, 0, tiled=True
    )
    depth = merge_weight.shape[0]
    grad_down, grad_up = place(
        f_levels, f_keys, nbits, where, ((0, True), (2 * D, False)), ((depth, D), (part, FF)), "place_ffn"
    )
    small_total = jnp.sum(everyone.astype(F32), axis=0)
    grad_proj, grad_merge, grad_value = place(
        r_levels,
        r_keys,
        nbits,
        where,
        ((0, False), (PROJ, True), (PROJ + 2 * D, False)),
        ((part, PROJ), (depth, D), (part, VALUE_WIDTH)),
        "place_rest",
    )
    return (
        output[None],
        input_grad[None],
        grad_proj,
        grad_value,
        grad_merge,
        grad_up,
        grad_down,
        small_total[48],
        small_total[49],
        small_total[50],
        small_total[0:16].T,
        small_total[16:32].T,
        small_total[32:48].T,
        small_total[56:59, :zpart].T,
    )


def solution(mesh):
    rows, flat = P("wsh", None), P("wsh")
    sequence = P("wsh", "ctx", None)
    placed = (sequence, P("wsh", "ctx"), P(), sequence) + (rows,) * 5 + (flat,) * 3 + (rows,) * 4
    return jax.shard_map(
        body,
        mesh=mesh,
        in_specs=placed,
        out_specs=(sequence, sequence) + (rows,) * 5 + (flat,) * 3 + (rows,) * 4,
        check_vma=False,
    )
```

```python
import functools

import jax
import jax.numpy as jnp
from jax import lax
from jax.experimental import pallas as pl
from jax.experimental.pallas import tpu as pltpu
from jax.sharding import PartitionSpec as P

D = 512
Z = 128
VALUE_WIDTH = 1024
NDIM = 16
BLOCK_TOKENS = 128
FF = 1024
PROJ = 2 * D + Z + VALUE_WIDTH
LANES = 128
GROUPS = D // LANES
STATES = NDIM * GROUPS
PARTS = 8
F32 = jnp.float32
BF16 = jnp.bfloat16
EPS = 1e-05
PACE = 1.0
GATE = 8.0
SCAN = 3.0
SLOPE = 9.0
ADJOINT = 6.0
FINISH = 7.0
SMALL_ROWS = 56
SCALE = Z ** (-0.5)
VM = pl.BlockSpec(memory_space=pltpu.VMEM)
SM = pl.BlockSpec(memory_space=pltpu.SMEM)
HBM = pl.BlockSpec(memory_space=pltpu.HBM)
ANY = pl.BlockSpec(memory_space=pl.ANY)


sigmoid = jax.nn.sigmoid


def swish_unit(v):
    return v * sigmoid(v)


def swish_slope(v):
    s = sigmoid(v)
    return s * (1.0 + v * (1.0 - s))


def cost(us):
    return pl.CostEstimate(flops=int(us * PACE * 1e9), bytes_accessed=int(us * PACE * 3e6), transcendentals=0)


def room(mib):
    return pltpu.CompilerParams(vmem_limit_bytes=mib * 1024 * 1024)


def in_hbm(array):
    return pltpu.with_memory_space_constraint(array, pltpu.HBM)


def resident(array):
    return pltpu.with_memory_space_constraint(array, pltpu.VMEM)


def shaped(shape, dtype=F32):
    return jax.ShapeDtypeStruct(shape, dtype)


def dot(a, b):
    return jnp.dot(a, b, preferred_element_type=F32)


def dot_nt(a, b):
    return lax.dot_general(a, b, (((1,), (1,)), ((), ())), preferred_element_type=F32)


def tree_sum(terms):
    terms = list(terms)
    while len(terms) > 1:
        terms = [terms[i] + terms[i + 1] if i + 1 < len(terms) else terms[i] for i in range(0, len(terms), 2)]
    return terms[0]


def decay_tables(par_ref):
    decay = par_ref[0:NDIM, :]
    rate = sigmoid(decay)
    width = jnp.sqrt(sigmoid(-decay) * (1.0 + rate))
    return decay, rate, width


def power_of_rate(decay, count):
    return jnp.exp(-count * jnp.log1p(jnp.exp(-decay)))


def spread(table, j, g):
    return jnp.broadcast_to(table[j : j + 1, g * LANES : (g + 1) * LANES], (PARTS, LANES))


def state_rows(j, g):
    return pl.ds((j * GROUPS + g) * PARTS, PARTS)


def put_runs(ref, value, run):
    stride = ref.shape[-2] // PARTS
    if len(ref.shape) == 2:
        for h in range(PARTS):
            ref[h * stride : h * stride + run, :] = value[h * run : (h + 1) * run, :]
    else:
        for g in range(GROUPS):
            for h in range(PARTS):
                ref[g, h * stride : h * stride + run, :] = value[
                    h * run : (h + 1) * run, g * LANES : (g + 1) * LANES
                ]


def get_runs(ref, run):
    stride = ref.shape[-2] // PARTS
    return jnp.concatenate(
        [
            jnp.concatenate([ref[g, h * stride : h * stride + run, :] for h in range(PARTS)], axis=0)
            for g in range(GROUPS)
        ],
        axis=1,
    )


def at_step(ref, t, g=None):
    stride = ref.shape[-2] // PARTS
    if g is None:
        return ref[pl.ds(t, PARTS, stride=stride), :]
    return ref[g, pl.ds(t, PARTS, stride=stride), :]


def set_step(ref, t, g, value):
    stride = ref.shape[-2] // PARTS
    ref[g, pl.ds(t, PARTS, stride=stride), :] = value


def column(ref, i):
    return jnp.broadcast_to(ref[:, i : i + 1], (ref.shape[0], LANES))


class Mover:
    def __init__(self, sems):
        self.sems = sems
        self.used = 0

    def start(self, *pairs):
        copies = []
        for src, dst in pairs:
            copies.append(pltpu.make_async_copy(src, dst, self.sems.at[self.used]))
            self.used += 1
        for copy in copies:
            copy.start()
        return copies


def wait_all(copies):
    for copy in copies:
        copy.wait()


WEIGHTS = (("proj", PROJ, False), ("value", VALUE_WIDTH, False), ("merge", D, True), ("up", FF, False), ("down", D, True))
TRAVEL = ((0, 1, 2), (3, 4))
TRAVEL_LEVEL = (0, 1)


def travel_cols(i):
    return WEIGHTS[i][1] * (2 if WEIGHTS[i][2] else 1)


def spans_of(weight, base, count, shard_rows):
    _, cols, tall = WEIGHTS[weight]
    if not tall:
        return [(base, 0, cols)]
    return [(base, 0, cols), (base + shard_rows // 2, cols, 2 * cols)]


def small_kernel(dec_ref, inp_ref, rdo_ref, ng_ref, fg_ref, sg_ref, qk_ref, out_ref):
    part = out_ref.shape[1]
    rows = qk_ref.shape[1]
    out_ref[0:NDIM, :] = dec_ref[...]
    out_ref[NDIM : 2 * NDIM, :] = inp_ref[...]
    out_ref[2 * NDIM : 3 * NDIM, :] = rdo_ref[...]
    gains = jnp.concatenate([ng_ref[...], fg_ref[...], sg_ref[...]], axis=0).astype(F32)
    qk = qk_ref[...].astype(F32)
    if rows < part:
        qk = jnp.concatenate([qk, jnp.zeros((3, part - rows), F32)], axis=1)
    out_ref[3 * NDIM : SMALL_ROWS, :] = jnp.concatenate([gains, qk, jnp.zeros((2, part), F32)], axis=0).astype(BF16)


def pack_kernel(me_ref, *refs):
    shards = refs[:5]
    halves = refs[5 : 5 + len(TRAVEL)]
    move = Mover(refs[-1])
    copies = []
    for group, level, half in zip(TRAVEL, TRAVEL_LEVEL, halves):
        side = (me_ref[1] >> level) & 1
        at = 0
        count = half.shape[0]
        for w in group:
            shard_rows = shards[w].shape[0]
            for base, start, stop in spans_of(w, pl.multiple_of(side * count, count), count, shard_rows):
                copies += move.start((shards[w].at[pl.ds(base, count), :], half.at[:, at + start : at + stop]))
            at += travel_cols(w)
    wait_all(copies)


def gate_kernel(*refs):
    refs[-1][...] = jnp.zeros_like(refs[-1])


def build_masks(seg_ref, run, blocks, cont, head, tail=None, labels=None):
    seg = seg_ref[...].astype(F32)
    rows = [seg[:, b * BLOCK_TOKENS : (b + 1) * BLOCK_TOKENS] for b in range(blocks)]
    turned = jnp.concatenate(rows + [rows[0]] * (8 - blocks), axis=0).T
    per_block = PARTS // blocks
    stride = head.shape[0] // PARTS
    top = lax.broadcasted_iota(jnp.int32, (BLOCK_TOKENS, LANES), 0) == 0
    for b in range(blocks):
        col = jnp.broadcast_to(turned[:, b : b + 1], (BLOCK_TOKENS, LANES))
        if labels is not None:
            labels[b * BLOCK_TOKENS : (b + 1) * BLOCK_TOKENS, :] = col
        joined = jnp.where(top | (col == pltpu.roll(col, 1, 0)), 1.0, 0.0)
        for r in range(per_block):
            first = r * run
            part = col[first : first + run, :]
            entry = col[max(first - 1, 0) : max(first - 1, 0) + 1, :]
            last = col[first + run - 1 : first + run, :]
            at = (b * per_block + r) * stride
            cont[at : at + run, :] = joined[first : first + run, :]
            head[at : at + run, :] = jnp.where(part == entry, 1.0, 0.0)
            if tail is not None:
                tail[at : at + run, :] = jnp.where(part == last, 1.0, 0.0)


def normalise(x, gain):
    centred = x - jnp.mean(x, axis=-1, keepdims=True)
    inv = lax.rsqrt(jnp.mean(centred * centred, axis=-1, keepdims=True) + EPS)
    return centred * inv, inv, centred * inv * gain


def front_kernel(keys, run, blocks, *refs):
    n = len(keys)
    me_ref, tok_ref, seg_ref = refs[:3]
    small_refs = refs[3 : 3 + n]
    par_ref, qk_ref, end_ref, pay_ref, far_ref, nrm_ref, mix_ref, cont, head, tail, lab_ref = refs[3 + n : 14 + n]
    xs, os, sums, small = refs[14 + n :]
    me = me_ref[0]
    size_w = small.shape[0]
    zpart = Z // size_w
    for ref, ks in zip(small_refs, keys):
        for i, k in enumerate(ks):
            small[me ^ k] = ref[i].astype(F32)
    par_ref[...] = jnp.concatenate([small[w] for w in range(size_w)], axis=1)
    qk_ref[0:3, :] = jnp.concatenate(
        [small[w, 3 * NDIM + 3 : 3 * NDIM + 6, 0:zpart] for w in range(size_w)], axis=1
    )
    qk_ref[3:8, :] = jnp.zeros((5, Z), F32)
    normed = normalise(tok_ref[...].astype(F32), par_ref[48:49, :])[2]
    nrm_ref[...] = normed
    put_runs(xs, normed, run)
    for ref in (cont, head, tail):
        ref[...] = jnp.zeros_like(ref)
    build_masks(seg_ref, run, blocks, cont, head, tail, lab_ref)
    decay, rate, width = decay_tables(par_ref)
    gain = par_ref[32:48, :] * width * par_ref[16:32, :]
    far = power_of_rate(decay, BLOCK_TOKENS)
    rate_run = power_of_rate(decay, run)
    head_end = at_step(head, run - 1)
    for g in range(GROUPS):
        rates = [spread(rate, j, g) for j in range(NDIM)]
        gains = [spread(gain, j, g) for j in range(NDIM)]
        for j in range(NDIM):
            far_ref[j * GROUPS + g : j * GROUPS + g + 1, :] = far[j : j + 1, g * LANES : (g + 1) * LANES]

        def step(t, states, g=g, rates=rates, gains=gains):
            x_t = at_step(xs, t, g)
            c_t = at_step(cont, t)
            new = [(c_t * rates[j]) * states[j] + x_t for j in range(NDIM)]
            set_step(os, t, g, tree_sum([gains[j] * new[j] for j in range(NDIM)]))
            return tuple(new)

        zero = tuple(jnp.zeros((PARTS, LANES), F32) for _ in range(NDIM))
        ends = lax.fori_loop(0, run, step, zero, unroll=4)
        for j in range(NDIM):
            end_ref[state_rows(j, g), :] = ends[j]
            sums[state_rows(j, g), :] = ends[j] + head_end * spread(rate_run, j, g) * pltpu.roll(ends[j], 1, 0)
    per_block = PARTS // blocks
    seg = seg_ref[...].astype(F32)
    for b in range(blocks):
        ends = [seg[:, b * BLOCK_TOKENS : b * BLOCK_TOKENS + 1], seg[:, (b + 1) * BLOCK_TOKENS - 1 : (b + 1) * BLOCK_TOKENS]]
        bounds = jnp.concatenate([jnp.broadcast_to(e, (1, LANES)) for e in ends] + [jnp.zeros((6, LANES), F32)], axis=0)
        mine = jnp.concatenate([sums[pl.ds((b + 1) * per_block - 1, STATES, stride=PARTS), :], bounds], axis=0)
        for c in range(pay_ref.shape[0]):
            pay_ref[c, b] = mine.astype(BF16)
    mix_ref[...] = get_runs(os, run)


def scan_kernel(blocks, me_ref, order_ref, got_ref, far_ref, table_ref, place, kept):
    def fetch(pos):
        return got_ref[pos, 0:STATES, :].astype(F32)

    scan_states(me_ref, order_ref, fetch, got_ref, far_ref, table_ref, place, kept, blocks, True)


def scan_states(me_ref, order_ref, fetch, bnd_ref, far_ref, table, place, kept, blocks, forward):
    count = place.shape[0]
    per_block = PARTS // blocks

    def note(p, carry):
        place[order_ref[p]] = p
        return carry

    lax.fori_loop(0, count, note, 0, unroll=8)
    far = far_ref[...]

    def step(i, carry):
        state, label = carry
        pos = place[i if forward else count - 1 - i]
        bnd = bnd_ref[pos, STATES : STATES + 2, :].astype(F32)
        first, last = bnd[0:1, :], bnd[1:2, :]
        state = jnp.where((first if forward else last) == label, state, 0.0)
        kept[pos] = state
        state = jnp.where(first == last, far * state, 0.0) + fetch(pos)
        return state, (last if forward else first)

    lax.fori_loop(0, count, step, (jnp.zeros((STATES, LANES), F32), jnp.full((1, LANES), -1.0, F32)), unroll=8)
    for b in range(blocks):
        state = kept[me_ref[1] * blocks + b]
        for r in range(per_block):
            table[pl.ds(b * per_block + r, STATES, stride=PARTS), :] = state


def weight_copies(move, weight, sources, place, me, target, part):
    _, cols, tall = WEIGHTS[weight]
    side = (place >> TRAVEL_LEVEL[next(i for i, g in enumerate(TRAVEL) if weight in g)]) & 1
    copies = []
    for ref, column, key, half in sources:
        tall_by = 2 if tall else 1
        base = (me ^ key) * (part * tall_by)
        if half is None:
            copies += move.start((ref, target.at[pl.ds(pl.multiple_of(base, part), part * tall_by), :]))
            continue
        count = part // 2
        base = base + (side if half == 0 else 1 - side) * count
        for s in range(tall_by):
            rows = pl.ds(pl.multiple_of(base + s * part, count), count)
            copies += move.start((ref.at[:, column + s * cols : column + (s + 1) * cols], target.at[rows, :]))
    return copies


def sources_of(weight, own, own_other, travelled, keys):
    group = next(i for i, g in enumerate(TRAVEL) if weight in g)
    column = sum(travel_cols(w) for w in TRAVEL[group] if w < weight)
    out = [(own, 0, 0, None), (own_other, 0, 1, None)]
    near, far, near_other, far_other = travelled[group]
    for i, k in enumerate(keys):
        out += [(near.at[i], column, k, 0), (far.at[i], column, k, 1)]
        out += [(near_other.at[i], column, k | 1, 0), (far_other.at[i], column, k | 1, 1)]
    return out


def shard_transpose(value, me, size_w, target):
    width = value.shape[1] // size_w
    turned = value[...].T
    for shard in range(size_w):
        p = me ^ shard
        at = ((p & 1) * (size_w // 2) + (p >> 1)) * width
        target[pl.ds(pl.multiple_of(at, width), width), :] = turned[shard * width : (shard + 1) * width, :]


def store_shares(res, size_w, keep_ref, send_ref, col, tall=False):
    half = size_w // 2
    width = res.shape[1]
    steps = 2 if tall else 1
    rows = res.shape[0] // (steps * size_w)
    for i in range(size_w):
        target = keep_ref if i < half else send_ref
        for s in range(steps):
            block = res[(steps * i + s) * rows : (steps * i + s + 1) * rows, :]
            target[i % half, :, col + s * width : col + (s + 1) * width] = block.astype(BF16)


def layer_kernel(wkeys, run, blocks, size_w, *refs):
    me_ref, table, end_ref, par_ref, qk_ref, head, lab_ref, seg_ref, _ = refs[:9]
    refs = (None,) + refs
    mix_h, nrm_h, tok_h, cot_h = refs[10:14]
    own, own_other = refs[14:19], refs[19:24]
    travelled = [refs[24 + 4 * i : 28 + 4 * i] for i in range(len(TRAVEL))]
    refs = refs[24 + 4 * len(TRAVEL) :]
    ein_ref, fgain_ref = refs[:2]
    outs = refs[2:20]
    places = refs[20:38]
    (mix, nrm, tok, cot, os, wp, wv, wm, wu, wd, hid, gat, two, inner, ups, turned, sems) = refs[38:]
    (out_s, keep, send, pre_s, act, low, mlow, gcol, dir_s, rg, ra, val, vsl, prob, q_s, k_s, ssl, sh) = places
    move = Mover(sems)
    pending = []

    def flush(*which):
        for i in which:
            pending.extend(move.start((places[i], outs[i])))

    me = me_ref[0]
    part = D // size_w
    fetched = move.start((mix_h, mix), (nrm_h, nrm), (tok_h, tok), (cot_h, cot))
    loads = []
    for w, target in enumerate((wp, wv, wm, wu, wd)):
        loads.append(
            weight_copies(move, w, sources_of(w, own[w], own_other[w], travelled, wkeys), me_ref[1], me, target, part)
        )

    decay, rate, width = decay_tables(par_ref)
    gain = par_ref[32:48, :] * width * par_ref[16:32, :]
    rate_run = power_of_rate(decay, run)
    head_end = at_step(head, run - 1)
    head_before = pltpu.roll(head_end, 1, 0)
    per_block = PARTS // blocks
    lead = lax.broadcasted_iota(jnp.int32, (PARTS, LANES), 0) % per_block == 0
    for g in range(GROUPS):
        rates = [spread(rate, j, g) for j in range(NDIM)]
        start = []
        for j in range(NDIM):
            ent = table[state_rows(j, g), :]
            inward = pltpu.roll(end_ref[state_rows(j, g), :], 1, 0) + head_before * spread(rate_run, j, g) * ent
            ent = jnp.where(lead, ent, inward)
            ein_ref[state_rows(j, g), :] = ent
            start.append(ent * spread(gain, j, g))

        def step(t, states, g=g, rates=rates):
            new = [rates[j] * states[j] for j in range(NDIM)]
            set_step(os, t, g, tree_sum(new) * at_step(head, t))
            return tuple(new)

        lax.fori_loop(0, run, step, tuple(start), unroll=4)
    wait_all(fetched)
    normed = nrm[...]
    pre = mix[...] + get_runs(os, run) + par_ref[50:51, :] * normed
    pre_s[...] = pre
    act[...] = swish_unit(pre).astype(BF16)
    low[...] = normed.astype(BF16)
    flush(3, 4, 5)

    wait_all(loads[0])
    gates = dot(act[...], wp[:, 0 : D + Z])
    gat[...] = sigmoid(gates[:, 0:D])
    shared_in = gates[:, D : D + Z]
    shared = swish_unit(shared_in)
    sh[...] = shared
    ssl[...] = swish_slope(shared_in)
    q_s[...] = (shared * qk_ref[0:1, :] + qk_ref[1:2, :]).astype(BF16)
    k_s[...] = (shared * qk_ref[2:3, :]).astype(BF16)
    hid[...] = dot(act[...], wp[:, D + Z + VALUE_WIDTH :])
    wait_all(loads[1])
    v = dot(low[...], wv[...])
    s = sigmoid(v)
    val[...] = (v * s).astype(BF16)
    vsl[...] = (s * (1.0 + v * (1.0 - s))).astype(BF16)
    causal = lax.broadcasted_iota(jnp.int32, (BLOCK_TOKENS, BLOCK_TOKENS), 0) >= lax.broadcasted_iota(
        jnp.int32, (BLOCK_TOKENS, BLOCK_TOKENS), 1
    )
    seg = seg_ref[...].astype(F32)
    for b in range(blocks):
        rows = slice(b * BLOCK_TOKENS, (b + 1) * BLOCK_TOKENS)
        allowed = causal & (lab_ref[rows, :] == seg[:, rows])
        scores = jnp.where(allowed, dot_nt(q_s[rows, :], k_s[rows, :]) * SCALE, -1e30)
        exps = jnp.exp(scores - jnp.max(scores, axis=-1, keepdims=True))
        prob[rows, :] = exps / jnp.sum(exps, axis=-1, keepdims=True)
    flush(11, 12, 13, 14, 15, 16, 17)
    r = dot(act[...], wp[:, D + Z : D + Z + VALUE_WIDTH])
    s = sigmoid(r)
    gate = r * s
    rg[...] = gate.astype(BF16)
    slope = s * (1.0 + r * (1.0 - s))
    att = jnp.concatenate(
        [
            dot(
                prob[b * BLOCK_TOKENS : (b + 1) * BLOCK_TOKENS, :].astype(BF16),
                val[b * BLOCK_TOKENS : (b + 1) * BLOCK_TOKENS, :],
            )
            for b in range(blocks)
        ],
        axis=0,
    )
    ra[...] = (slope * att).astype(BF16)
    mlow[...] = (gate * att).astype(BF16)
    flush(6, 9, 10)
    wait_all(loads[2])
    hm = hid[...] + dot(mlow[...], wm[...])
    hid[...] = hm
    x = tok[...].astype(F32)
    residual = x + gat[...] * (swish_unit(hm) - x)
    n, inv, normed_two = normalise(residual, par_ref[49:50, :])
    two[...] = normed_two.astype(BF16)

    wait_all(loads[3])
    u = dot(two[...], wu[...])
    s = sigmoid(u)
    inner[...] = (u * s).astype(BF16)
    slope = s * (1.0 + u * (1.0 - s))
    wait_all(loads[4])
    ups[...] = (dot_nt(cot[...], wd[...]) * slope).astype(BF16)
    shard_transpose(inner, me, size_w, turned)
    store_shares(dot(turned[...], cot[...]), size_w, keep, send, 0, True)
    shard_transpose(two, me, size_w, turned.at[0:D])
    store_shares(dot(turned[0:D, :], ups[...]), size_w, keep, send, 2 * D)
    flush(1, 2)
    out_s[...] = (residual + dot(inner[...], wd[...])).astype(BF16)
    flush(0)
    g_two = dot_nt(ups[...], wu[...])
    fgain_ref[...] = jnp.sum(g_two * n, axis=0, keepdims=True)
    h = g_two * par_ref[49:50, :]
    g_res = cot[...].astype(F32) + inv * (
        h - jnp.mean(h, axis=-1, keepdims=True) - n * jnp.mean(h * n, axis=-1, keepdims=True)
    )
    gate = gat[...]
    s = sigmoid(hm)
    gcol[:, 0:D] = (g_res * (hm * s - x) * gate * (1.0 - gate)).astype(BF16)
    gcol[:, D : 2 * D] = (g_res * gate * (s * (1.0 + hm * (1.0 - s)))).astype(BF16)
    dir_s[...] = g_res * (1.0 - gate)
    flush(7, 8)
    wait_all(pending)


def back_kernel(wkeys, blocks, size_w, *refs):
    me_ref, qk_ref = refs[:2]
    inputs = refs[2:13]
    own, own_other = refs[13], refs[14]
    travelled = refs[15:19]
    refs = refs[19:]
    gqk_ref = refs[0]
    outs = refs[1:5]
    held = refs[5:16]
    keep, send, gproj, gval = refs[16:20]
    wm, gatt, turned, sems = refs[20:]
    gcol, rg, ra, val, prob, k_s, q_s, sh, ssl, vsl, act = held
    move = Mover(sems)
    me = me_ref[0]
    part = D // size_w
    fetched = {0: move.start((inputs[0], held[0]))}
    loads = weight_copies(move, 2, sources_of(2, own, own_other, (travelled,), wkeys), me_ref[1], me, wm, part)
    for i in range(1, 11):
        fetched[i] = move.start((inputs[i], held[i]))

    def need(*which):
        for i in which:
            wait_all(fetched[i])

    need(0)
    wait_all(loads)
    gp = dot_nt(gcol[:, D : 2 * D], wm[...])
    need(1, 2)
    gatt[...] = (gp * rg[...].astype(F32)).astype(BF16)
    gproj[:, D + Z : D + Z + VALUE_WIDTH] = (gp * ra[...].astype(F32)).astype(BF16)
    gproj[:, 0:D] = gcol[:, 0:D]
    gproj[:, D + Z + VALUE_WIDTH :] = gcol[:, D : 2 * D]
    need(3, 4, 5, 6, 7, 8, 9)
    sums = [jnp.zeros((1, Z), F32)] * 3
    for b in range(blocks):
        rows = slice(b * BLOCK_TOKENS, (b + 1) * BLOCK_TOKENS)
        p = prob[rows, :]
        g_att = gatt[rows, :]
        g_probs = dot_nt(g_att, val[rows, :])
        g_values = dot(p.T.astype(BF16), g_att)
        gval[rows, :] = (g_values * vsl[rows, :].astype(F32)).astype(BF16)
        g_scores = p * (g_probs - jnp.sum(g_probs * p, axis=-1, keepdims=True))
        g_raw = g_scores * SCALE
        g_q = dot(g_raw.astype(BF16), k_s[rows, :])
        g_k = dot(g_raw.T.astype(BF16), q_s[rows, :])
        shared = sh[rows, :]
        for i, term in enumerate((g_q * shared, g_q, g_k * shared)):
            sums[i] = sums[i] + jnp.sum(term, axis=0, keepdims=True)
        g_shared = g_q * qk_ref[0:1, :] + g_k * qk_ref[2:3, :]
        gproj[rows, D : D + Z] = (g_shared * ssl[rows, :]).astype(BF16)
    gqk_ref[...] = jnp.concatenate(sums + [jnp.zeros((5, Z), F32)], axis=0)
    pending = move.start((gproj, outs[2]), (gval, outs[3]))
    need(10)
    shard_transpose(act, me, size_w, turned)
    split = D + Z + D
    store_shares(dot(turned[...], gproj[:, 0:split]), size_w, keep, send, 0)
    store_shares(dot(turned[...], gproj[:, split:]), size_w, keep, send, split)
    pending += move.start((send, outs[1]), (keep, outs[0]))
    wait_all(pending)


def back_rest_kernel(wkeys, size_w, *refs):
    me_ref = refs[0]
    inputs = refs[1:6]
    own, own_other = refs[6:8], refs[8:10]
    travelled = [refs[10:14]]
    refs = refs[14:]
    outs = refs[0:4]
    held = refs[4:9]
    keep, send, gact, gnv = refs[9:13]
    wp, wv, turned, sems = refs[13:]
    mlow, gcol, low, gval, gproj = held
    move = Mover(sems)
    me = me_ref[0]
    part = D // size_w
    fetched = [move.start((inputs[i], held[i])) for i in range(5)]
    loads = [
        weight_copies(move, w, sources_of(w, own[w], own_other[w], travelled, wkeys), me_ref[1], me, target, part)
        for w, target in enumerate((wp, wv))
    ]
    wait_all(fetched[0] + fetched[1])
    shard_transpose(mlow, me, size_w, turned)
    store_shares(dot(turned[...], gcol[:, D : 2 * D]), size_w, keep, send, 0, True)
    wait_all(fetched[2] + fetched[3])
    shard_transpose(low, me, size_w, turned.at[0:D])
    store_shares(dot(turned[0:D, :], gval[...]), size_w, keep, send, 2 * D)
    pending = move.start((send, outs[1]), (keep, outs[0]))
    wait_all(fetched[4] + loads[0])
    gact[...] = dot_nt(gproj[...], wp[...])
    pending += move.start((gact, outs[2]))
    wait_all(loads[1])
    gnv[...] = dot_nt(gval[...], wv[...])
    pending += move.start((gnv, outs[3]))
    wait_all(pending)


def adjoint_kernel(run, blocks, gact_ref, pre_ref, nrm_ref, par_ref, cont, head, gmix_ref, gn_ref, lead_ref, pay_ref, gs_ref, gs, os, sums):
    normed = nrm_ref[...]
    g_mix = gact_ref[...] * swish_slope(pre_ref[...])
    gmix_ref[...] = g_mix
    gs_ref[...] = jnp.sum(g_mix * normed, axis=0, keepdims=True)
    put_runs(gs, g_mix, run)
    decay, rate, width = decay_tables(par_ref)
    gain = par_ref[32:48, :] * width * par_ref[16:32, :]
    rate_run = power_of_rate(decay, run)
    head_end = at_step(head, run - 1)
    zero = jnp.zeros((PARTS, LANES), F32)
    for g in range(GROUPS):
        rates = [spread(rate, j, g) for j in range(NDIM)]
        gains = [spread(gain, j, g) for j in range(NDIM)]

        def back(i, carries, g=g, rates=rates, gains=gains):
            t = run - 1 - i
            g_t = at_step(gs, t, g)
            c_t = at_step(cont, t)
            bs = [g_t + carries[j] for j in range(NDIM)]
            set_step(os, t, g, tree_sum([gains[j] * bs[j] for j in range(NDIM)]))
            return tuple((c_t * rates[j]) * bs[j] for j in range(NDIM))

        ends = lax.fori_loop(0, run, back, (zero,) * NDIM, unroll=4)
        for j in range(NDIM):
            lead_ref[state_rows(j, g), :] = ends[j]
            sums[state_rows(j, g), :] = ends[j] + head_end * spread(rate_run, j, g) * pltpu.roll(ends[j], PARTS - 1, 0)
    gn_ref[...] = get_runs(os, run) + par_ref[50:51, :] * g_mix
    per_block = PARTS // blocks
    for b in range(blocks):
        pay_ref[0, b] = sums[pl.ds(b * per_block, STATES, stride=PARTS), :].astype(BF16)


def slope_kernel(run, gmix_ref, nrm_ref, ein_ref, par_ref, cont, u_ref, v_ref, ve_ref, xs, gs):
    put_runs(xs, nrm_ref[...], run)
    put_runs(gs, gmix_ref[...], run)
    _, rate, _ = decay_tables(par_ref)
    zero = jnp.zeros((PARTS, LANES), F32)
    half = NDIM // 2
    for g in range(GROUPS):
        rates = [spread(rate, j, g) for j in range(NDIM)]
        for first in (0, half):
            picks = range(first, first + half)

            def ahead(t, carry, g=g, picks=picks, rates=rates):
                us, vs, uacc, vacc = carry
                g_t = at_step(gs, t, g)
                x_t = at_step(xs, t, g)
                c_t = at_step(cont, t)
                nu, nv, nua, nva = [], [], [], []
                for i, j in enumerate(picks):
                    r = c_t * rates[j]
                    v = r * vs[i] + c_t * us[i]
                    u = r * us[i] + x_t
                    nu.append(u)
                    nv.append(v)
                    nua.append(uacc[i] + g_t * u)
                    nva.append(vacc[i] + g_t * v)
                return tuple(nu), tuple(nv), tuple(nua), tuple(nva)

            us = tuple(ein_ref[state_rows(j, g), :] for j in picks)
            zeros = (zero,) * half
            us, vs, uacc, vacc = lax.fori_loop(0, run, ahead, (us, zeros, zeros, zeros), unroll=4)
            for i, j in enumerate(picks):
                u_ref[state_rows(j, g), :] = uacc[i]
                v_ref[state_rows(j, g), :] = vacc[i]
                ve_ref[state_rows(j, g), :] = vs[i]


def finish_kernel(run, blocks, keys, me_ref, order_ref, *refs):
    n = len(keys)
    back_refs = refs[:n]
    finish(run, blocks, keys, me_ref, order_ref, back_refs, *refs[n:])


def finish(run, blocks, keys, me_ref, order_ref, back_refs, bnd_ref, far_ref, gn_ref, gnv_ref, lead_ref, u_ref, v_ref, ve_ref, tok_ref, dir_ref, par_ref, head, tail, gs_ref, fg_ref, gqk_ref, ig_ref, small_ref, os, table, place, kept, gathered):
    for ref, ks in zip(back_refs, keys):
        for i, k in enumerate(ks):
            gathered[me_ref[1] ^ k] = ref[i].astype(F32)

    def fetch(pos):
        return gathered[pos // blocks, pos % blocks]

    scan_states(me_ref, order_ref, fetch, bnd_ref, far_ref, table, place, kept, blocks, False)
    decay, rate, width = decay_tables(par_ref)
    drive_in = par_ref[16:32, :]
    readout = par_ref[32:48, :]
    drive = width * drive_in
    gain = readout * drive
    rate_run = power_of_rate(decay, run)
    head_after = pltpu.roll(at_step(head, run - 1), PARTS - 1, 0)
    per_block = PARTS // blocks
    final = lax.broadcasted_iota(jnp.int32, (PARTS, LANES), 0) % per_block == per_block - 1
    u_rows, v_rows = [], []
    for g in range(GROUPS):
        rates = [spread(rate, j, g) for j in range(NDIM)]
        start = []
        u_list, v_list = [], []
        for j in range(NDIM):
            at = state_rows(j, g)
            que = table[at, :]
            inward = pltpu.roll(lead_ref[at, :], PARTS - 1, 0) + head_after * spread(rate_run, j, g) * que
            que = jnp.where(final, que, inward)
            start.append(que * spread(gain, j, g))
            u_list.append(jnp.sum(u_ref[at, :], axis=0, keepdims=True))
            v_list.append(jnp.sum(v_ref[at, :] + que * ve_ref[at, :], axis=0, keepdims=True))
        u_rows.append(jnp.concatenate(u_list, axis=0))
        v_rows.append(jnp.concatenate(v_list, axis=0))

        def step(i, states, g=g, rates=rates):
            t = run - 1 - i
            set_step(os, t, g, tree_sum(states) * at_step(tail, t))
            return tuple(rates[j] * states[j] for j in range(NDIM))

        lax.fori_loop(0, run, step, tuple(start), unroll=4)
    u_all = jnp.concatenate(u_rows, axis=1)
    v_all = jnp.concatenate(v_rows, axis=1)
    g_normed = gn_ref[...] + gnv_ref[...] + get_runs(os, run)
    x = tok_ref[...].astype(F32)
    centred = x - jnp.mean(x, axis=-1, keepdims=True)
    var = jnp.mean(centred * centred, axis=-1, keepdims=True)
    inv = lax.rsqrt(var + EPS)
    n = centred * inv
    h = g_normed * par_ref[48:49, :]
    back = inv * (h - jnp.mean(h, axis=-1, keepdims=True) - n * jnp.mean(h * n, axis=-1, keepdims=True))
    ig_ref[...] = (dir_ref[...] + back).astype(BF16)
    size_w = 2 * small_ref.shape[1]
    half = size_w // 2
    part = small_ref.shape[3]
    zpart = Z // size_w
    me = me_ref[0]
    grads = jnp.concatenate(
        [
            readout * drive * v_all * rate * (1.0 - rate)
            - readout * u_all * drive_in * rate * rate * (1.0 - rate) / width,
            readout * u_all * width,
            drive * u_all,
            jnp.sum(g_normed * n, axis=0, keepdims=True),
            fg_ref[...],
            gs_ref[...],
            jnp.zeros((5, D), F32),
        ],
        axis=0,
    )
    for w in range(size_w):
        p = me ^ w
        qk = gqk_ref[0:8, w * zpart : (w + 1) * zpart]
        if zpart < part:
            qk = jnp.concatenate([qk, jnp.zeros((8, part - zpart), F32)], axis=1)
        both = jnp.concatenate([grads[:, w * part : (w + 1) * part], qk], axis=0)
        small_ref[p & 1, p >> 1] = both.astype(BF16)


def swap(value, axis, bit):
    size = lax.axis_size(axis)
    return lax.ppermute(value, axis, [(i, i ^ bit) for i in range(size)])


def bits_of(size):
    out, bit = [], 1
    while bit < size:
        out.append(bit)
        bit *= 2
    return out


def tie(*values):
    return lax.optimization_barrier(values)


class Share:
    def __init__(self, terms, count, cols):
        self.terms = terms
        self.count = count
        self.cols = cols

    def halve(self, level):
        count = self.count // 2

        def moved(first, other):
            return lambda me: first(me) + (((me >> level) & 1) ^ other) * count

        stay = Share([(a, i, moved(f, 0), c) for a, i, f, c in self.terms], count, self.cols)
        go = Share([(a, i, moved(f, 1), c) for a, i, f, c in self.terms], count, self.cols)
        return stay, go

    def plus(self, array, lead=(), col=0):
        return Share(self.terms + [(array, lead, lambda me: 0, col)], self.count, self.cols)


def plain_sum(share, me):
    total = None
    for array, lead, first, col in share.terms:
        for i in lead:
            array = array[i]
        array = lax.dynamic_slice_in_dim(array, first(me), share.count, 0)[:, :, col : col + share.cols].astype(F32)
        total = array if total is None else total + array
    return total.astype(BF16)


def sum_kernel(plan, n, *refs):
    me = refs[0][1]
    arrays = refs[1 : 1 + n]
    outs = refs[1 + n :]
    for out, stacked in zip(outs, plan):
        for i, row in enumerate(stacked):
            column = 0
            for terms, count, cols in row:
                total = None
                for k, lead, first, col in terms:
                    value = arrays[k][(*lead, pl.ds(first(me), count), slice(None), slice(col, col + cols))].astype(F32)
                    total = value if total is None else total + value
                out[i, :, :, column : column + cols] = total.astype(BF16)
                column += cols


def sums(where, *outputs):
    first = outputs[0][0][0]
    rows = first.terms[0][0].shape[-2]
    if rows % 8:
        return [
            jnp.stack([jnp.concatenate([plain_sum(share, where[1]) for share in row], axis=2) for row in stacked])
            for stacked in outputs
        ]
    arrays, plan, shapes = [], [], []
    for stacked in outputs:
        rows_plan = []
        for row in stacked:
            row_plan = []
            for share in row:
                terms = []
                for array, lead, start, col in share.terms:
                    k = next((k for k, a in enumerate(arrays) if a is array), None)
                    if k is None:
                        k = len(arrays)
                        arrays.append(array)
                    terms.append((k, lead, start, col))
                row_plan.append((terms, share.count, share.cols))
            rows_plan.append(row_plan)
        plan.append(rows_plan)
        shapes.append(pltpu.VMEM((len(stacked), stacked[0][0].count, rows, sum(s.cols for s in stacked[0])), BF16))
    return pl.pallas_call(
        functools.partial(sum_kernel, plan, len(arrays)),
        out_shape=tuple(shapes),
        in_specs=[SM] + [VM] * len(arrays),
        out_specs=(VM,) * len(shapes),
        cost_estimate=cost(1),
        compiler_params=room(12),
        name="sums",
    )(where, *[resident(array) for array in arrays])


def far_keys(size):
    keys = []
    for bit in reversed(bits_of(size)[1:]):
        keys += [k | bit for k in [0] + keys]
    return keys


def position(place, order):
    out = 0
    for i, level in enumerate(order):
        out = out | (((place >> level) & 1) << (len(order) - 1 - i))
    return out


def place_kernel(keys, order, spans, *refs):
    n = len(keys)
    me = refs[0][1]
    pieces = refs[1 : 1 + n]
    outs = refs[1 + n :]
    for ref, ks in zip(pieces, keys):
        rows = ref.shape[1]
        for i, k in enumerate(ks):
            base = position(me ^ k, order) * rows
            for out, (start, tall) in zip(outs, spans):
                width = out.shape[1]
                for s in range(2 if tall else 1):
                    at = pl.ds(pl.multiple_of(base + s * (out.shape[0] // 2), rows), rows)
                    out[at, :] = ref[i, :, start + s * width : start + (s + 1) * width].astype(F32)


def place(levels, keys, order, where, spans, shapes, name):
    rows = levels[0].shape[1]
    if rows % 8:
        return place_by_gather(levels, keys, order, where, spans, shapes)
    return pl.pallas_call(
        functools.partial(place_kernel, keys, order, spans),
        out_shape=tuple(shaped(s) for s in shapes),
        in_specs=[SM] + [VM] * len(levels),
        cost_estimate=cost(2.5),
        compiler_params=room(16),
        name=name,
    )(where, *[resident(level) for level in levels])


def place_by_gather(levels, keys, order, where, spans, shapes):
    flat = [k for level in keys for k in level]
    index = jnp.array([flat.index(k) for k in range(len(flat))], jnp.int32)
    holder = {position(device, order): device for device in range(len(flat))}
    picks = index[where[1] ^ jnp.array([holder[i] for i in range(len(flat))], jnp.int32)]
    block = jnp.concatenate(levels, axis=0)[picks].astype(F32)
    block = block.reshape(-1, block.shape[-1])
    outs = []
    for (start, tall), (rows, width) in zip(spans, shapes):
        columns = [block[:, start + s * width : start + (s + 1) * width] for s in range(2 if tall else 1)]
        outs.append(jnp.concatenate(columns, axis=0))
    return tuple(outs)


def body(
    tokens,
    segments,
    deal_order,
    cotangent,
    proj_weight,
    value_weight,
    merge_weight,
    ffn_up,
    ffn_down,
    norm_gain,
    ffn_gain,
    skip_gain,
    ema_decay,
    ema_input,
    ema_output,
    query_key,
):
    size_w, size_c = lax.axis_size("wsh"), lax.axis_size("ctx")
    me_w, me_c = lax.axis_index("wsh"), lax.axis_index("ctx")
    where = jnp.stack([me_w, me_c]).astype(jnp.int32)
    wbits, cbits = bits_of(size_w), bits_of(size_c)
    part = D // size_w
    zpart = Z // size_w
    half = size_w // 2
    rc = tokens.shape[1]
    blocks = rc // BLOCK_TOKENS
    run = rc // PARTS
    count = deal_order.shape[0]
    shards = (proj_weight, value_weight, merge_weight, ffn_up, ffn_down)
    group_cols = [sum(travel_cols(w) for w in group) for group in TRAVEL]

    small = pl.pallas_call(small_kernel, out_shape=shaped((SMALL_ROWS, part), BF16), cost_estimate=cost(1), compiler_params=room(2), name="small")(
        ema_decay.T,
        ema_input.T,
        ema_output.T,
        norm_gain[None],
        ffn_gain[None],
        skip_gain[None],
        query_key.T,
    )
    travel = pl.pallas_call(
        pack_kernel,
        out_shape=tuple(shaped((part // 2, c), BF16) for c in group_cols),
        in_specs=[SM] + [HBM] * 5,
        scratch_shapes=[pltpu.SemaphoreType.DMA((16,))],
        cost_estimate=cost(3),
        compiler_params=room(8),
        name="pack",
    )(where, *shards)

    def far_pieces(block):
        have = []
        for bit in reversed(wbits[1:]):
            sent = jnp.concatenate([block[None]] + have, axis=0) if have else block[None]
            have.append(swap(sent, "wsh", bit))
        return have[0] if len(have) == 1 else jnp.concatenate(have, axis=0)

    wkeys = far_keys(size_w)
    small_near = swap(small[None], "wsh", 1)
    small_far = far_pieces(small)
    near = [far_pieces(travel[0])]
    small_far, second = tie(small_far, travel[1])
    near.append(far_pieces(second))
    small_last = swap(small_far, "wsh", 1)
    skeys = [[0], [1], wkeys, [k | 1 for k in wkeys]]

    pad_run = run + 1
    runs_scratch = pltpu.VMEM((GROUPS, PARTS * pad_run, LANES), F32)
    mask_shape = shaped((PARTS * pad_run, LANES))
    kept_scratch = pltpu.VMEM((count, STATES, LANES), F32)
    table_scratch = pltpu.VMEM((STATES * PARTS, LANES), F32)
    table = shaped((STATES * PARTS, LANES))
    par, qk, ends, payload, far, normed, mix_local, cont, head, tail, label_cols = pl.pallas_call(
        functools.partial(front_kernel, skeys, run, blocks),
        out_shape=(
            shaped((SMALL_ROWS, D)),
            shaped((8, Z)),
            table,
            shaped((size_c, blocks, STATES + 8, LANES), BF16),
            shaped((STATES, LANES)),
            shaped((rc, D)),
            shaped((rc, D)),
            mask_shape,
            mask_shape,
            mask_shape,
            shaped((rc, LANES)),
        ),
        in_specs=[SM] + [VM] * 6,
        scratch_shapes=[
            runs_scratch,
            runs_scratch,
            table_scratch,
            pltpu.VMEM((size_w, SMALL_ROWS, part), F32),
        ],
        cost_estimate=cost(7),
        compiler_params=room(60),
        name="front",
    )(where, tokens[0], segments, small[None], small_near, small_far, small_last)
    got = lax.all_to_all(payload, "ctx", 0, 0, tiled=True).reshape(count, STATES + 8, LANES)

    for i in range(len(TRAVEL)):
        near[i] = tie(payload, near[i])[1]
    across = [swap(piece, "ctx", 1 << level) for piece, level in zip(near, TRAVEL_LEVEL)]
    near_other = [swap(piece, "wsh", 1) for piece in near]
    gate = pl.pallas_call(
        gate_kernel,
        out_shape=shaped((8, LANES)),
        in_specs=[ANY] * len(TRAVEL),
        cost_estimate=cost(GATE),
        compiler_params=room(1),
        name="gate",
    )(*across)
    tied = tie(payload, *shards)
    own_other = [swap(shard, "wsh", 1) for shard in tied[1:]]
    travelled = [(a, b, c, swap(b, "wsh", 1)) for a, b, c in zip(near, across, near_other)]

    entered = pl.pallas_call(
        functools.partial(scan_kernel, blocks),
        out_shape=table,
        in_specs=[SM, SM, VM, VM],
        scratch_shapes=[pltpu.SMEM((count,), jnp.int32), kept_scratch],
        cost_estimate=cost(SCAN),
        compiler_params=room(8),
        name="scan",
    )(where, deal_order, got, far)

    saved = (
        shaped((rc, D), BF16),
        shaped((half, part, 2 * D + FF), BF16),
        shaped((half, part, 2 * D + FF), BF16),
        shaped((rc, D)),
        shaped((rc, D), BF16),
        shaped((rc, D), BF16),
        shaped((rc, VALUE_WIDTH), BF16),
        shaped((rc, 2 * D), BF16),
        shaped((rc, D)),
        shaped((rc, VALUE_WIDTH), BF16),
        shaped((rc, VALUE_WIDTH), BF16),
        shaped((rc, VALUE_WIDTH), BF16),
        shaped((rc, VALUE_WIDTH), BF16),
        shaped((rc, BLOCK_TOKENS)),
        shaped((rc, Z), BF16),
        shaped((rc, Z), BF16),
        shaped((rc, Z)),
        shaped((rc, Z)),
    )

    def pinned(shapes):
        return tuple(pltpu.HBM(s.shape, s.dtype) for s in shapes)

    def vmem_of(shapes):
        return [pltpu.VMEM(s.shape, s.dtype) for s in shapes]

    copies_each = 2 + 4 * len(wkeys)
    results = pl.pallas_call(
        functools.partial(layer_kernel, wkeys, run, blocks, size_w),
        out_shape=(table, shaped((1, D))) + pinned(saved),
        in_specs=[SM] + [VM] * 8 + [HBM] * (4 + 10 + 4 * len(TRAVEL)),
        out_specs=(VM, VM) + (HBM,) * len(saved),
        scratch_shapes=vmem_of(saved)
        + [
            pltpu.VMEM((rc, D), F32),
            pltpu.VMEM((rc, D), F32),
            pltpu.VMEM((rc, D), BF16),
            pltpu.VMEM((rc, D), BF16),
            runs_scratch,
            pltpu.VMEM((D, PROJ), BF16),
            pltpu.VMEM((D, VALUE_WIDTH), BF16),
            pltpu.VMEM((VALUE_WIDTH, D), BF16),
            pltpu.VMEM((D, FF), BF16),
            pltpu.VMEM((FF, D), BF16),
            pltpu.VMEM((rc, D), F32),
            pltpu.VMEM((rc, D), F32),
            pltpu.VMEM((rc, D), BF16),
            pltpu.VMEM((rc, FF), BF16),
            pltpu.VMEM((rc, FF), BF16),
            pltpu.VMEM((FF, rc), BF16),
            pltpu.SemaphoreType.DMA((4 + len(saved) + 7 * copies_each,)),
        ],
        cost_estimate=cost(17),
        compiler_params=room(60),
        name="layer",
    )(
        where,
        entered,
        ends,
        par,
        qk,
        head,
        label_cols,
        segments,
        gate,
        *map(in_hbm, (mix_local, normed, tokens[0], cotangent[0], *shards, *own_other)),
        *[in_hbm(piece) for group in travelled for piece in group],
    )
    ein, grad_ffn_gain = results[:2]
    (
        output,
        ffn_keep,
        ffn_send,
        pre_active,
        active_low,
        normed_low,
        merged_low,
        gcols,
        direct,
        reset_gate,
        reset_slope,
        values,
        value_slope,
        probs,
        queries,
        keys_low,
        shared_slope,
        shared,
    ) = results[2:]

    def shares_of(keep, got):
        cut = (half, size_c, keep.shape[1] // size_c, keep.shape[2])
        keep, got = keep.reshape(cut), got.reshape(cut)
        return [
            Share([(keep, (i,), lambda me: 0, 0), (got, (i,), lambda me: 0, 0)], size_c, cut[3]) for i in range(half)
        ]

    def plus_all(shares, got):
        return [share.plus(got, (i,)) for i, share in enumerate(shares)]

    def rows_of(shares):
        return [[share] for share in shares]

    def widen(levels, keys, bit):
        block = levels[0] if len(levels) == 1 else jnp.concatenate(levels, axis=0)
        return levels + [swap(block, "ctx", bit)], keys + [[k | bit for level in keys for k in level]]

    f_got = swap(ffn_send, "wsh", 1)
    copies_weight = 2 * copies_each
    gproj_shape, gval_shape = shaped((rc, PROJ), BF16), shaped((rc, VALUE_WIDTH), BF16)
    back_in = (
        gcols,
        reset_gate,
        reset_slope,
        values,
        probs,
        keys_low,
        queries,
        shared,
        shared_slope,
        value_slope,
        active_low,
    )
    p_shapes = (shaped((half, part, PROJ), BF16),) * 2 + (gproj_shape, gval_shape)
    grad_qk, p_keep, p_send, gproj, gval = pl.pallas_call(
        functools.partial(back_kernel, wkeys, blocks, size_w),
        out_shape=(shaped((8, Z)),) + pinned(p_shapes),
        in_specs=[SM, VM] + [HBM] * (11 + 2 + 4),
        out_specs=(VM,) + (HBM,) * 4,
        scratch_shapes=vmem_of(back_in)
        + vmem_of(p_shapes)
        + [
            pltpu.VMEM((VALUE_WIDTH, D), BF16),
            pltpu.VMEM((rc, VALUE_WIDTH), BF16),
            pltpu.VMEM((D, rc), BF16),
            pltpu.SemaphoreType.DMA((15 + copies_weight,)),
        ],
        cost_estimate=cost(9),
        compiler_params=room(30),
        name="back",
    )(where, qk, *map(in_hbm, (*back_in, merge_weight, own_other[2], *travelled[0])))
    f_got, p_send = tie(f_got, p_send)
    p_got = swap(p_send, "wsh", 1)
    gproj = tie(p_send, gproj)[1]
    rest_in = (merged_low, gcols, normed_low, gval, gproj)
    q_cols = 2 * D + VALUE_WIDTH
    q_shapes = (shaped((half, part, q_cols), BF16),) * 2 + (shaped((rc, D)),) * 2
    q_keep, q_send, grad_active, grad_normed_value = pl.pallas_call(
        functools.partial(back_rest_kernel, wkeys, size_w),
        out_shape=pinned(q_shapes),
        in_specs=[SM] + [HBM] * (5 + 4 + 4),
        out_specs=(HBM,) * 4,
        scratch_shapes=vmem_of(rest_in)
        + vmem_of(q_shapes)
        + [
            pltpu.VMEM((D, PROJ), BF16),
            pltpu.VMEM((D, VALUE_WIDTH), BF16),
            pltpu.VMEM((VALUE_WIDTH, rc), BF16),
            pltpu.SemaphoreType.DMA((9 + copies_weight,)),
        ],
        cost_estimate=cost(7),
        compiler_params=room(30),
        name="back_rest",
    )(where, *map(in_hbm, (*rest_in, *shards[:2], *own_other[:2], *travelled[0])))

    top = len(cbits)
    pq_rounds = [(("w", k), ("c", 0) if k == 0 else ("w", k - 1)) for k in range(len(wbits) - 1)]
    pq_rounds.append((("c", 0), ("w", len(wbits) - 2)))
    r_order = [0] + list(range(1, top))
    f_steps = [("c", 1)] + [("w", k) for k in range(len(wbits) - 1)]
    f_steps += [("c", k) for k in range(2, top)] + [("c", 0)]
    f_order = list(range(1, top)) + [0]

    def cut(shares, step):
        kind, k = step
        if kind == "w":
            return shares[0::2], rows_of(shares[1::2])
        both = [share.halve(k) for share in shares]
        return [stay for stay, _ in both], rows_of([away for _, away in both])

    def send(value, step):
        kind, k = step
        return swap(value, "wsh", wbits[k + 1]) if kind == "w" else swap(value, "ctx", cbits[k])

    p_shares, f_shares = shares_of(p_keep, p_got), shares_of(ffn_keep, f_got)
    p_shares, p_rows = cut(p_shares, pq_rounds[0][0])
    f_shares, f_rows = cut(f_shares, f_steps[0])
    p_go, f_go = sums(where, p_rows, f_rows)
    p_go, f_go, q_send = tie(p_go, f_go, q_send)
    q_got = swap(q_send, "wsh", 1)
    p_got, f_got = send(p_go, pq_rounds[0][0]), send(f_go, f_steps[0])
    q_shares, q_rows = cut(shares_of(q_keep, q_got), pq_rounds[0][1])
    (q_go,) = sums(where, q_rows)
    q_go, grad_active = tie(q_go, grad_active)
    q_got = send(q_go, pq_rounds[0][1])
    g_mix, gn_local, leads, payload_back, grad_skip = pl.pallas_call(
        functools.partial(adjoint_kernel, run, blocks),
        out_shape=(
            shaped((rc, D)),
            shaped((rc, D)),
            table,
            shaped((1, blocks, STATES, LANES), BF16),
            shaped((1, D)),
        ),
        scratch_shapes=[runs_scratch] * 2 + [table_scratch],
        cost_estimate=cost(ADJOINT),
        compiler_params=room(20),
        name="adjoint",
    )(grad_active, pre_active, normed, par, cont, head)
    b_got = swap(payload_back, "ctx", cbits[-1])
    u_part, v_part, v_end = pl.pallas_call(
        functools.partial(slope_kernel, run),
        out_shape=(table, table, table),
        scratch_shapes=[runs_scratch] * 2,
        cost_estimate=cost(SLOPE),
        compiler_params=room(16),
        name="slope",
    )(g_mix, normed, ein, par, cont)

    p_got, q_got, f_got, b_got, u_part = tie(p_got, q_got, f_got, b_got, u_part)
    b_levels, b_keys = [payload_back, b_got], [[0], [cbits[-1]]]
    b_bits = list(reversed(cbits[:-1]))

    def spread_back(levels, keys):
        bit = b_bits.pop(0)
        block = jnp.concatenate(levels, axis=0)
        return levels + [swap(block, "ctx", bit)], keys + [[k | bit for level in keys for k in level]]

    p_shares, q_shares, f_shares = plus_all(p_shares, p_got), plus_all(q_shares, q_got), plus_all(f_shares, f_got)
    for number in range(1, len(pq_rounds)):
        p_step, q_step = pq_rounds[number]
        p_shares, p_rows = cut(p_shares, p_step)
        q_shares, q_rows = cut(q_shares, q_step)
        f_shares, f_rows = cut(f_shares, f_steps[number])
        p_go, q_go, f_go = sums(where, p_rows, q_rows, f_rows)
        p_go, q_go, f_go, b_levels[-1] = tie(p_go, q_go, f_go, b_levels[-1])
        p_got, q_got, f_got = send(p_go, p_step), send(q_go, q_step), send(f_go, f_steps[number])
        if len(b_bits) > 1:
            b_levels, b_keys = spread_back(b_levels, b_keys)
        p_got, q_got, f_got, b_levels[-1] = tie(p_got, q_got, f_got, b_levels[-1])
        p_shares, q_shares, f_shares = plus_all(p_shares, p_got), plus_all(q_shares, q_got), plus_all(f_shares, f_got)
    (p_share,), (q_share,) = p_shares, q_shares

    def finished():
        input_grad, small_share = pl.pallas_call(
            functools.partial(finish_kernel, run, blocks, b_keys),
            out_shape=(shaped((rc, D), BF16), shaped((2, half, SMALL_ROWS + 8, part), BF16)),
            in_specs=[SM, SM] + [VM] * (16 + len(b_keys)),
            scratch_shapes=[
                runs_scratch,
                table_scratch,
                pltpu.SMEM((count,), jnp.int32),
                kept_scratch,
                pltpu.VMEM((size_c, blocks, STATES, LANES), F32),
            ],
            cost_estimate=cost(FINISH),
            compiler_params=room(20),
            name="finish",
        )(
            where,
            deal_order,
            *b_levels,
            got,
            far,
            gn_local,
            grad_normed_value,
            leads,
            u_part,
            v_part,
            v_end,
            tokens[0],
            direct,
            par,
            head,
            tail,
            grad_skip,
            grad_ffn_gain,
            grad_qk,
        )
        return input_grad, small_share

    late = None
    for k in range(1, top):
        f_step = f_steps[len(pq_rounds) + k - 1]
        p_share, p_away = p_share.halve(k)
        q_share, q_away = q_share.halve(k)
        f_shares, f_rows = cut(f_shares, f_step)
        r_go, f_go = sums(where, [[p_away, q_away]], f_rows)
        r_go, f_go, b_levels[-1] = tie(r_go, f_go, b_levels[-1])
        r_got, f_got = swap(r_go, "ctx", cbits[k]), send(f_go, f_step)
        if b_bits:
            b_levels, b_keys = spread_back(b_levels, b_keys)
            r_got, f_got, b_levels[-1] = tie(r_got, f_got, b_levels[-1])
        elif late is None:
            input_grad, late = finished()
            r_got, f_got, late = tie(r_got, f_got, late)
        p_share, q_share = p_share.plus(r_got, (0,)), q_share.plus(r_got, (0,), PROJ)
        f_shares = plus_all(f_shares, f_got)
    r_own, f_own = sums(where, [[p_share, q_share]], rows_of(f_shares))
    r_own, f_own, late = tie(r_own, f_own, late)
    r_levels, r_keys, f_levels, f_keys = [r_own[0]], [[0]], [f_own[0]], [[0]]
    s_steps = [("w", k) for k in range(len(wbits))] + [("c", k) for k in range(top)]
    s_pieces = late

    def small_step(pieces, step):
        kind, k = step
        if kind == "w" and k == 0:
            return pieces[0].astype(F32) + swap(pieces[1], "wsh", 1).astype(F32)
        if kind == "w":
            return pieces[0::2] + swap(pieces[1::2].astype(BF16), "wsh", wbits[k]).astype(F32)
        low = pieces.astype(BF16)
        return low.astype(F32) + swap(low, "ctx", cbits[k]).astype(F32)

    for number, (r_bit, f_bit) in enumerate(zip(reversed(cbits), [1] + cbits[:0:-1])):
        r_levels, r_keys = widen(r_levels, r_keys, r_bit)
        f_levels, f_keys = widen(f_levels, f_keys, f_bit)
        rounds_left = top - number
        todo = -(-len(s_steps) // rounds_left)
        for step in s_steps[:todo]:
            s_pieces = small_step(s_pieces, step)
        s_steps = s_steps[todo:]
        if r_bit > 1:
            r_last, f_last, s_pieces = tie(r_levels[-1], f_levels[-1], s_pieces)
            r_levels, f_levels = r_levels[:-1] + [r_last], f_levels[:-1] + [f_last]
    small_total = s_pieces[0]
    depth = merge_weight.shape[0]
    grad_down, grad_up = place(
        f_levels, f_keys, f_order, where, ((0, True), (2 * D, False)), ((depth, D), (part, FF)), "place_ffn"
    )
    grad_proj, grad_merge, grad_value = place(
        r_levels,
        r_keys,
        r_order,
        where,
        ((0, False), (PROJ, True), (PROJ + 2 * D, False)),
        ((part, PROJ), (depth, D), (part, VALUE_WIDTH)),
        "place_rest",
    )
    return (
        output[None],
        input_grad[None],
        grad_proj,
        grad_value,
        grad_merge,
        grad_up,
        grad_down,
        small_total[48],
        small_total[49],
        small_total[50],
        small_total[0:16].T,
        small_total[16:32].T,
        small_total[32:48].T,
        small_total[56:59, :zpart].T,
    )


def solution(mesh):
    rows, flat = P("wsh", None), P("wsh")
    sequence = P("wsh", "ctx", None)
    placed = (sequence, P("wsh", "ctx"), P(), sequence) + (rows,) * 5 + (flat,) * 3 + (rows,) * 4
    return jax.shard_map(
        body,
        mesh=mesh,
        in_specs=placed,
        out_specs=(sequence, sequence) + (rows,) * 5 + (flat,) * 3 + (rows,) * 4,
        check_vma=False,
    )
```

```python
import functools

import jax
import jax.numpy as jnp
from jax import lax
from jax.experimental import pallas as pl
from jax.experimental.pallas import tpu as pltpu
from jax.sharding import PartitionSpec as P

D = 512
Z = 128
VALUE_WIDTH = 1024
NDIM = 16
BLOCK_TOKENS = 128
FF = 1024
PROJ = 2 * D + Z + VALUE_WIDTH
LANES = 128
GROUPS = D // LANES
STATES = NDIM * GROUPS
PARTS = 8
F32 = jnp.float32
BF16 = jnp.bfloat16
EPS = 1e-05
PACE = 1.0
FRONT = 3.0
GATE = 8.0
SCAN = 0.1
SLOPE = 3.0
ADJOINT = 2.0
FINISH = 1.0
SMALL_ROWS = 56
SCALE = Z ** (-0.5)
VM = pl.BlockSpec(memory_space=pltpu.VMEM)
SM = pl.BlockSpec(memory_space=pltpu.SMEM)
HBM = pl.BlockSpec(memory_space=pltpu.HBM)
ANY = pl.BlockSpec(memory_space=pl.ANY)


sigmoid = jax.nn.sigmoid


def swish_unit(v):
    return v * sigmoid(v)


def swish_slope(v):
    s = sigmoid(v)
    return s * (1.0 + v * (1.0 - s))


def cost(us):
    return pl.CostEstimate(flops=int(us * PACE * 1e9), bytes_accessed=int(us * PACE * 3e6), transcendentals=0)


def room(mib):
    return pltpu.CompilerParams(vmem_limit_bytes=mib * 1024 * 1024)


def in_hbm(array):
    return pltpu.with_memory_space_constraint(array, pltpu.HBM)


def resident(array):
    return pltpu.with_memory_space_constraint(array, pltpu.VMEM)


def shaped(shape, dtype=F32):
    return jax.ShapeDtypeStruct(shape, dtype)


def dot(a, b):
    return jnp.dot(a, b, preferred_element_type=F32)


def dot_nt(a, b):
    return lax.dot_general(a, b, (((1,), (1,)), ((), ())), preferred_element_type=F32)


def tree_sum(terms):
    terms = list(terms)
    while len(terms) > 1:
        terms = [terms[i] + terms[i + 1] if i + 1 < len(terms) else terms[i] for i in range(0, len(terms), 2)]
    return terms[0]


def decay_tables(par_ref):
    decay = par_ref[0:NDIM, :]
    rate = sigmoid(decay)
    width = jnp.sqrt(sigmoid(-decay) * (1.0 + rate))
    return decay, rate, width


def power_of_rate(decay, count):
    return jnp.exp(-count * jnp.log1p(jnp.exp(-decay)))


def spread(table, j, g):
    return jnp.broadcast_to(table[j : j + 1, g * LANES : (g + 1) * LANES], (PARTS, LANES))


def state_rows(j, g):
    return pl.ds((j * GROUPS + g) * PARTS, PARTS)


def put_runs(ref, value, run):
    stride = ref.shape[-2] // PARTS
    if len(ref.shape) == 2:
        for h in range(PARTS):
            ref[h * stride : h * stride + run, :] = value[h * run : (h + 1) * run, :]
    else:
        for g in range(GROUPS):
            for h in range(PARTS):
                ref[g, h * stride : h * stride + run, :] = value[
                    h * run : (h + 1) * run, g * LANES : (g + 1) * LANES
                ]


def get_runs(ref, run):
    stride = ref.shape[-2] // PARTS
    return jnp.concatenate(
        [
            jnp.concatenate([ref[g, h * stride : h * stride + run, :] for h in range(PARTS)], axis=0)
            for g in range(GROUPS)
        ],
        axis=1,
    )


def at_step(ref, t, g=None):
    stride = ref.shape[-2] // PARTS
    if g is None:
        return ref[pl.ds(t, PARTS, stride=stride), :]
    return ref[g, pl.ds(t, PARTS, stride=stride), :]


def set_step(ref, t, g, value):
    stride = ref.shape[-2] // PARTS
    ref[g, pl.ds(t, PARTS, stride=stride), :] = value


def column(ref, i):
    return jnp.broadcast_to(ref[:, i : i + 1], (ref.shape[0], LANES))


class Mover:
    def __init__(self, sems):
        self.sems = sems
        self.used = 0

    def start(self, *pairs):
        copies = []
        for src, dst in pairs:
            copies.append(pltpu.make_async_copy(src, dst, self.sems.at[self.used]))
            self.used += 1
        for copy in copies:
            copy.start()
        return copies


def wait_all(copies):
    for copy in copies:
        copy.wait()


WEIGHTS = (("proj", PROJ, False), ("value", VALUE_WIDTH, False), ("merge", D, True), ("up", FF, False), ("down", D, True))
TRAVEL = ((0, 1, 2), (3, 4))
TRAVEL_LEVEL = (0, 1)


def travel_cols(i):
    return WEIGHTS[i][1] * (2 if WEIGHTS[i][2] else 1)


def spans_of(weight, base, count, shard_rows):
    _, cols, tall = WEIGHTS[weight]
    if not tall:
        return [(base, 0, cols)]
    return [(base, 0, cols), (base + shard_rows // 2, cols, 2 * cols)]


def small_kernel(dec_ref, inp_ref, rdo_ref, ng_ref, fg_ref, sg_ref, qk_ref, out_ref):
    part = out_ref.shape[1]
    rows = qk_ref.shape[1]
    out_ref[0:NDIM, :] = dec_ref[...]
    out_ref[NDIM : 2 * NDIM, :] = inp_ref[...]
    out_ref[2 * NDIM : 3 * NDIM, :] = rdo_ref[...]
    gains = jnp.concatenate([ng_ref[...], fg_ref[...], sg_ref[...]], axis=0).astype(F32)
    qk = qk_ref[...].astype(F32)
    if rows < part:
        qk = jnp.concatenate([qk, jnp.zeros((3, part - rows), F32)], axis=1)
    out_ref[3 * NDIM : SMALL_ROWS, :] = jnp.concatenate([gains, qk, jnp.zeros((2, part), F32)], axis=0).astype(BF16)


def pack_kernel(me_ref, *refs):
    shards = refs[:5]
    halves = refs[5 : 5 + len(TRAVEL)]
    move = Mover(refs[-1])
    copies = []
    for group, level, half in zip(TRAVEL, TRAVEL_LEVEL, halves):
        side = (me_ref[1] >> level) & 1
        at = 0
        count = half.shape[0]
        for w in group:
            shard_rows = shards[w].shape[0]
            for base, start, stop in spans_of(w, pl.multiple_of(side * count, count), count, shard_rows):
                copies += move.start((shards[w].at[pl.ds(base, count), :], half.at[:, at + start : at + stop]))
            at += travel_cols(w)
    wait_all(copies)


def gate_kernel(*refs):
    refs[-1][...] = jnp.zeros_like(refs[-1])


def build_masks(seg_ref, run, blocks, cont, head, tail=None, labels=None):
    seg = seg_ref[...].astype(F32)
    rows = [seg[:, b * BLOCK_TOKENS : (b + 1) * BLOCK_TOKENS] for b in range(blocks)]
    turned = jnp.concatenate(rows + [rows[0]] * (8 - blocks), axis=0).T
    per_block = PARTS // blocks
    stride = head.shape[0] // PARTS
    top = lax.broadcasted_iota(jnp.int32, (BLOCK_TOKENS, LANES), 0) == 0
    for b in range(blocks):
        col = jnp.broadcast_to(turned[:, b : b + 1], (BLOCK_TOKENS, LANES))
        if labels is not None:
            labels[b * BLOCK_TOKENS : (b + 1) * BLOCK_TOKENS, :] = col
        joined = jnp.where(top | (col == pltpu.roll(col, 1, 0)), 1.0, 0.0)
        for r in range(per_block):
            first = r * run
            part = col[first : first + run, :]
            entry = col[max(first - 1, 0) : max(first - 1, 0) + 1, :]
            last = col[first + run - 1 : first + run, :]
            at = (b * per_block + r) * stride
            cont[at : at + run, :] = joined[first : first + run, :]
            head[at : at + run, :] = jnp.where(part == entry, 1.0, 0.0)
            if tail is not None:
                tail[at : at + run, :] = jnp.where(part == last, 1.0, 0.0)


def normalise(x, gain):
    centred = x - jnp.mean(x, axis=-1, keepdims=True)
    inv = lax.rsqrt(jnp.mean(centred * centred, axis=-1, keepdims=True) + EPS)
    return centred * inv, inv, centred * inv * gain


def front_kernel(keys, run, blocks, *refs):
    n = len(keys)
    me_ref, tok_ref, seg_ref = refs[:3]
    small_refs = refs[3 : 3 + n]
    par_ref, qk_ref, end_ref, pay_ref, far_ref, nrm_ref, mix_ref, cont, head, tail, lab_ref = refs[3 + n : 14 + n]
    xs, os, sums, small = refs[14 + n :]
    me = me_ref[0]
    size_w = small.shape[0]
    zpart = Z // size_w
    for ref, ks in zip(small_refs, keys):
        for i, k in enumerate(ks):
            small[me ^ k] = ref[i].astype(F32)
    par_ref[...] = jnp.concatenate([small[w] for w in range(size_w)], axis=1)
    qk_ref[0:3, :] = jnp.concatenate(
        [small[w, 3 * NDIM + 3 : 3 * NDIM + 6, 0:zpart] for w in range(size_w)], axis=1
    )
    qk_ref[3:8, :] = jnp.zeros((5, Z), F32)
    normed = normalise(tok_ref[...].astype(F32), par_ref[48:49, :])[2]
    nrm_ref[...] = normed
    put_runs(xs, normed, run)
    for ref in (cont, head, tail):
        ref[...] = jnp.zeros_like(ref)
    build_masks(seg_ref, run, blocks, cont, head, tail, lab_ref)
    decay, rate, width = decay_tables(par_ref)
    gain = par_ref[32:48, :] * width * par_ref[16:32, :]
    far = power_of_rate(decay, BLOCK_TOKENS)
    rate_run = power_of_rate(decay, run)
    head_end = at_step(head, run - 1)
    for g in range(GROUPS):
        rates = [spread(rate, j, g) for j in range(NDIM)]
        gains = [spread(gain, j, g) for j in range(NDIM)]
        for j in range(NDIM):
            far_ref[j * GROUPS + g : j * GROUPS + g + 1, :] = far[j : j + 1, g * LANES : (g + 1) * LANES]

        def step(t, states, g=g, rates=rates, gains=gains):
            x_t = at_step(xs, t, g)
            c_t = at_step(cont, t)
            new = [(c_t * rates[j]) * states[j] + x_t for j in range(NDIM)]
            set_step(os, t, g, tree_sum([gains[j] * new[j] for j in range(NDIM)]))
            return tuple(new)

        zero = tuple(jnp.zeros((PARTS, LANES), F32) for _ in range(NDIM))
        ends = lax.fori_loop(0, run, step, zero, unroll=4)
        for j in range(NDIM):
            end_ref[state_rows(j, g), :] = ends[j]
            sums[state_rows(j, g), :] = ends[j] + head_end * spread(rate_run, j, g) * pltpu.roll(ends[j], 1, 0)
    per_block = PARTS // blocks
    seg = seg_ref[...].astype(F32)
    for b in range(blocks):
        ends = [seg[:, b * BLOCK_TOKENS : b * BLOCK_TOKENS + 1], seg[:, (b + 1) * BLOCK_TOKENS - 1 : (b + 1) * BLOCK_TOKENS]]
        bounds = jnp.concatenate([jnp.broadcast_to(e, (1, LANES)) for e in ends] + [jnp.zeros((6, LANES), F32)], axis=0)
        mine = jnp.concatenate([sums[pl.ds((b + 1) * per_block - 1, STATES, stride=PARTS), :], bounds], axis=0)
        for c in range(pay_ref.shape[0]):
            pay_ref[c, b] = mine.astype(BF16)
    mix_ref[...] = get_runs(os, run)


def scan_kernel(blocks, me_ref, order_ref, got_ref, far_ref, table_ref, place, kept):
    def fetch(pos):
        return got_ref[pos, 0:STATES, :].astype(F32)

    scan_states(me_ref, order_ref, fetch, got_ref, far_ref, table_ref, place, kept, blocks, True)


def scan_states(me_ref, order_ref, fetch, bnd_ref, far_ref, table, place, kept, blocks, forward):
    count = place.shape[0]
    per_block = PARTS // blocks

    def note(p, carry):
        place[order_ref[p]] = p
        return carry

    lax.fori_loop(0, count, note, 0, unroll=8)
    far = far_ref[...]

    def step(i, carry):
        state, label = carry
        pos = place[i if forward else count - 1 - i]
        bnd = bnd_ref[pos, STATES : STATES + 2, :].astype(F32)
        first, last = bnd[0:1, :], bnd[1:2, :]
        state = jnp.where((first if forward else last) == label, state, 0.0)
        kept[pos] = state
        state = jnp.where(first == last, far * state, 0.0) + fetch(pos)
        return state, (last if forward else first)

    lax.fori_loop(0, count, step, (jnp.zeros((STATES, LANES), F32), jnp.full((1, LANES), -1.0, F32)), unroll=8)
    for b in range(blocks):
        state = kept[me_ref[1] * blocks + b]
        for r in range(per_block):
            table[pl.ds(b * per_block + r, STATES, stride=PARTS), :] = state


def weight_copies(move, weight, sources, place, me, target, part):
    _, cols, tall = WEIGHTS[weight]
    side = (place >> TRAVEL_LEVEL[next(i for i, g in enumerate(TRAVEL) if weight in g)]) & 1
    copies = []
    for ref, column, key, half in sources:
        tall_by = 2 if tall else 1
        base = (me ^ key) * (part * tall_by)
        if half is None:
            copies += move.start((ref, target.at[pl.ds(pl.multiple_of(base, part), part * tall_by), :]))
            continue
        count = part // 2
        base = base + (side if half == 0 else 1 - side) * count
        for s in range(tall_by):
            rows = pl.ds(pl.multiple_of(base + s * part, count), count)
            copies += move.start((ref.at[:, column + s * cols : column + (s + 1) * cols], target.at[rows, :]))
    return copies


def sources_of(weight, own, own_other, travelled, keys):
    group = next(i for i, g in enumerate(TRAVEL) if weight in g)
    column = sum(travel_cols(w) for w in TRAVEL[group] if w < weight)
    out = [(own, 0, 0, None), (own_other, 0, 1, None)]
    near, far, near_other, far_other = travelled[group]
    for i, k in enumerate(keys):
        out += [(near.at[i], column, k, 0), (far.at[i], column, k, 1)]
        out += [(near_other.at[i], column, k | 1, 0), (far_other.at[i], column, k | 1, 1)]
    return out


def shard_transpose(value, me, size_w, target):
    width = value.shape[1] // size_w
    turned = value[...].T
    for shard in range(size_w):
        p = me ^ shard
        at = ((p & 1) * (size_w // 2) + (p >> 1)) * width
        target[pl.ds(pl.multiple_of(at, width), width), :] = turned[shard * width : (shard + 1) * width, :]


def store_shares(res, size_w, keep_ref, send_ref, col, tall=False):
    half = size_w // 2
    width = res.shape[1]
    steps = 2 if tall else 1
    rows = res.shape[0] // (steps * size_w)
    for i in range(size_w):
        target = keep_ref if i < half else send_ref
        for s in range(steps):
            block = res[(steps * i + s) * rows : (steps * i + s + 1) * rows, :]
            target[i % half, :, col + s * width : col + (s + 1) * width] = block.astype(BF16)


def layer_kernel(wkeys, run, blocks, size_w, *refs):
    me_ref, table, end_ref, par_ref, qk_ref, head, lab_ref, seg_ref, _ = refs[:9]
    refs = (None,) + refs
    mix_h, nrm_h, tok_h, cot_h = refs[10:14]
    own, own_other = refs[14:19], refs[19:24]
    travelled = [refs[24 + 4 * i : 28 + 4 * i] for i in range(len(TRAVEL))]
    refs = refs[24 + 4 * len(TRAVEL) :]
    out_h, ein_ref, fgain_ref, keep, send, pre_s, act, low, mlow, gcol, dir_s, rg, ra, val, vsl, prob, q_s, k_s, ssl, sh, wp, wv, wm = refs[:23]
    (out_s, mix, nrm, tok, cot, os, wu, wd, hid, gat, two, inner, ups, turned, sems) = refs[23:]
    move = Mover(sems)
    me = me_ref[0]
    part = D // size_w
    fetched = move.start((mix_h, mix), (nrm_h, nrm), (tok_h, tok), (cot_h, cot))
    loads = []
    for w, target in enumerate((wp, wv, wm, wu, wd)):
        loads.append(
            weight_copies(move, w, sources_of(w, own[w], own_other[w], travelled, wkeys), me_ref[1], me, target, part)
        )

    decay, rate, width = decay_tables(par_ref)
    gain = par_ref[32:48, :] * width * par_ref[16:32, :]
    rate_run = power_of_rate(decay, run)
    head_end = at_step(head, run - 1)
    head_before = pltpu.roll(head_end, 1, 0)
    per_block = PARTS // blocks
    lead = lax.broadcasted_iota(jnp.int32, (PARTS, LANES), 0) % per_block == 0
    for g in range(GROUPS):
        rates = [spread(rate, j, g) for j in range(NDIM)]
        start = []
        for j in range(NDIM):
            ent = table[state_rows(j, g), :]
            inward = pltpu.roll(end_ref[state_rows(j, g), :], 1, 0) + head_before * spread(rate_run, j, g) * ent
            ent = jnp.where(lead, ent, inward)
            ein_ref[state_rows(j, g), :] = ent
            start.append(ent * spread(gain, j, g))

        def step(t, states, g=g, rates=rates):
            new = [rates[j] * states[j] for j in range(NDIM)]
            set_step(os, t, g, tree_sum(new) * at_step(head, t))
            return tuple(new)

        lax.fori_loop(0, run, step, tuple(start), unroll=4)
    wait_all(fetched)
    normed = nrm[...]
    pre = mix[...] + get_runs(os, run) + par_ref[50:51, :] * normed
    pre_s[...] = pre
    act[...] = swish_unit(pre).astype(BF16)
    low[...] = normed.astype(BF16)

    wait_all(loads[0])
    gates = dot(act[...], wp[:, 0 : D + Z])
    gat[...] = sigmoid(gates[:, 0:D])
    shared_in = gates[:, D : D + Z]
    shared = swish_unit(shared_in)
    sh[...] = shared
    ssl[...] = swish_slope(shared_in)
    q_s[...] = (shared * qk_ref[0:1, :] + qk_ref[1:2, :]).astype(BF16)
    k_s[...] = (shared * qk_ref[2:3, :]).astype(BF16)
    hid[...] = dot(act[...], wp[:, D + Z + VALUE_WIDTH :])
    wait_all(loads[1])
    v = dot(low[...], wv[...])
    s = sigmoid(v)
    val[...] = (v * s).astype(BF16)
    vsl[...] = (s * (1.0 + v * (1.0 - s))).astype(BF16)
    causal = lax.broadcasted_iota(jnp.int32, (BLOCK_TOKENS, BLOCK_TOKENS), 0) >= lax.broadcasted_iota(
        jnp.int32, (BLOCK_TOKENS, BLOCK_TOKENS), 1
    )
    seg = seg_ref[...].astype(F32)
    for b in range(blocks):
        rows = slice(b * BLOCK_TOKENS, (b + 1) * BLOCK_TOKENS)
        allowed = causal & (lab_ref[rows, :] == seg[:, rows])
        scores = jnp.where(allowed, dot_nt(q_s[rows, :], k_s[rows, :]) * SCALE, -1e30)
        exps = jnp.exp(scores - jnp.max(scores, axis=-1, keepdims=True))
        prob[rows, :] = exps / jnp.sum(exps, axis=-1, keepdims=True)
    r = dot(act[...], wp[:, D + Z : D + Z + VALUE_WIDTH])
    s = sigmoid(r)
    gate = r * s
    rg[...] = gate.astype(BF16)
    slope = s * (1.0 + r * (1.0 - s))
    att = jnp.concatenate(
        [
            dot(
                prob[b * BLOCK_TOKENS : (b + 1) * BLOCK_TOKENS, :].astype(BF16),
                val[b * BLOCK_TOKENS : (b + 1) * BLOCK_TOKENS, :],
            )
            for b in range(blocks)
        ],
        axis=0,
    )
    ra[...] = (slope * att).astype(BF16)
    mlow[...] = (gate * att).astype(BF16)
    wait_all(loads[2])
    hm = hid[...] + dot(mlow[...], wm[...])
    hid[...] = hm
    x = tok[...].astype(F32)
    residual = x + gat[...] * (swish_unit(hm) - x)
    n, inv, normed_two = normalise(residual, par_ref[49:50, :])
    two[...] = normed_two.astype(BF16)

    wait_all(loads[3])
    u = dot(two[...], wu[...])
    s = sigmoid(u)
    inner[...] = (u * s).astype(BF16)
    slope = s * (1.0 + u * (1.0 - s))
    wait_all(loads[4])
    ups[...] = (dot_nt(cot[...], wd[...]) * slope).astype(BF16)
    shard_transpose(inner, me, size_w, turned)
    store_shares(dot(turned[...], cot[...]), size_w, keep, send, 0, True)
    shard_transpose(two, me, size_w, turned.at[0:D])
    store_shares(dot(turned[0:D, :], ups[...]), size_w, keep, send, 2 * D)
    out_s[...] = (residual + dot(inner[...], wd[...])).astype(BF16)
    written = move.start((out_s, out_h))
    g_two = dot_nt(ups[...], wu[...])
    fgain_ref[...] = jnp.sum(g_two * n, axis=0, keepdims=True)
    h = g_two * par_ref[49:50, :]
    g_res = cot[...].astype(F32) + inv * (
        h - jnp.mean(h, axis=-1, keepdims=True) - n * jnp.mean(h * n, axis=-1, keepdims=True)
    )
    gate = gat[...]
    s = sigmoid(hm)
    gcol[:, 0:D] = (g_res * (hm * s - x) * gate * (1.0 - gate)).astype(BF16)
    gcol[:, D : 2 * D] = (g_res * gate * (s * (1.0 + hm * (1.0 - s)))).astype(BF16)
    dir_s[...] = g_res * (1.0 - gate)
    wait_all(written)


def back_kernel(
    blocks,
    size_w,
    me_ref,
    qk_ref,
    gcol,
    rg,
    ra,
    val,
    prob,
    k_s,
    q_s,
    sh,
    ssl,
    vsl,
    act,
    wm,
    gqk_ref,
    keep,
    send,
    gproj,
    gval,
    gatt,
    turned,
):
    me = me_ref[0]
    gp = dot_nt(gcol[:, D : 2 * D], wm[...])
    gatt[...] = (gp * rg[...].astype(F32)).astype(BF16)
    gproj[:, D + Z : D + Z + VALUE_WIDTH] = (gp * ra[...].astype(F32)).astype(BF16)
    gproj[:, 0:D] = gcol[:, 0:D]
    gproj[:, D + Z + VALUE_WIDTH :] = gcol[:, D : 2 * D]
    sums = [jnp.zeros((1, Z), F32)] * 3
    for b in range(blocks):
        rows = slice(b * BLOCK_TOKENS, (b + 1) * BLOCK_TOKENS)
        p = prob[rows, :]
        g_att = gatt[rows, :]
        g_probs = dot_nt(g_att, val[rows, :])
        g_values = dot(p.T.astype(BF16), g_att)
        gval[rows, :] = (g_values * vsl[rows, :].astype(F32)).astype(BF16)
        g_scores = p * (g_probs - jnp.sum(g_probs * p, axis=-1, keepdims=True))
        g_raw = g_scores * SCALE
        g_q = dot(g_raw.astype(BF16), k_s[rows, :])
        g_k = dot(g_raw.T.astype(BF16), q_s[rows, :])
        shared = sh[rows, :]
        for i, term in enumerate((g_q * shared, g_q, g_k * shared)):
            sums[i] = sums[i] + jnp.sum(term, axis=0, keepdims=True)
        g_shared = g_q * qk_ref[0:1, :] + g_k * qk_ref[2:3, :]
        gproj[rows, D : D + Z] = (g_shared * ssl[rows, :]).astype(BF16)
    gqk_ref[...] = jnp.concatenate(sums + [jnp.zeros((5, Z), F32)], axis=0)
    shard_transpose(act, me, size_w, turned)
    split = D + Z + D
    store_shares(dot(turned[...], gproj[:, 0:split]), size_w, keep, send, 0)
    store_shares(dot(turned[...], gproj[:, split:]), size_w, keep, send, split)


def back_rest_kernel(size_w, me_ref, mlow, gcol, low, gval, gproj, wp, wv, keep, send, gact, gnv, turned):
    me = me_ref[0]
    shard_transpose(mlow, me, size_w, turned)
    store_shares(dot(turned[...], gcol[:, D : 2 * D]), size_w, keep, send, 0, True)
    shard_transpose(low, me, size_w, turned.at[0:D])
    store_shares(dot(turned[0:D, :], gval[...]), size_w, keep, send, 2 * D)
    gact[...] = dot_nt(gproj[...], wp[...])
    gnv[...] = dot_nt(gval[...], wv[...])


def adjoint_kernel(run, blocks, gact_ref, pre_ref, nrm_ref, par_ref, cont, head, gmix_ref, gn_ref, lead_ref, pay_ref, gs_ref, gs, os, sums):
    normed = nrm_ref[...]
    g_mix = gact_ref[...] * swish_slope(pre_ref[...])
    gmix_ref[...] = g_mix
    gs_ref[...] = jnp.sum(g_mix * normed, axis=0, keepdims=True)
    put_runs(gs, g_mix, run)
    decay, rate, width = decay_tables(par_ref)
    gain = par_ref[32:48, :] * width * par_ref[16:32, :]
    rate_run = power_of_rate(decay, run)
    head_end = at_step(head, run - 1)
    zero = jnp.zeros((PARTS, LANES), F32)
    for g in range(GROUPS):
        rates = [spread(rate, j, g) for j in range(NDIM)]
        gains = [spread(gain, j, g) for j in range(NDIM)]

        def back(i, carries, g=g, rates=rates, gains=gains):
            t = run - 1 - i
            g_t = at_step(gs, t, g)
            c_t = at_step(cont, t)
            bs = [g_t + carries[j] for j in range(NDIM)]
            set_step(os, t, g, tree_sum([gains[j] * bs[j] for j in range(NDIM)]))
            return tuple((c_t * rates[j]) * bs[j] for j in range(NDIM))

        ends = lax.fori_loop(0, run, back, (zero,) * NDIM, unroll=4)
        for j in range(NDIM):
            lead_ref[state_rows(j, g), :] = ends[j]
            sums[state_rows(j, g), :] = ends[j] + head_end * spread(rate_run, j, g) * pltpu.roll(ends[j], PARTS - 1, 0)
    gn_ref[...] = get_runs(os, run) + par_ref[50:51, :] * g_mix
    per_block = PARTS // blocks
    for b in range(blocks):
        pay_ref[0, b] = sums[pl.ds(b * per_block, STATES, stride=PARTS), :].astype(BF16)


def slope_kernel(run, gmix_ref, nrm_ref, ein_ref, par_ref, cont, u_ref, v_ref, ve_ref, xs, gs):
    put_runs(xs, nrm_ref[...], run)
    put_runs(gs, gmix_ref[...], run)
    _, rate, _ = decay_tables(par_ref)
    zero = jnp.zeros((PARTS, LANES), F32)
    half = NDIM // 2
    for g in range(GROUPS):
        rates = [spread(rate, j, g) for j in range(NDIM)]
        for first in (0, half):
            picks = range(first, first + half)

            def ahead(t, carry, g=g, picks=picks, rates=rates):
                us, vs, uacc, vacc = carry
                g_t = at_step(gs, t, g)
                x_t = at_step(xs, t, g)
                c_t = at_step(cont, t)
                nu, nv, nua, nva = [], [], [], []
                for i, j in enumerate(picks):
                    r = c_t * rates[j]
                    v = r * vs[i] + c_t * us[i]
                    u = r * us[i] + x_t
                    nu.append(u)
                    nv.append(v)
                    nua.append(uacc[i] + g_t * u)
                    nva.append(vacc[i] + g_t * v)
                return tuple(nu), tuple(nv), tuple(nua), tuple(nva)

            us = tuple(ein_ref[state_rows(j, g), :] for j in picks)
            zeros = (zero,) * half
            us, vs, uacc, vacc = lax.fori_loop(0, run, ahead, (us, zeros, zeros, zeros), unroll=4)
            for i, j in enumerate(picks):
                u_ref[state_rows(j, g), :] = uacc[i]
                v_ref[state_rows(j, g), :] = vacc[i]
                ve_ref[state_rows(j, g), :] = vs[i]


def finish_kernel(run, blocks, keys, me_ref, order_ref, *refs):
    n = len(keys)
    back_refs = refs[:n]
    finish(run, blocks, keys, me_ref, order_ref, back_refs, *refs[n:])


def finish(run, blocks, keys, me_ref, order_ref, back_refs, bnd_ref, far_ref, gn_ref, gnv_ref, lead_ref, u_ref, v_ref, ve_ref, tok_ref, dir_ref, par_ref, head, tail, gs_ref, fg_ref, gqk_ref, ig_ref, small_ref, os, table, place, kept, gathered):
    for ref, ks in zip(back_refs, keys):
        for i, k in enumerate(ks):
            gathered[me_ref[1] ^ k] = ref[i].astype(F32)

    def fetch(pos):
        return gathered[pos // blocks, pos % blocks]

    scan_states(me_ref, order_ref, fetch, bnd_ref, far_ref, table, place, kept, blocks, False)
    decay, rate, width = decay_tables(par_ref)
    drive_in = par_ref[16:32, :]
    readout = par_ref[32:48, :]
    drive = width * drive_in
    gain = readout * drive
    rate_run = power_of_rate(decay, run)
    head_after = pltpu.roll(at_step(head, run - 1), PARTS - 1, 0)
    per_block = PARTS // blocks
    final = lax.broadcasted_iota(jnp.int32, (PARTS, LANES), 0) % per_block == per_block - 1
    u_rows, v_rows = [], []
    for g in range(GROUPS):
        rates = [spread(rate, j, g) for j in range(NDIM)]
        start = []
        u_list, v_list = [], []
        for j in range(NDIM):
            at = state_rows(j, g)
            que = table[at, :]
            inward = pltpu.roll(lead_ref[at, :], PARTS - 1, 0) + head_after * spread(rate_run, j, g) * que
            que = jnp.where(final, que, inward)
            start.append(que * spread(gain, j, g))
            u_list.append(jnp.sum(u_ref[at, :], axis=0, keepdims=True))
            v_list.append(jnp.sum(v_ref[at, :] + que * ve_ref[at, :], axis=0, keepdims=True))
        u_rows.append(jnp.concatenate(u_list, axis=0))
        v_rows.append(jnp.concatenate(v_list, axis=0))

        def step(i, states, g=g, rates=rates):
            t = run - 1 - i
            set_step(os, t, g, tree_sum(states) * at_step(tail, t))
            return tuple(rates[j] * states[j] for j in range(NDIM))

        lax.fori_loop(0, run, step, tuple(start), unroll=4)
    u_all = jnp.concatenate(u_rows, axis=1)
    v_all = jnp.concatenate(v_rows, axis=1)
    g_normed = gn_ref[...] + gnv_ref[...] + get_runs(os, run)
    x = tok_ref[...].astype(F32)
    centred = x - jnp.mean(x, axis=-1, keepdims=True)
    var = jnp.mean(centred * centred, axis=-1, keepdims=True)
    inv = lax.rsqrt(var + EPS)
    n = centred * inv
    h = g_normed * par_ref[48:49, :]
    back = inv * (h - jnp.mean(h, axis=-1, keepdims=True) - n * jnp.mean(h * n, axis=-1, keepdims=True))
    ig_ref[...] = (dir_ref[...] + back).astype(BF16)
    size_w = 2 * small_ref.shape[1]
    half = size_w // 2
    part = small_ref.shape[3]
    zpart = Z // size_w
    me = me_ref[0]
    grads = jnp.concatenate(
        [
            readout * drive * v_all * rate * (1.0 - rate)
            - readout * u_all * drive_in * rate * rate * (1.0 - rate) / width,
            readout * u_all * width,
            drive * u_all,
            jnp.sum(g_normed * n, axis=0, keepdims=True),
            fg_ref[...],
            gs_ref[...],
            jnp.zeros((5, D), F32),
        ],
        axis=0,
    )
    for w in range(size_w):
        p = me ^ w
        qk = gqk_ref[0:8, w * zpart : (w + 1) * zpart]
        if zpart < part:
            qk = jnp.concatenate([qk, jnp.zeros((8, part - zpart), F32)], axis=1)
        both = jnp.concatenate([grads[:, w * part : (w + 1) * part], qk], axis=0)
        small_ref[p & 1, p >> 1] = both.astype(BF16)


def swap(value, axis, bit):
    size = lax.axis_size(axis)
    return lax.ppermute(value, axis, [(i, i ^ bit) for i in range(size)])


def bits_of(size):
    out, bit = [], 1
    while bit < size:
        out.append(bit)
        bit *= 2
    return out


def tie(*values):
    return lax.optimization_barrier(values)


class Share:
    def __init__(self, terms, count, cols):
        self.terms = terms
        self.count = count
        self.cols = cols

    def halve(self, level):
        count = self.count // 2

        def moved(first, other):
            return lambda me: first(me) + (((me >> level) & 1) ^ other) * count

        stay = Share([(a, i, moved(f, 0), c) for a, i, f, c in self.terms], count, self.cols)
        go = Share([(a, i, moved(f, 1), c) for a, i, f, c in self.terms], count, self.cols)
        return stay, go

    def plus(self, array, lead=(), col=0):
        return Share(self.terms + [(array, lead, lambda me: 0, col)], self.count, self.cols)


def plain_sum(share, me):
    total = None
    for array, lead, first, col in share.terms:
        for i in lead:
            array = array[i]
        array = lax.dynamic_slice_in_dim(array, first(me), share.count, 0)[:, :, col : col + share.cols].astype(F32)
        total = array if total is None else total + array
    return total.astype(BF16)


def sum_kernel(plan, n, *refs):
    me = refs[0][1]
    arrays = refs[1 : 1 + n]
    outs = refs[1 + n :]
    for out, stacked in zip(outs, plan):
        for i, row in enumerate(stacked):
            column = 0
            for terms, count, cols in row:
                total = None
                for k, lead, first, col in terms:
                    value = arrays[k][(*lead, pl.ds(first(me), count), slice(None), slice(col, col + cols))].astype(F32)
                    total = value if total is None else total + value
                out[i, :, :, column : column + cols] = total.astype(BF16)
                column += cols


def sums(where, *outputs):
    first = outputs[0][0][0]
    rows = first.terms[0][0].shape[-2]
    if rows % 8:
        return [
            jnp.stack([jnp.concatenate([plain_sum(share, where[1]) for share in row], axis=2) for row in stacked])
            for stacked in outputs
        ]
    arrays, plan, shapes = [], [], []
    for stacked in outputs:
        rows_plan = []
        for row in stacked:
            row_plan = []
            for share in row:
                terms = []
                for array, lead, start, col in share.terms:
                    k = next((k for k, a in enumerate(arrays) if a is array), None)
                    if k is None:
                        k = len(arrays)
                        arrays.append(array)
                    terms.append((k, lead, start, col))
                row_plan.append((terms, share.count, share.cols))
            rows_plan.append(row_plan)
        plan.append(rows_plan)
        shapes.append(pltpu.VMEM((len(stacked), stacked[0][0].count, rows, sum(s.cols for s in stacked[0])), BF16))
    return pl.pallas_call(
        functools.partial(sum_kernel, plan, len(arrays)),
        out_shape=tuple(shapes),
        in_specs=[SM] + [VM] * len(arrays),
        out_specs=(VM,) * len(shapes),
        cost_estimate=cost(1),
        compiler_params=room(12),
        name="sums",
    )(where, *[resident(array) for array in arrays])


def far_keys(size):
    keys = []
    for bit in reversed(bits_of(size)[1:]):
        keys += [k | bit for k in [0] + keys]
    return keys


def position(place, order):
    out = 0
    for i, level in enumerate(order):
        out = out | (((place >> level) & 1) << (len(order) - 1 - i))
    return out


def place_kernel(keys, order, spans, *refs):
    n = len(keys)
    me = refs[0][1]
    pieces = refs[1 : 1 + n]
    outs = refs[1 + n :]
    for ref, ks in zip(pieces, keys):
        rows = ref.shape[1]
        for i, k in enumerate(ks):
            base = position(me ^ k, order) * rows
            for out, (start, tall) in zip(outs, spans):
                width = out.shape[1]
                for s in range(2 if tall else 1):
                    at = pl.ds(pl.multiple_of(base + s * (out.shape[0] // 2), rows), rows)
                    out[at, :] = ref[i, :, start + s * width : start + (s + 1) * width].astype(F32)


def place(levels, keys, order, where, spans, shapes, name):
    rows = levels[0].shape[1]
    if rows % 8:
        return place_by_gather(levels, keys, order, where, spans, shapes)
    return pl.pallas_call(
        functools.partial(place_kernel, keys, order, spans),
        out_shape=tuple(shaped(s) for s in shapes),
        in_specs=[SM] + [VM] * len(levels),
        cost_estimate=cost(2.5),
        compiler_params=room(16),
        name=name,
    )(where, *[resident(level) for level in levels])


def place_by_gather(levels, keys, order, where, spans, shapes):
    flat = [k for level in keys for k in level]
    index = jnp.array([flat.index(k) for k in range(len(flat))], jnp.int32)
    holder = {position(device, order): device for device in range(len(flat))}
    picks = index[where[1] ^ jnp.array([holder[i] for i in range(len(flat))], jnp.int32)]
    block = jnp.concatenate(levels, axis=0)[picks].astype(F32)
    block = block.reshape(-1, block.shape[-1])
    outs = []
    for (start, tall), (rows, width) in zip(spans, shapes):
        columns = [block[:, start + s * width : start + (s + 1) * width] for s in range(2 if tall else 1)]
        outs.append(jnp.concatenate(columns, axis=0))
    return tuple(outs)


def body(
    tokens,
    segments,
    deal_order,
    cotangent,
    proj_weight,
    value_weight,
    merge_weight,
    ffn_up,
    ffn_down,
    norm_gain,
    ffn_gain,
    skip_gain,
    ema_decay,
    ema_input,
    ema_output,
    query_key,
):
    size_w, size_c = lax.axis_size("wsh"), lax.axis_size("ctx")
    me_w, me_c = lax.axis_index("wsh"), lax.axis_index("ctx")
    where = jnp.stack([me_w, me_c]).astype(jnp.int32)
    wbits, cbits = bits_of(size_w), bits_of(size_c)
    part = D // size_w
    zpart = Z // size_w
    half = size_w // 2
    rc = tokens.shape[1]
    blocks = rc // BLOCK_TOKENS
    run = rc // PARTS
    count = deal_order.shape[0]
    shards = (proj_weight, value_weight, merge_weight, ffn_up, ffn_down)
    group_cols = [sum(travel_cols(w) for w in group) for group in TRAVEL]

    small = pl.pallas_call(small_kernel, out_shape=shaped((SMALL_ROWS, part), BF16), cost_estimate=cost(1), compiler_params=room(60), name="small")(
        ema_decay.T,
        ema_input.T,
        ema_output.T,
        norm_gain[None],
        ffn_gain[None],
        skip_gain[None],
        query_key.T,
    )
    travel = pl.pallas_call(
        pack_kernel,
        out_shape=tuple(shaped((part // 2, c), BF16) for c in group_cols),
        in_specs=[SM] + [HBM] * 5,
        scratch_shapes=[pltpu.SemaphoreType.DMA((16,))],
        cost_estimate=cost(3),
        compiler_params=room(8),
        name="pack",
    )(where, *shards)

    def far_pieces(block):
        have = []
        for bit in reversed(wbits[1:]):
            sent = jnp.concatenate([block[None]] + have, axis=0) if have else block[None]
            have.append(swap(sent, "wsh", bit))
        return have[0] if len(have) == 1 else jnp.concatenate(have, axis=0)

    wkeys = far_keys(size_w)
    small_near = swap(small[None], "wsh", 1)
    small_far = far_pieces(small)
    near = [far_pieces(travel[0])]
    small_far, second = tie(small_far, travel[1])
    near.append(far_pieces(second))
    small_last = swap(small_far, "wsh", 1)
    skeys = [[0], [1], wkeys, [k | 1 for k in wkeys]]

    pad_run = run + 1
    runs_scratch = pltpu.VMEM((GROUPS, PARTS * pad_run, LANES), F32)
    mask_shape = shaped((PARTS * pad_run, LANES))
    kept_scratch = pltpu.VMEM((count, STATES, LANES), F32)
    table_scratch = pltpu.VMEM((STATES * PARTS, LANES), F32)
    table = shaped((STATES * PARTS, LANES))
    par, qk, ends, payload, far, normed, mix_local, cont, head, tail, label_cols = pl.pallas_call(
        functools.partial(front_kernel, skeys, run, blocks),
        out_shape=(
            shaped((SMALL_ROWS, D)),
            shaped((8, Z)),
            table,
            shaped((size_c, blocks, STATES + 8, LANES), BF16),
            shaped((STATES, LANES)),
            shaped((rc, D)),
            shaped((rc, D)),
            mask_shape,
            mask_shape,
            mask_shape,
            shaped((rc, LANES)),
        ),
        in_specs=[SM] + [VM] * 6,
        scratch_shapes=[
            runs_scratch,
            runs_scratch,
            table_scratch,
            pltpu.VMEM((size_w, SMALL_ROWS, part), F32),
        ],
        cost_estimate=cost(FRONT),
        compiler_params=room(60),
        name="front",
    )(where, tokens[0], segments, small[None], small_near, small_far, small_last)
    got = lax.all_to_all(payload, "ctx", 0, 0, tiled=True).reshape(count, STATES + 8, LANES)

    for i in range(len(TRAVEL)):
        near[i] = tie(payload, near[i])[1]
    across = [swap(piece, "ctx", 1 << level) for piece, level in zip(near, TRAVEL_LEVEL)]
    near_other = [swap(piece, "wsh", 1) for piece in near]
    gate = pl.pallas_call(
        gate_kernel,
        out_shape=shaped((8, LANES)),
        in_specs=[ANY] * len(TRAVEL),
        cost_estimate=cost(GATE),
        compiler_params=room(1),
        name="gate",
    )(*across)
    tied = tie(payload, *shards)
    own_other = [swap(shard, "wsh", 1) for shard in tied[1:]]
    travelled = [(a, b, c, swap(b, "wsh", 1)) for a, b, c in zip(near, across, near_other)]

    entered = pl.pallas_call(
        functools.partial(scan_kernel, blocks),
        out_shape=table,
        in_specs=[SM, SM, VM, VM],
        scratch_shapes=[pltpu.SMEM((count,), jnp.int32), kept_scratch],
        cost_estimate=cost(SCAN),
        compiler_params=room(8),
        name="scan",
    )(where, deal_order, got, far)

    saved = (
        shaped((half, part, 2 * D + FF), BF16),
        shaped((half, part, 2 * D + FF), BF16),
        shaped((rc, D)),
        shaped((rc, D), BF16),
        shaped((rc, D), BF16),
        shaped((rc, VALUE_WIDTH), BF16),
        shaped((rc, 2 * D), BF16),
        shaped((rc, D)),
        shaped((rc, VALUE_WIDTH), BF16),
        shaped((rc, VALUE_WIDTH), BF16),
        shaped((rc, VALUE_WIDTH), BF16),
        shaped((rc, VALUE_WIDTH), BF16),
        shaped((rc, BLOCK_TOKENS)),
        shaped((rc, Z), BF16),
        shaped((rc, Z), BF16),
        shaped((rc, Z)),
        shaped((rc, Z)),
        shaped((D, PROJ), BF16),
        shaped((D, VALUE_WIDTH), BF16),
        shaped((VALUE_WIDTH, D), BF16),
    )

    def held(*shapes):
        return tuple(pltpu.VMEM(s.shape, s.dtype) for s in shapes)

    copies_each = 2 + 4 * len(wkeys)
    results = pl.pallas_call(
        functools.partial(layer_kernel, wkeys, run, blocks, size_w),
        out_shape=(pltpu.HBM((rc, D), BF16), table, shaped((1, D))) + held(*saved),
        in_specs=[SM] + [VM] * 8 + [HBM] * (4 + 10 + 4 * len(TRAVEL)),
        out_specs=(HBM, VM, VM) + (VM,) * len(saved),
        scratch_shapes=[
            pltpu.VMEM((rc, D), BF16),
            pltpu.VMEM((rc, D), F32),
            pltpu.VMEM((rc, D), F32),
            pltpu.VMEM((rc, D), BF16),
            pltpu.VMEM((rc, D), BF16),
            runs_scratch,
            pltpu.VMEM((D, FF), BF16),
            pltpu.VMEM((FF, D), BF16),
            pltpu.VMEM((rc, D), F32),
            pltpu.VMEM((rc, D), F32),
            pltpu.VMEM((rc, D), BF16),
            pltpu.VMEM((rc, FF), BF16),
            pltpu.VMEM((rc, FF), BF16),
            pltpu.VMEM((FF, rc), BF16),
            pltpu.SemaphoreType.DMA((5 + 7 * copies_each,)),
        ],
        cost_estimate=cost(17),
        compiler_params=room(32),
        name="layer",
    )(
        where,
        entered,
        ends,
        par,
        qk,
        head,
        label_cols,
        segments,
        gate,
        *map(in_hbm, (mix_local, normed, tokens[0], cotangent[0], *shards, *own_other)),
        *[in_hbm(piece) for group in travelled for piece in group],
    )
    output, ein, grad_ffn_gain = results[:3]
    (
        ffn_keep,
        ffn_send,
        pre_active,
        active_low,
        normed_low,
        merged_low,
        gcols,
        direct,
        reset_gate,
        reset_slope,
        values,
        value_slope,
        probs,
        queries,
        keys_low,
        shared_slope,
        shared,
        proj_full,
        value_full,
        merge_full,
    ) = results[3:]

    def shares_of(keep, got):
        cut = (half, size_c, keep.shape[1] // size_c, keep.shape[2])
        keep, got = keep.reshape(cut), got.reshape(cut)
        return [
            Share([(keep, (i,), lambda me: 0, 0), (got, (i,), lambda me: 0, 0)], size_c, cut[3]) for i in range(half)
        ]

    def plus_all(shares, got):
        return [share.plus(got, (i,)) for i, share in enumerate(shares)]

    def rows_of(shares):
        return [[share] for share in shares]

    def widen(levels, keys, bit):
        block = levels[0] if len(levels) == 1 else jnp.concatenate(levels, axis=0)
        return levels + [swap(block, "ctx", bit)], keys + [[k | bit for level in keys for k in level]]

    f_got = swap(ffn_send, "wsh", 1)
    gproj_shape, gval_shape = shaped((rc, PROJ), BF16), shaped((rc, VALUE_WIDTH), BF16)
    p_shape = shaped((half, part, PROJ), BF16)
    grad_qk, p_keep, p_send, gproj, gval = pl.pallas_call(
        functools.partial(back_kernel, blocks, size_w),
        out_shape=(shaped((8, Z)),) + held(p_shape, p_shape, gproj_shape, gval_shape),
        in_specs=[SM] + [VM] * 13,
        scratch_shapes=held(gval_shape, shaped((D, rc), BF16)),
        cost_estimate=cost(9),
        compiler_params=room(20),
        name="back",
    )(
        where,
        qk,
        *map(
            resident,
            (
                gcols,
                reset_gate,
                reset_slope,
                values,
                probs,
                keys_low,
                queries,
                shared,
                shared_slope,
                value_slope,
                active_low,
                merge_full,
            ),
        ),
    )
    p_got = swap(p_send, "wsh", 1)
    gproj = tie(p_send, gproj)[1]
    q_shape = shaped((half, part, 2 * D + VALUE_WIDTH), BF16)
    q_keep, q_send, grad_active, grad_normed_value = pl.pallas_call(
        functools.partial(back_rest_kernel, size_w),
        out_shape=held(q_shape, q_shape, shaped((rc, D)), shaped((rc, D))),
        in_specs=[SM] + [VM] * 7,
        scratch_shapes=[pltpu.VMEM((VALUE_WIDTH, rc), BF16)],
        cost_estimate=cost(7),
        compiler_params=room(20),
        name="back_rest",
    )(where, *map(resident, (merged_low, gcols, normed_low, gval, gproj, proj_full, value_full)))

    top = len(cbits)
    pq_rounds = [(("w", k), ("c", 0) if k == 0 else ("w", k - 1)) for k in range(len(wbits) - 1)]
    pq_rounds.append((("c", 0), ("w", len(wbits) - 2)))
    r_order = [0] + list(range(1, top))
    f_steps = [("c", 1)] + [("w", k) for k in range(len(wbits) - 1)]
    f_steps += [("c", k) for k in range(2, top)] + [("c", 0)]
    f_order = list(range(1, top)) + [0]

    def cut(shares, step):
        kind, k = step
        if kind == "w":
            return shares[0::2], rows_of(shares[1::2])
        both = [share.halve(k) for share in shares]
        return [stay for stay, _ in both], rows_of([away for _, away in both])

    def send(value, step):
        kind, k = step
        return swap(value, "wsh", wbits[k + 1]) if kind == "w" else swap(value, "ctx", cbits[k])

    p_shares, f_shares = shares_of(p_keep, p_got), shares_of(ffn_keep, f_got)
    p_shares, p_rows = cut(p_shares, pq_rounds[0][0])
    f_shares, f_rows = cut(f_shares, f_steps[0])
    p_go, f_go = sums(where, p_rows, f_rows)
    p_go, f_go, q_send = tie(p_go, f_go, q_send)
    q_got = swap(q_send, "wsh", 1)
    p_got, f_got = send(p_go, pq_rounds[0][0]), send(f_go, f_steps[0])
    q_shares, q_rows = cut(shares_of(q_keep, q_got), pq_rounds[0][1])
    (q_go,) = sums(where, q_rows)
    q_go, grad_active = tie(q_go, grad_active)
    q_got = send(q_go, pq_rounds[0][1])
    g_mix, gn_local, leads, payload_back, grad_skip = pl.pallas_call(
        functools.partial(adjoint_kernel, run, blocks),
        out_shape=(
            shaped((rc, D)),
            shaped((rc, D)),
            table,
            shaped((1, blocks, STATES, LANES), BF16),
            shaped((1, D)),
        ),
        scratch_shapes=[runs_scratch] * 2 + [table_scratch],
        cost_estimate=cost(ADJOINT),
        compiler_params=room(20),
        name="adjoint",
    )(grad_active, pre_active, normed, par, cont, head)
    b_levels, b_keys = [payload_back], [[0]]
    for bit in reversed(cbits[3:]):
        b_levels, b_keys = widen(b_levels, b_keys, bit)
    block = b_levels[0] if len(b_levels) == 1 else jnp.concatenate(b_levels, axis=0)
    flat = [k for level in b_keys for k in level]
    for bit in (cbits[2], cbits[1], cbits[1] | cbits[2]):
        b_levels.append(swap(block, "ctx", bit))
        b_keys.append([k | bit for k in flat])
    u_part, v_part, v_end = pl.pallas_call(
        functools.partial(slope_kernel, run),
        out_shape=(table, table, table),
        scratch_shapes=[runs_scratch] * 2,
        cost_estimate=cost(SLOPE),
        compiler_params=room(16),
        name="slope",
    )(g_mix, normed, ein, par, cont)

    p_got, q_got, f_got, u_part, *b_levels = tie(p_got, q_got, f_got, u_part, *b_levels)
    p_shares, q_shares, f_shares = plus_all(p_shares, p_got), plus_all(q_shares, q_got), plus_all(f_shares, f_got)
    for number in range(1, len(pq_rounds)):
        p_step, q_step = pq_rounds[number]
        p_shares, p_rows = cut(p_shares, p_step)
        q_shares, q_rows = cut(q_shares, q_step)
        f_shares, f_rows = cut(f_shares, f_steps[number])
        p_go, q_go, f_go = sums(where, p_rows, q_rows, f_rows)
        p_go, q_go, f_go, b_levels[-1] = tie(p_go, q_go, f_go, b_levels[-1])
        p_got, q_got, f_got = send(p_go, p_step), send(q_go, q_step), send(f_go, f_steps[number])
        if number == 1:
            b_levels, b_keys = widen(b_levels, b_keys, 1)
        p_got, q_got, f_got, b_levels[-1] = tie(p_got, q_got, f_got, b_levels[-1])
        p_shares, q_shares, f_shares = plus_all(p_shares, p_got), plus_all(q_shares, q_got), plus_all(f_shares, f_got)
    (p_share,), (q_share,) = p_shares, q_shares

    def finished():
        input_grad, small_share = pl.pallas_call(
            functools.partial(finish_kernel, run, blocks, b_keys),
            out_shape=(shaped((rc, D), BF16), shaped((2, half, SMALL_ROWS + 8, part), BF16)),
            in_specs=[SM, SM] + [VM] * (16 + len(b_keys)),
            scratch_shapes=[
                runs_scratch,
                table_scratch,
                pltpu.SMEM((count,), jnp.int32),
                kept_scratch,
                pltpu.VMEM((size_c, blocks, STATES, LANES), F32),
            ],
            cost_estimate=cost(FINISH),
            compiler_params=room(20),
            name="finish",
        )(
            where,
            deal_order,
            *b_levels,
            got,
            far,
            gn_local,
            grad_normed_value,
            leads,
            u_part,
            v_part,
            v_end,
            tokens[0],
            direct,
            par,
            head,
            tail,
            grad_skip,
            grad_ffn_gain,
            grad_qk,
        )
        return input_grad, small_share

    late = None
    for k in range(1, top):
        f_step = f_steps[len(pq_rounds) + k - 1]
        p_share, p_away = p_share.halve(k)
        q_share, q_away = q_share.halve(k)
        f_shares, f_rows = cut(f_shares, f_step)
        r_go, f_go = sums(where, [[p_away, q_away]], f_rows)
        if k == 1:
            r_go, f_go, b_levels[-1] = tie(r_go, f_go, b_levels[-1])
        else:
            r_go, f_go, late = tie(r_go, f_go, late)
        r_got, f_got = swap(r_go, "ctx", cbits[k]), send(f_go, f_step)
        if k == 1:
            input_grad, late = finished()
            r_got, f_got, late = tie(r_got, f_got, late)
            late = late[0].astype(F32) + swap(late[1], "wsh", 1).astype(F32)
        elif k == 2:
            for wbit in wbits[1:]:
                late = late[0::2] + swap(late[1::2].astype(BF16), "wsh", wbit).astype(F32)
            r_got, f_got, late = tie(r_got, f_got, late)
        p_share, q_share = p_share.plus(r_got, (0,)), q_share.plus(r_got, (0,), PROJ)
        f_shares = plus_all(f_shares, f_got)
    r_own, f_own = sums(where, [[p_share, q_share]], rows_of(f_shares))
    r_own, f_own, late = tie(r_own, f_own, late)
    r_levels, r_keys, f_levels, f_keys = [r_own[0]], [[0]], [f_own[0]], [[0]]
    s_steps = list(range(top))
    s_pieces = late

    def small_step(pieces, level):
        low = pieces.astype(BF16)
        return low.astype(F32) + swap(low, "ctx", cbits[level]).astype(F32)

    for number, (r_bit, f_bit) in enumerate(zip(reversed(cbits), [1] + cbits[:0:-1])):
        r_levels, r_keys = widen(r_levels, r_keys, r_bit)
        f_levels, f_keys = widen(f_levels, f_keys, f_bit)
        todo = len(s_steps) // (top - number)
        for step in s_steps[:todo]:
            s_pieces = small_step(s_pieces, step)
        s_steps = s_steps[todo:]
        if r_bit > 1:
            r_last, f_last, s_pieces = tie(r_levels[-1], f_levels[-1], s_pieces)
            r_levels, f_levels = r_levels[:-1] + [r_last], f_levels[:-1] + [f_last]
    small_total = s_pieces[0]
    depth = merge_weight.shape[0]
    grad_down, grad_up = place(
        f_levels, f_keys, f_order, where, ((0, True), (2 * D, False)), ((depth, D), (part, FF)), "place_ffn"
    )
    grad_proj, grad_merge, grad_value = place(
        r_levels,
        r_keys,
        r_order,
        where,
        ((0, False), (PROJ, True), (PROJ + 2 * D, False)),
        ((part, PROJ), (depth, D), (part, VALUE_WIDTH)),
        "place_rest",
    )
    return (
        output[None],
        input_grad[None],
        grad_proj,
        grad_value,
        grad_merge,
        grad_up,
        grad_down,
        small_total[48],
        small_total[49],
        small_total[50],
        small_total[0:16].T,
        small_total[16:32].T,
        small_total[32:48].T,
        small_total[56:59, :zpart].T,
    )


def solution(mesh):
    rows, flat = P("wsh", None), P("wsh")
    sequence = P("wsh", "ctx", None)
    placed = (sequence, P("wsh", "ctx"), P(), sequence) + (rows,) * 5 + (flat,) * 3 + (rows,) * 4
    return jax.shard_map(
        body,
        mesh=mesh,
        in_specs=placed,
        out_specs=(sequence, sequence) + (rows,) * 5 + (flat,) * 3 + (rows,) * 4,
        check_vma=False,
    )
```

```python
import functools

import jax
import jax.numpy as jnp
from jax import lax
from jax.experimental import pallas as pl
from jax.experimental.pallas import tpu as pltpu
from jax.sharding import PartitionSpec as P

D = 512
Z = 128
VALUE_WIDTH = 1024
NDIM = 16
BLOCK_TOKENS = 128
FF = 1024
PROJ = 2 * D + Z + VALUE_WIDTH
LANES = 128
GROUPS = D // LANES
STATES = NDIM * GROUPS
PARTS = 8
F32 = jnp.float32
BF16 = jnp.bfloat16
EPS = 1e-05
PACE = 1.0
FRONT = 3
GATE = 4
SCAN = 12
SLOPE = 3.0
ADJOINT = 2.0
FINISH = 1.0
SMALL_ROWS = 56
SCALE = Z ** (-0.5)
VM = pl.BlockSpec(memory_space=pltpu.VMEM)
SM = pl.BlockSpec(memory_space=pltpu.SMEM)
HBM = pl.BlockSpec(memory_space=pltpu.HBM)
ANY = pl.BlockSpec(memory_space=pl.ANY)


sigmoid = jax.nn.sigmoid


def swish_unit(v):
    return v * sigmoid(v)


def swish_slope(v):
    s = sigmoid(v)
    return s * (1.0 + v * (1.0 - s))


def cost(us):
    return pl.CostEstimate(flops=int(us * PACE * 1e9), bytes_accessed=int(us * PACE * 3e6), transcendentals=0)


def room(mib):
    return pltpu.CompilerParams(vmem_limit_bytes=mib * 1024 * 1024)


def in_hbm(array):
    return pltpu.with_memory_space_constraint(array, pltpu.HBM)


def resident(array):
    return pltpu.with_memory_space_constraint(array, pltpu.VMEM)


def shaped(shape, dtype=F32):
    return jax.ShapeDtypeStruct(shape, dtype)


def dot(a, b):
    return jnp.dot(a, b, preferred_element_type=F32)


def dot_nt(a, b):
    return lax.dot_general(a, b, (((1,), (1,)), ((), ())), preferred_element_type=F32)


def tree_sum(terms):
    terms = list(terms)
    while len(terms) > 1:
        terms = [terms[i] + terms[i + 1] if i + 1 < len(terms) else terms[i] for i in range(0, len(terms), 2)]
    return terms[0]


def decay_tables(par_ref):
    decay = par_ref[0:NDIM, :]
    rate = sigmoid(decay)
    width = jnp.sqrt(sigmoid(-decay) * (1.0 + rate))
    return decay, rate, width


def power_of_rate(decay, count):
    return jnp.exp(-count * jnp.log1p(jnp.exp(-decay)))


def spread(table, j, g):
    return jnp.broadcast_to(table[j : j + 1, g * LANES : (g + 1) * LANES], (PARTS, LANES))


def state_rows(j, g):
    return pl.ds((j * GROUPS + g) * PARTS, PARTS)


def put_runs(ref, value, run):
    stride = ref.shape[-2] // PARTS
    if len(ref.shape) == 2:
        for h in range(PARTS):
            ref[h * stride : h * stride + run, :] = value[h * run : (h + 1) * run, :]
    else:
        for g in range(GROUPS):
            for h in range(PARTS):
                ref[g, h * stride : h * stride + run, :] = value[
                    h * run : (h + 1) * run, g * LANES : (g + 1) * LANES
                ]


def get_runs(ref, run):
    stride = ref.shape[-2] // PARTS
    return jnp.concatenate(
        [
            jnp.concatenate([ref[g, h * stride : h * stride + run, :] for h in range(PARTS)], axis=0)
            for g in range(GROUPS)
        ],
        axis=1,
    )


def at_step(ref, t, g=None):
    stride = ref.shape[-2] // PARTS
    if g is None:
        return ref[pl.ds(t, PARTS, stride=stride), :]
    return ref[g, pl.ds(t, PARTS, stride=stride), :]


def set_step(ref, t, g, value):
    stride = ref.shape[-2] // PARTS
    ref[g, pl.ds(t, PARTS, stride=stride), :] = value


def column(ref, i):
    return jnp.broadcast_to(ref[:, i : i + 1], (ref.shape[0], LANES))


class Mover:
    def __init__(self, sems):
        self.sems = sems
        self.used = 0

    def start(self, *pairs):
        copies = []
        for src, dst in pairs:
            copies.append(pltpu.make_async_copy(src, dst, self.sems.at[self.used]))
            self.used += 1
        for copy in copies:
            copy.start()
        return copies


def wait_all(copies):
    for copy in copies:
        copy.wait()


WEIGHTS = (("proj", PROJ, False), ("value", VALUE_WIDTH, False), ("merge", D, True), ("up", FF, False), ("down", D, True))
TRAVEL = ((0, 1), (2, 3, 4))
TRAVEL_LEVEL = (0, None)
WHOLE = 2


def travel_cols(i):
    return WEIGHTS[i][1] * (2 if WEIGHTS[i][2] else 1)


def spans_of(weight, base, count, shard_rows):
    _, cols, tall = WEIGHTS[weight]
    if not tall:
        return [(base, 0, cols)]
    return [(base, 0, cols), (base + shard_rows // 2, cols, 2 * cols)]


def small_kernel(dec_ref, inp_ref, rdo_ref, ng_ref, fg_ref, sg_ref, qk_ref, out_ref):
    part = out_ref.shape[1]
    rows = qk_ref.shape[1]
    out_ref[0:NDIM, :] = dec_ref[...]
    out_ref[NDIM : 2 * NDIM, :] = inp_ref[...]
    out_ref[2 * NDIM : 3 * NDIM, :] = rdo_ref[...]
    gains = jnp.concatenate([ng_ref[...], fg_ref[...], sg_ref[...]], axis=0).astype(F32)
    qk = qk_ref[...].astype(F32)
    if rows < part:
        qk = jnp.concatenate([qk, jnp.zeros((3, part - rows), F32)], axis=1)
    out_ref[3 * NDIM : SMALL_ROWS, :] = jnp.concatenate([gains, qk, jnp.zeros((2, part), F32)], axis=0).astype(BF16)


def pack_kernel(me_ref, *refs):
    shards = refs[:5]
    halves = refs[5 : 5 + len(TRAVEL)]
    move = Mover(refs[-1])
    copies = []
    for group, level, half in zip(TRAVEL, TRAVEL_LEVEL, halves):
        count = half.shape[0]
        side = 0 if level is None else (me_ref[1] >> level) & 1
        at = 0
        for w in group:
            shard_rows = shards[w].shape[0]
            for base, start, stop in spans_of(w, 0 if level is None else pl.multiple_of(side * count, count), count, shard_rows):
                copies += move.start((shards[w].at[pl.ds(base, count), :], half.at[:, at + start : at + stop]))
            at += travel_cols(w)
    wait_all(copies)


def pack_own_kernel(*refs):
    shards, out_ref = refs[:5], refs[5]
    at = 0
    for w, shard in enumerate(shards):
        rows, cols = out_ref.shape[0], shard.shape[1]
        for s in range(shard.shape[0] // rows):
            out_ref[:, at : at + cols] = shard[s * rows : (s + 1) * rows, :]
            at += cols


def gate_kernel(*refs):
    refs[-1][...] = jnp.zeros_like(refs[-1])


def build_masks(seg_ref, run, blocks, cont, head, tail=None, labels=None):
    seg = seg_ref[...].astype(F32)
    rows = [seg[:, b * BLOCK_TOKENS : (b + 1) * BLOCK_TOKENS] for b in range(blocks)]
    turned = jnp.concatenate(rows + [rows[0]] * (8 - blocks), axis=0).T
    per_block = PARTS // blocks
    stride = head.shape[0] // PARTS
    top = lax.broadcasted_iota(jnp.int32, (BLOCK_TOKENS, LANES), 0) == 0
    for b in range(blocks):
        col = jnp.broadcast_to(turned[:, b : b + 1], (BLOCK_TOKENS, LANES))
        if labels is not None:
            labels[b * BLOCK_TOKENS : (b + 1) * BLOCK_TOKENS, :] = col
        joined = jnp.where(top | (col == pltpu.roll(col, 1, 0)), 1.0, 0.0)
        for r in range(per_block):
            first = r * run
            part = col[first : first + run, :]
            entry = col[max(first - 1, 0) : max(first - 1, 0) + 1, :]
            last = col[first + run - 1 : first + run, :]
            at = (b * per_block + r) * stride
            cont[at : at + run, :] = joined[first : first + run, :]
            head[at : at + run, :] = jnp.where(part == entry, 1.0, 0.0)
            if tail is not None:
                tail[at : at + run, :] = jnp.where(part == last, 1.0, 0.0)


def normalise(x, gain):
    centred = x - jnp.mean(x, axis=-1, keepdims=True)
    inv = lax.rsqrt(jnp.mean(centred * centred, axis=-1, keepdims=True) + EPS)
    return centred * inv, inv, centred * inv * gain


def front_kernel(keys, run, blocks, *refs):
    n = len(keys)
    me_ref, tok_ref, seg_ref = refs[:3]
    small_refs = refs[3 : 3 + n]
    par_ref, qk_ref, end_ref, pay_ref, far_ref, nrm_ref, mix_ref, cont, head, tail, lab_ref = refs[3 + n : 14 + n]
    xs, os, sums, small = refs[14 + n :]
    me = me_ref[0]
    size_w = small.shape[0]
    zpart = Z // size_w
    for ref, ks in zip(small_refs, keys):
        for i, k in enumerate(ks):
            small[me ^ k] = ref[i].astype(F32)
    par_ref[...] = jnp.concatenate([small[w] for w in range(size_w)], axis=1)
    qk_ref[0:3, :] = jnp.concatenate(
        [small[w, 3 * NDIM + 3 : 3 * NDIM + 6, 0:zpart] for w in range(size_w)], axis=1
    )
    qk_ref[3:8, :] = jnp.zeros((5, Z), F32)
    normed = normalise(tok_ref[...].astype(F32), par_ref[48:49, :])[2]
    nrm_ref[...] = normed
    put_runs(xs, normed, run)
    for ref in (cont, head, tail):
        ref[...] = jnp.zeros_like(ref)
    build_masks(seg_ref, run, blocks, cont, head, tail, lab_ref)
    decay, rate, width = decay_tables(par_ref)
    gain = par_ref[32:48, :] * width * par_ref[16:32, :]
    far = power_of_rate(decay, BLOCK_TOKENS)
    rate_run = power_of_rate(decay, run)
    head_end = at_step(head, run - 1)
    for g in range(GROUPS):
        rates = [spread(rate, j, g) for j in range(NDIM)]
        gains = [spread(gain, j, g) for j in range(NDIM)]
        for j in range(NDIM):
            far_ref[j * GROUPS + g : j * GROUPS + g + 1, :] = far[j : j + 1, g * LANES : (g + 1) * LANES]

        def step(t, states, g=g, rates=rates, gains=gains):
            x_t = at_step(xs, t, g)
            c_t = at_step(cont, t)
            new = [(c_t * rates[j]) * states[j] + x_t for j in range(NDIM)]
            set_step(os, t, g, tree_sum([gains[j] * new[j] for j in range(NDIM)]))
            return tuple(new)

        zero = tuple(jnp.zeros((PARTS, LANES), F32) for _ in range(NDIM))
        ends = lax.fori_loop(0, run, step, zero, unroll=8)
        for j in range(NDIM):
            end_ref[state_rows(j, g), :] = ends[j]
            sums[state_rows(j, g), :] = ends[j] + head_end * spread(rate_run, j, g) * pltpu.roll(ends[j], 1, 0)
    per_block = PARTS // blocks
    seg = seg_ref[...].astype(F32)
    for b in range(blocks):
        ends = [seg[:, b * BLOCK_TOKENS : b * BLOCK_TOKENS + 1], seg[:, (b + 1) * BLOCK_TOKENS - 1 : (b + 1) * BLOCK_TOKENS]]
        bounds = jnp.concatenate([jnp.broadcast_to(e, (1, LANES)) for e in ends] + [jnp.zeros((6, LANES), F32)], axis=0)
        mine = jnp.concatenate([sums[pl.ds((b + 1) * per_block - 1, STATES, stride=PARTS), :], bounds], axis=0)
        for c in range(pay_ref.shape[0]):
            pay_ref[c, b] = mine.astype(BF16)
    mix_ref[...] = get_runs(os, run)


def scan_kernel(blocks, me_ref, order_ref, got_ref, far_ref, table_ref, place, kept):
    def fetch(pos):
        return got_ref[pos, 0:STATES, :].astype(F32)

    scan_states(me_ref, order_ref, fetch, got_ref, far_ref, table_ref, place, kept, blocks, True)


def scan_states(me_ref, order_ref, fetch, bnd_ref, far_ref, table, place, kept, blocks, forward):
    count = place.shape[0]
    per_block = PARTS // blocks

    def note(p, carry):
        place[order_ref[p]] = p
        return carry

    lax.fori_loop(0, count, note, 0, unroll=8)
    far = far_ref[...]

    def step(i, carry):
        state, label = carry
        pos = place[i if forward else count - 1 - i]
        bnd = bnd_ref[pos, STATES : STATES + 2, :].astype(F32)
        first, last = bnd[0:1, :], bnd[1:2, :]
        state = jnp.where((first if forward else last) == label, state, 0.0)
        kept[pos] = state
        state = jnp.where(first == last, far * state, 0.0) + fetch(pos)
        return state, (last if forward else first)

    lax.fori_loop(0, count, step, (jnp.zeros((STATES, LANES), F32), jnp.full((1, LANES), -1.0, F32)), unroll=8)
    for b in range(blocks):
        state = kept[me_ref[1] * blocks + b]
        for r in range(per_block):
            table[pl.ds(b * per_block + r, STATES, stride=PARTS), :] = state


def weight_copies(move, weight, sources, place, me, target, part):
    _, cols, tall = WEIGHTS[weight]
    level = TRAVEL_LEVEL[next(i for i, g in enumerate(TRAVEL) if weight in g)]
    side = 0 if level is None else (place >> level) & 1
    copies = []
    for ref, column, key, half in sources:
        tall_by = 2 if tall else 1
        base = (me ^ key) * (part * tall_by)
        if half is None:
            copies += move.start((ref, target.at[pl.ds(pl.multiple_of(base, part), part * tall_by), :]))
            continue
        count = part if half == WHOLE else part // 2
        base = base + (0 if half == WHOLE else side if half == 0 else 1 - side) * count
        for s in range(tall_by):
            rows = pl.ds(pl.multiple_of(base + s * part, count), count)
            copies += move.start((ref.at[:, column + s * cols : column + (s + 1) * cols], target.at[rows, :]))
    return copies


def sources_of(weight, own, own_other, travelled, keys):
    group = next(i for i, g in enumerate(TRAVEL) if weight in g)
    column = sum(travel_cols(w) for w in TRAVEL[group] if w < weight)
    out = [(own, 0, 0, None), (own_other, sum(travel_cols(w) for w in range(weight)), 1, WHOLE)]
    if TRAVEL_LEVEL[group] is None:
        near, near_other = travelled[group]
        for i, k in enumerate(keys):
            out += [(near.at[i], column, k, WHOLE), (near_other.at[i], column, k | 1, WHOLE)]
        return out
    near, far, near_other, far_other = travelled[group]
    for i, k in enumerate(keys):
        out += [(near.at[i], column, k, 0), (far.at[i], column, k, 1)]
        out += [(near_other.at[i], column, k | 1, 0), (far_other.at[i], column, k | 1, 1)]
    return out


def shard_transpose(value, me, size_w, target):
    width = value.shape[1] // size_w
    turned = value[...].T
    for shard in range(size_w):
        p = me ^ shard
        at = ((p & 1) * (size_w // 2) + (p >> 1)) * width
        target[pl.ds(pl.multiple_of(at, width), width), :] = turned[shard * width : (shard + 1) * width, :]


def store_shares(res, size_w, keep_ref, send_ref, col, tall=False):
    half = size_w // 2
    width = res.shape[1]
    steps = 2 if tall else 1
    rows = res.shape[0] // (steps * size_w)
    for i in range(size_w):
        target = keep_ref if i < half else send_ref
        for s in range(steps):
            block = res[(steps * i + s) * rows : (steps * i + s + 1) * rows, :]
            target[i % half, :, col + s * width : col + (s + 1) * width] = block.astype(BF16)


def layer_kernel(wkeys, run, blocks, size_w, *refs):
    me_ref, table, end_ref, par_ref, qk_ref, head, lab_ref, seg_ref, _ = refs[:9]
    refs = (None,) + refs
    mix, nrm, tok, cot = refs[10:14]
    own, own_other = refs[14:19], refs[19]
    travelled, at = [], 20
    for level in TRAVEL_LEVEL:
        travelled.append(refs[at : at + (2 if level is None else 4)])
        at += len(travelled[-1])
    refs = refs[at:]
    out_h, ein_ref, fgain_ref, keep, send, pre_s, act, low, mlow, gcol, dir_s, rg, ra, val, vsl, prob, q_s, k_s, ssl, sh, wp, wv, wm = refs[:23]
    (out_s, os, wu, wd, hid, gat, two, inner, ups, turned, sems) = refs[23:]
    move = Mover(sems)
    me = me_ref[0]
    part = D // size_w
    loads = []
    for w, target in enumerate((wp, wv, wm, wu, wd)):
        loads.append(
            weight_copies(move, w, sources_of(w, own[w], own_other, travelled, wkeys), me_ref[1], me, target, part)
        )

    decay, rate, width = decay_tables(par_ref)
    gain = par_ref[32:48, :] * width * par_ref[16:32, :]
    rate_run = power_of_rate(decay, run)
    head_end = at_step(head, run - 1)
    head_before = pltpu.roll(head_end, 1, 0)
    per_block = PARTS // blocks
    lead = lax.broadcasted_iota(jnp.int32, (PARTS, LANES), 0) % per_block == 0
    for g in range(GROUPS):
        rates = [spread(rate, j, g) for j in range(NDIM)]
        start = []
        for j in range(NDIM):
            ent = table[state_rows(j, g), :]
            inward = pltpu.roll(end_ref[state_rows(j, g), :], 1, 0) + head_before * spread(rate_run, j, g) * ent
            ent = jnp.where(lead, ent, inward)
            ein_ref[state_rows(j, g), :] = ent
            start.append(ent * spread(gain, j, g))

        def step(t, states, g=g, rates=rates):
            new = [rates[j] * states[j] for j in range(NDIM)]
            set_step(os, t, g, tree_sum(new) * at_step(head, t))
            return tuple(new)

        lax.fori_loop(0, run, step, tuple(start), unroll=8)
    normed = nrm[...]
    pre = mix[...] + get_runs(os, run) + par_ref[50:51, :] * normed
    pre_s[...] = pre
    act[...] = swish_unit(pre).astype(BF16)
    low[...] = normed.astype(BF16)

    wait_all(loads[0])
    gates = dot(act[...], wp[:, 0 : D + Z])
    gat[...] = sigmoid(gates[:, 0:D])
    shared_in = gates[:, D : D + Z]
    shared = swish_unit(shared_in)
    sh[...] = shared
    ssl[...] = swish_slope(shared_in)
    q_s[...] = (shared * qk_ref[0:1, :] + qk_ref[1:2, :]).astype(BF16)
    k_s[...] = (shared * qk_ref[2:3, :]).astype(BF16)
    hid[...] = dot(act[...], wp[:, D + Z + VALUE_WIDTH :])
    wait_all(loads[1])
    v = dot(low[...], wv[...])
    s = sigmoid(v)
    val[...] = (v * s).astype(BF16)
    vsl[...] = (s * (1.0 + v * (1.0 - s))).astype(BF16)
    causal = lax.broadcasted_iota(jnp.int32, (BLOCK_TOKENS, BLOCK_TOKENS), 0) >= lax.broadcasted_iota(
        jnp.int32, (BLOCK_TOKENS, BLOCK_TOKENS), 1
    )
    seg = seg_ref[...].astype(F32)
    for b in range(blocks):
        rows = slice(b * BLOCK_TOKENS, (b + 1) * BLOCK_TOKENS)
        allowed = causal & (lab_ref[rows, :] == seg[:, rows])
        scores = jnp.where(allowed, dot_nt(q_s[rows, :], k_s[rows, :]) * SCALE, -1e30)
        exps = jnp.exp(scores - jnp.max(scores, axis=-1, keepdims=True))
        prob[rows, :] = exps / jnp.sum(exps, axis=-1, keepdims=True)
    r = dot(act[...], wp[:, D + Z : D + Z + VALUE_WIDTH])
    s = sigmoid(r)
    gate = r * s
    rg[...] = gate.astype(BF16)
    slope = s * (1.0 + r * (1.0 - s))
    att = jnp.concatenate(
        [
            dot(
                prob[b * BLOCK_TOKENS : (b + 1) * BLOCK_TOKENS, :].astype(BF16),
                val[b * BLOCK_TOKENS : (b + 1) * BLOCK_TOKENS, :],
            )
            for b in range(blocks)
        ],
        axis=0,
    )
    ra[...] = (slope * att).astype(BF16)
    mlow[...] = (gate * att).astype(BF16)
    wait_all(loads[2])
    hm = hid[...] + dot(mlow[...], wm[...])
    hid[...] = hm
    x = tok[...].astype(F32)
    residual = x + gat[...] * (swish_unit(hm) - x)
    n, inv, normed_two = normalise(residual, par_ref[49:50, :])
    two[...] = normed_two.astype(BF16)

    wait_all(loads[3])
    u = dot(two[...], wu[...])
    s = sigmoid(u)
    inner[...] = (u * s).astype(BF16)
    slope = s * (1.0 + u * (1.0 - s))
    wait_all(loads[4])
    ups[...] = (dot_nt(cot[...], wd[...]) * slope).astype(BF16)
    shard_transpose(inner, me, size_w, turned)
    store_shares(dot(turned[...], cot[...]), size_w, keep, send, 0, True)
    shard_transpose(two, me, size_w, turned.at[0:D])
    store_shares(dot(turned[0:D, :], ups[...]), size_w, keep, send, 2 * D)
    out_s[...] = (residual + dot(inner[...], wd[...])).astype(BF16)
    written = move.start((out_s, out_h))
    g_two = dot_nt(ups[...], wu[...])
    fgain_ref[...] = jnp.sum(g_two * n, axis=0, keepdims=True)
    h = g_two * par_ref[49:50, :]
    g_res = cot[...].astype(F32) + inv * (
        h - jnp.mean(h, axis=-1, keepdims=True) - n * jnp.mean(h * n, axis=-1, keepdims=True)
    )
    gate = gat[...]
    s = sigmoid(hm)
    gcol[:, 0:D] = (g_res * (hm * s - x) * gate * (1.0 - gate)).astype(BF16)
    gcol[:, D : 2 * D] = (g_res * gate * (s * (1.0 + hm * (1.0 - s)))).astype(BF16)
    dir_s[...] = g_res * (1.0 - gate)
    wait_all(written)


def back_kernel(
    blocks,
    size_w,
    me_ref,
    qk_ref,
    gcol,
    rg,
    ra,
    val,
    prob,
    k_s,
    q_s,
    sh,
    ssl,
    vsl,
    act,
    wm,
    gqk_ref,
    keep,
    send,
    gproj,
    gval,
    gatt,
    turned,
):
    me = me_ref[0]
    gp = dot_nt(gcol[:, D : 2 * D], wm[...])
    gatt[...] = (gp * rg[...].astype(F32)).astype(BF16)
    gproj[:, D + Z : D + Z + VALUE_WIDTH] = (gp * ra[...].astype(F32)).astype(BF16)
    gproj[:, 0:D] = gcol[:, 0:D]
    gproj[:, D + Z + VALUE_WIDTH :] = gcol[:, D : 2 * D]
    sums = [jnp.zeros((1, Z), F32)] * 3
    for b in range(blocks):
        rows = slice(b * BLOCK_TOKENS, (b + 1) * BLOCK_TOKENS)
        p = prob[rows, :]
        g_att = gatt[rows, :]
        g_probs = dot_nt(g_att, val[rows, :])
        g_values = dot(p.T.astype(BF16), g_att)
        gval[rows, :] = (g_values * vsl[rows, :].astype(F32)).astype(BF16)
        g_scores = p * (g_probs - jnp.sum(g_probs * p, axis=-1, keepdims=True))
        g_raw = g_scores * SCALE
        g_q = dot(g_raw.astype(BF16), k_s[rows, :])
        g_k = dot(g_raw.T.astype(BF16), q_s[rows, :])
        shared = sh[rows, :]
        for i, term in enumerate((g_q * shared, g_q, g_k * shared)):
            sums[i] = sums[i] + jnp.sum(term, axis=0, keepdims=True)
        g_shared = g_q * qk_ref[0:1, :] + g_k * qk_ref[2:3, :]
        gproj[rows, D : D + Z] = (g_shared * ssl[rows, :]).astype(BF16)
    gqk_ref[...] = jnp.concatenate(sums + [jnp.zeros((5, Z), F32)], axis=0)
    shard_transpose(act, me, size_w, turned)
    split = D + Z + D
    store_shares(dot(turned[...], gproj[:, 0:split]), size_w, keep, send, 0)
    store_shares(dot(turned[...], gproj[:, split:]), size_w, keep, send, split)


def back_rest_kernel(size_w, me_ref, mlow, gcol, low, gval, gproj, wp, wv, keep, send, gact, gnv, turned):
    me = me_ref[0]
    shard_transpose(mlow, me, size_w, turned)
    store_shares(dot(turned[...], gcol[:, D : 2 * D]), size_w, keep, send, 0, True)
    shard_transpose(low, me, size_w, turned.at[0:D])
    store_shares(dot(turned[0:D, :], gval[...]), size_w, keep, send, 2 * D)
    gact[...] = dot_nt(gproj[...], wp[...])
    gnv[...] = dot_nt(gval[...], wv[...])


def adjoint_kernel(run, blocks, gact_ref, pre_ref, nrm_ref, par_ref, cont, head, gmix_ref, gn_ref, lead_ref, pay_ref, gs_ref, gs, os, sums):
    normed = nrm_ref[...]
    g_mix = gact_ref[...] * swish_slope(pre_ref[...])
    gmix_ref[...] = g_mix
    gs_ref[...] = jnp.sum(g_mix * normed, axis=0, keepdims=True)
    put_runs(gs, g_mix, run)
    decay, rate, width = decay_tables(par_ref)
    gain = par_ref[32:48, :] * width * par_ref[16:32, :]
    rate_run = power_of_rate(decay, run)
    head_end = at_step(head, run - 1)
    zero = jnp.zeros((PARTS, LANES), F32)
    for g in range(GROUPS):
        rates = [spread(rate, j, g) for j in range(NDIM)]
        gains = [spread(gain, j, g) for j in range(NDIM)]

        def back(i, carries, g=g, rates=rates, gains=gains):
            t = run - 1 - i
            g_t = at_step(gs, t, g)
            c_t = at_step(cont, t)
            bs = [g_t + carries[j] for j in range(NDIM)]
            set_step(os, t, g, tree_sum([gains[j] * bs[j] for j in range(NDIM)]))
            return tuple((c_t * rates[j]) * bs[j] for j in range(NDIM))

        ends = lax.fori_loop(0, run, back, (zero,) * NDIM, unroll=8)
        for j in range(NDIM):
            lead_ref[state_rows(j, g), :] = ends[j]
            sums[state_rows(j, g), :] = ends[j] + head_end * spread(rate_run, j, g) * pltpu.roll(ends[j], PARTS - 1, 0)
    gn_ref[...] = get_runs(os, run) + par_ref[50:51, :] * g_mix
    per_block = PARTS // blocks
    for b in range(blocks):
        pay_ref[0, b] = sums[pl.ds(b * per_block, STATES, stride=PARTS), :].astype(BF16)


def slope_kernel(run, gmix_ref, nrm_ref, ein_ref, par_ref, cont, u_ref, v_ref, ve_ref, xs, gs):
    put_runs(xs, nrm_ref[...], run)
    put_runs(gs, gmix_ref[...], run)
    _, rate, _ = decay_tables(par_ref)
    zero = jnp.zeros((PARTS, LANES), F32)
    half = NDIM // 2
    for g in range(GROUPS):
        rates = [spread(rate, j, g) for j in range(NDIM)]
        for first in (0, half):
            picks = range(first, first + half)

            def ahead(t, carry, g=g, picks=picks, rates=rates):
                us, vs, uacc, vacc = carry
                g_t = at_step(gs, t, g)
                x_t = at_step(xs, t, g)
                c_t = at_step(cont, t)
                nu, nv, nua, nva = [], [], [], []
                for i, j in enumerate(picks):
                    r = c_t * rates[j]
                    v = r * vs[i] + c_t * us[i]
                    u = r * us[i] + x_t
                    nu.append(u)
                    nv.append(v)
                    nua.append(uacc[i] + g_t * u)
                    nva.append(vacc[i] + g_t * v)
                return tuple(nu), tuple(nv), tuple(nua), tuple(nva)

            us = tuple(ein_ref[state_rows(j, g), :] for j in picks)
            zeros = (zero,) * half
            us, vs, uacc, vacc = lax.fori_loop(0, run, ahead, (us, zeros, zeros, zeros), unroll=8)
            for i, j in enumerate(picks):
                u_ref[state_rows(j, g), :] = uacc[i]
                v_ref[state_rows(j, g), :] = vacc[i]
                ve_ref[state_rows(j, g), :] = vs[i]


def finish_kernel(run, blocks, keys, me_ref, order_ref, *refs):
    n = len(keys)
    back_refs = refs[:n]
    finish(run, blocks, keys, me_ref, order_ref, back_refs, *refs[n:])


def finish(run, blocks, keys, me_ref, order_ref, back_refs, bnd_ref, far_ref, gn_ref, gnv_ref, lead_ref, u_ref, v_ref, ve_ref, tok_ref, dir_ref, par_ref, head, tail, gs_ref, fg_ref, gqk_ref, ig_ref, small_ref, os, table, place, kept, gathered):
    for ref, ks in zip(back_refs, keys):
        for i, k in enumerate(ks):
            gathered[me_ref[1] ^ k] = ref[i].astype(F32)

    def fetch(pos):
        return gathered[pos // blocks, pos % blocks]

    scan_states(me_ref, order_ref, fetch, bnd_ref, far_ref, table, place, kept, blocks, False)
    decay, rate, width = decay_tables(par_ref)
    drive_in = par_ref[16:32, :]
    readout = par_ref[32:48, :]
    drive = width * drive_in
    gain = readout * drive
    rate_run = power_of_rate(decay, run)
    head_after = pltpu.roll(at_step(head, run - 1), PARTS - 1, 0)
    per_block = PARTS // blocks
    final = lax.broadcasted_iota(jnp.int32, (PARTS, LANES), 0) % per_block == per_block - 1
    u_rows, v_rows = [], []
    for g in range(GROUPS):
        rates = [spread(rate, j, g) for j in range(NDIM)]
        start = []
        u_list, v_list = [], []
        for j in range(NDIM):
            at = state_rows(j, g)
            que = table[at, :]
            inward = pltpu.roll(lead_ref[at, :], PARTS - 1, 0) + head_after * spread(rate_run, j, g) * que
            que = jnp.where(final, que, inward)
            start.append(que * spread(gain, j, g))
            u_list.append(jnp.sum(u_ref[at, :], axis=0, keepdims=True))
            v_list.append(jnp.sum(v_ref[at, :] + que * ve_ref[at, :], axis=0, keepdims=True))
        u_rows.append(jnp.concatenate(u_list, axis=0))
        v_rows.append(jnp.concatenate(v_list, axis=0))

        def step(i, states, g=g, rates=rates):
            t = run - 1 - i
            set_step(os, t, g, tree_sum(states) * at_step(tail, t))
            return tuple(rates[j] * states[j] for j in range(NDIM))

        lax.fori_loop(0, run, step, tuple(start), unroll=8)
    u_all = jnp.concatenate(u_rows, axis=1)
    v_all = jnp.concatenate(v_rows, axis=1)
    g_normed = gn_ref[...] + gnv_ref[...] + get_runs(os, run)
    x = tok_ref[...].astype(F32)
    centred = x - jnp.mean(x, axis=-1, keepdims=True)
    var = jnp.mean(centred * centred, axis=-1, keepdims=True)
    inv = lax.rsqrt(var + EPS)
    n = centred * inv
    h = g_normed * par_ref[48:49, :]
    back = inv * (h - jnp.mean(h, axis=-1, keepdims=True) - n * jnp.mean(h * n, axis=-1, keepdims=True))
    ig_ref[...] = (dir_ref[...] + back).astype(BF16)
    size_w = 2 * small_ref.shape[1]
    half = size_w // 2
    part = small_ref.shape[3]
    zpart = Z // size_w
    me = me_ref[0]
    grads = jnp.concatenate(
        [
            readout * drive * v_all * rate * (1.0 - rate)
            - readout * u_all * drive_in * rate * rate * (1.0 - rate) / width,
            readout * u_all * width,
            drive * u_all,
            jnp.sum(g_normed * n, axis=0, keepdims=True),
            fg_ref[...],
            gs_ref[...],
            jnp.zeros((5, D), F32),
        ],
        axis=0,
    )
    for w in range(size_w):
        p = me ^ w
        qk = gqk_ref[0:8, w * zpart : (w + 1) * zpart]
        if zpart < part:
            qk = jnp.concatenate([qk, jnp.zeros((8, part - zpart), F32)], axis=1)
        both = jnp.concatenate([grads[:, w * part : (w + 1) * part], qk], axis=0)
        small_ref[p & 1, p >> 1] = both.astype(BF16)


def swap(value, axis, bit):
    size = lax.axis_size(axis)
    return lax.ppermute(value, axis, [(i, i ^ bit) for i in range(size)])


def bits_of(size):
    out, bit = [], 1
    while bit < size:
        out.append(bit)
        bit *= 2
    return out


def tie(*values):
    return lax.optimization_barrier(values)


class Share:
    def __init__(self, terms, count, cols):
        self.terms = terms
        self.count = count
        self.cols = cols

    def halve(self, level):
        count = self.count // 2

        def moved(first, other):
            return lambda me: first(me) + (((me >> level) & 1) ^ other) * count

        stay = Share([(a, i, moved(f, 0), c) for a, i, f, c in self.terms], count, self.cols)
        go = Share([(a, i, moved(f, 1), c) for a, i, f, c in self.terms], count, self.cols)
        return stay, go

    def plus(self, array, lead=(), col=0):
        return Share(self.terms + [(array, lead, lambda me: 0, col)], self.count, self.cols)


def plain_sum(share, me):
    total = None
    for array, lead, first, col in share.terms:
        for i in lead:
            array = array[i]
        array = lax.dynamic_slice_in_dim(array, first(me), share.count, 0)[:, :, col : col + share.cols].astype(F32)
        total = array if total is None else total + array
    return total.astype(BF16)


def sum_kernel(plan, n, *refs):
    me = refs[0][1]
    arrays = refs[1 : 1 + n]
    outs = refs[1 + n :]
    for out, stacked in zip(outs, plan):
        for i, row in enumerate(stacked):
            column = 0
            for terms, count, cols in row:
                total = None
                for k, lead, first, col in terms:
                    value = arrays[k][(*lead, pl.ds(first(me), count), slice(None), slice(col, col + cols))].astype(F32)
                    total = value if total is None else total + value
                out[i, :, :, column : column + cols] = total.astype(BF16)
                column += cols


def sums(where, *outputs):
    first = outputs[0][0][0]
    rows = first.terms[0][0].shape[-2]
    if rows % 8:
        return [
            jnp.stack([jnp.concatenate([plain_sum(share, where[1]) for share in row], axis=2) for row in stacked])
            for stacked in outputs
        ]
    arrays, plan, shapes = [], [], []
    for stacked in outputs:
        rows_plan = []
        for row in stacked:
            row_plan = []
            for share in row:
                terms = []
                for array, lead, start, col in share.terms:
                    k = next((k for k, a in enumerate(arrays) if a is array), None)
                    if k is None:
                        k = len(arrays)
                        arrays.append(array)
                    terms.append((k, lead, start, col))
                row_plan.append((terms, share.count, share.cols))
            rows_plan.append(row_plan)
        plan.append(rows_plan)
        shapes.append(pltpu.VMEM((len(stacked), stacked[0][0].count, rows, sum(s.cols for s in stacked[0])), BF16))
    return pl.pallas_call(
        functools.partial(sum_kernel, plan, len(arrays)),
        out_shape=tuple(shapes),
        in_specs=[SM] + [VM] * len(arrays),
        out_specs=(VM,) * len(shapes),
        cost_estimate=cost(1),
        compiler_params=room(12),
        name="sums",
    )(where, *[resident(array) for array in arrays])


def far_keys(size):
    keys = []
    for bit in reversed(bits_of(size)[1:]):
        keys += [k | bit for k in [0] + keys]
    return keys


def position(place, order):
    out = 0
    for i, level in enumerate(order):
        out = out | (((place >> level) & 1) << (len(order) - 1 - i))
    return out


def place_kernel(keys, order, spans, *refs):
    n = len(keys)
    me = refs[0][1]
    pieces = refs[1 : 1 + n]
    outs = refs[1 + n :]
    for ref, ks in zip(pieces, keys):
        rows = ref.shape[1]
        for i, k in enumerate(ks):
            base = position(me ^ k, order) * rows
            for out, (start, tall) in zip(outs, spans):
                width = out.shape[1]
                for s in range(2 if tall else 1):
                    at = pl.ds(pl.multiple_of(base + s * (out.shape[0] // 2), rows), rows)
                    out[at, :] = ref[i, :, start + s * width : start + (s + 1) * width].astype(F32)


def place(levels, keys, order, where, spans, shapes, name):
    rows = levels[0].shape[1]
    if rows % 8:
        return place_by_gather(levels, keys, order, where, spans, shapes)
    return pl.pallas_call(
        functools.partial(place_kernel, keys, order, spans),
        out_shape=tuple(shaped(s) for s in shapes),
        in_specs=[SM] + [VM] * len(levels),
        cost_estimate=cost(0.1),
        compiler_params=room(16),
        name=name,
    )(where, *[resident(level) for level in levels])


def place_part_kernel(keys, order, spans, given, *refs):
    n = len(keys)
    me = refs[0][1]
    pieces = refs[1 : 1 + n]
    outs = refs[1 + n + given : 1 + n + given + len(spans)]
    wide, sems = refs[-2:]
    move = Mover(sems)
    copies, at = [], 0
    for ref, ks in zip(pieces, keys):
        rows = ref.shape[1]
        for i, k in enumerate(ks):
            wide[at] = ref[i].astype(F32)
            base = position(me ^ k, order) * rows
            for out, (start, tall) in zip(outs, spans):
                width = out.shape[1]
                for s in range(2 if tall else 1):
                    where = pl.ds(pl.multiple_of(base + s * (out.shape[0] // 2), rows), rows)
                    source = wide.at[at, :, start + s * width : start + (s + 1) * width]
                    copies += move.start((source, out.at[where, :]))
            at += 1
    wait_all(copies)


def place_part(levels, keys, order, where, spans, shapes, given, name):
    count = sum(map(len, keys))
    rows, cols = levels[0].shape[1:]
    return pl.pallas_call(
        functools.partial(place_part_kernel, keys, order, spans, len(given)),
        out_shape=tuple(pltpu.HBM(s, F32) for s in shapes),
        in_specs=[SM] + [VM] * len(levels) + [HBM] * len(given),
        out_specs=(HBM,) * len(shapes),
        input_output_aliases={1 + len(levels) + i: i for i in range(len(given))},
        scratch_shapes=[
            pltpu.VMEM((count, rows, cols), F32),
            pltpu.SemaphoreType.DMA((count * sum(2 if tall else 1 for _, tall in spans),)),
        ],
        cost_estimate=cost(0.1 if given else 4.0),
        compiler_params=room(16),
        name=name,
    )(where, *[resident(level) for level in levels], *given)


def place_by_gather(levels, keys, order, where, spans, shapes):
    flat = [k for level in keys for k in level]
    index = jnp.array([flat.index(k) for k in range(len(flat))], jnp.int32)
    holder = {position(device, order): device for device in range(len(flat))}
    picks = index[where[1] ^ jnp.array([holder[i] for i in range(len(flat))], jnp.int32)]
    block = jnp.concatenate(levels, axis=0)[picks].astype(F32)
    block = block.reshape(-1, block.shape[-1])
    outs = []
    for (start, tall), (rows, width) in zip(spans, shapes):
        columns = [block[:, start + s * width : start + (s + 1) * width] for s in range(2 if tall else 1)]
        outs.append(jnp.concatenate(columns, axis=0))
    return tuple(outs)


def body(
    tokens,
    segments,
    deal_order,
    cotangent,
    proj_weight,
    value_weight,
    merge_weight,
    ffn_up,
    ffn_down,
    norm_gain,
    ffn_gain,
    skip_gain,
    ema_decay,
    ema_input,
    ema_output,
    query_key,
):
    size_w, size_c = lax.axis_size("wsh"), lax.axis_size("ctx")
    me_w, me_c = lax.axis_index("wsh"), lax.axis_index("ctx")
    where = jnp.stack([me_w, me_c]).astype(jnp.int32)
    wbits, cbits = bits_of(size_w), bits_of(size_c)
    part = D // size_w
    zpart = Z // size_w
    half = size_w // 2
    rc = tokens.shape[1]
    blocks = rc // BLOCK_TOKENS
    run = rc // PARTS
    count = deal_order.shape[0]
    shards = (proj_weight, value_weight, merge_weight, ffn_up, ffn_down)
    group_cols = [sum(travel_cols(w) for w in group) for group in TRAVEL]

    small = pl.pallas_call(small_kernel, out_shape=shaped((SMALL_ROWS, part), BF16), cost_estimate=cost(1), compiler_params=room(60), name="small")(
        ema_decay.T,
        ema_input.T,
        ema_output.T,
        norm_gain[None],
        ffn_gain[None],
        skip_gain[None],
        query_key.T,
    )
    travel = pl.pallas_call(
        pack_kernel,
        out_shape=tuple(
            shaped((part if level is None else part // 2, c), BF16) for c, level in zip(group_cols, TRAVEL_LEVEL)
        ),
        in_specs=[SM] + [HBM] * 5,
        scratch_shapes=[pltpu.SemaphoreType.DMA((16,))],
        cost_estimate=cost(3),
        compiler_params=room(8),
        name="pack",
    )(where, *shards)

    def far_pieces(block):
        have = []
        for bit in reversed(wbits[1:]):
            sent = jnp.concatenate([block[None]] + have, axis=0) if have else block[None]
            have.append(swap(sent, "wsh", bit))
        return have[0] if len(have) == 1 else jnp.concatenate(have, axis=0)

    wkeys = far_keys(size_w)
    small_near = swap(small[None], "wsh", 1)
    small_far = far_pieces(small)
    small_far, *travel = tie(small_far, *travel)
    near = [far_pieces(block) for block in travel]
    small_last = swap(small_far, "wsh", 1)
    skeys = [[0], [1], wkeys, [k | 1 for k in wkeys]]

    pad_run = run + 1
    runs_scratch = pltpu.VMEM((GROUPS, PARTS * pad_run, LANES), F32)
    mask_shape = shaped((PARTS * pad_run, LANES))
    kept_scratch = pltpu.VMEM((count, STATES, LANES), F32)
    table_scratch = pltpu.VMEM((STATES * PARTS, LANES), F32)
    table = shaped((STATES * PARTS, LANES))
    par, qk, ends, payload, far, normed, mix_local, cont, head, tail, label_cols = pl.pallas_call(
        functools.partial(front_kernel, skeys, run, blocks),
        out_shape=(
            shaped((SMALL_ROWS, D)),
            shaped((8, Z)),
            table,
            shaped((size_c, blocks, STATES + 8, LANES), BF16),
            shaped((STATES, LANES)),
            shaped((rc, D)),
            shaped((rc, D)),
            mask_shape,
            mask_shape,
            mask_shape,
            shaped((rc, LANES)),
        ),
        in_specs=[SM] + [VM] * 6,
        scratch_shapes=[
            runs_scratch,
            runs_scratch,
            table_scratch,
            pltpu.VMEM((size_w, SMALL_ROWS, part), F32),
        ],
        cost_estimate=cost(FRONT),
        compiler_params=room(60),
        name="front",
    )(where, tokens[0], segments, small[None], small_near, small_far, small_last)
    got = lax.all_to_all(payload, "ctx", 0, 0, tiled=True).reshape(count, STATES + 8, LANES)

    for i in range(len(TRAVEL)):
        near[i] = tie(payload, near[i])[1]
    across = [
        None if level is None else swap(piece, "ctx", 1 << level) for piece, level in zip(near, TRAVEL_LEVEL)
    ]
    for i, level in enumerate(TRAVEL_LEVEL):
        if level is None:
            _, near[i] = tie(across[0], near[i])
    near_other = [swap(piece, "wsh", 1) for piece in near]
    gate = pl.pallas_call(
        gate_kernel,
        out_shape=shaped((8, LANES)),
        in_specs=[ANY] * sum(b is not None for b in across),
        cost_estimate=cost(GATE),
        compiler_params=room(1),
        name="gate",
    )(*[b for b in across if b is not None])
    tied = tie(payload, *shards)
    packed_own = pl.pallas_call(
        pack_own_kernel,
        out_shape=shaped((part, sum(travel_cols(w) for w in range(len(WEIGHTS)))), BF16),
        cost_estimate=cost(2),
        compiler_params=room(60),
        name="pack_own",
    )(*tied[1:])
    own_other = swap(packed_own, "wsh", 1)
    travelled = [
        (a, c) if b is None else (a, b, c, swap(b, "wsh", 1)) for a, b, c in zip(near, across, near_other)
    ]

    entered = pl.pallas_call(
        functools.partial(scan_kernel, blocks),
        out_shape=table,
        in_specs=[SM, SM, VM, VM],
        scratch_shapes=[pltpu.SMEM((count,), jnp.int32), kept_scratch],
        cost_estimate=cost(SCAN),
        compiler_params=room(8),
        name="scan",
    )(where, deal_order, got, far)

    saved = (
        shaped((half, part, 2 * D + FF), BF16),
        shaped((half, part, 2 * D + FF), BF16),
        shaped((rc, D)),
        shaped((rc, D), BF16),
        shaped((rc, D), BF16),
        shaped((rc, VALUE_WIDTH), BF16),
        shaped((rc, 2 * D), BF16),
        shaped((rc, D)),
        shaped((rc, VALUE_WIDTH), BF16),
        shaped((rc, VALUE_WIDTH), BF16),
        shaped((rc, VALUE_WIDTH), BF16),
        shaped((rc, VALUE_WIDTH), BF16),
        shaped((rc, BLOCK_TOKENS)),
        shaped((rc, Z), BF16),
        shaped((rc, Z), BF16),
        shaped((rc, Z)),
        shaped((rc, Z)),
        shaped((D, PROJ), BF16),
        shaped((D, VALUE_WIDTH), BF16),
        shaped((VALUE_WIDTH, D), BF16),
    )

    def held(*shapes):
        return tuple(pltpu.VMEM(s.shape, s.dtype) for s in shapes)

    copies_each = 2 + 4 * len(wkeys)
    results = pl.pallas_call(
        functools.partial(layer_kernel, wkeys, run, blocks, size_w),
        out_shape=(pltpu.HBM((rc, D), BF16), table, shaped((1, D))) + held(*saved),
        in_specs=[SM] + [VM] * 12 + [HBM] * 5 + [ANY] * (1 + sum(map(len, travelled))),
        out_specs=(HBM, VM, VM) + (VM,) * len(saved),
        scratch_shapes=[
            pltpu.VMEM((rc, D), BF16),
            runs_scratch,
            pltpu.VMEM((D, FF), BF16),
            pltpu.VMEM((FF, D), BF16),
            pltpu.VMEM((rc, D), F32),
            pltpu.VMEM((rc, D), F32),
            pltpu.VMEM((rc, D), BF16),
            pltpu.VMEM((rc, FF), BF16),
            pltpu.VMEM((rc, FF), BF16),
            pltpu.VMEM((FF, rc), BF16),
            pltpu.SemaphoreType.DMA((1 + 7 * (copies_each + 1),)),
        ],
        cost_estimate=cost(17),
        compiler_params=room(32),
        name="layer",
    )(
        where,
        entered,
        ends,
        par,
        qk,
        head,
        label_cols,
        segments,
        gate,
        *map(resident, (mix_local, normed, tokens[0], cotangent[0])),
        *map(in_hbm, shards),
        own_other,
        *[piece for group in travelled for piece in group],
    )
    output, ein, grad_ffn_gain = results[:3]
    (
        ffn_keep,
        ffn_send,
        pre_active,
        active_low,
        normed_low,
        merged_low,
        gcols,
        direct,
        reset_gate,
        reset_slope,
        values,
        value_slope,
        probs,
        queries,
        keys_low,
        shared_slope,
        shared,
        proj_full,
        value_full,
        merge_full,
    ) = results[3:]

    def shares_of(keep, got):
        cut = (half, size_c, keep.shape[1] // size_c, keep.shape[2])
        keep, got = keep.reshape(cut), got.reshape(cut)
        return [
            Share([(keep, (i,), lambda me: 0, 0), (got, (i,), lambda me: 0, 0)], size_c, cut[3]) for i in range(half)
        ]

    def plus_all(shares, got):
        return [share.plus(got, (i,)) for i, share in enumerate(shares)]

    def rows_of(shares):
        return [[share] for share in shares]

    def widen(levels, keys, bit):
        block = levels[0] if len(levels) == 1 else jnp.concatenate(levels, axis=0)
        return levels + [swap(block, "ctx", bit)], keys + [[k | bit for level in keys for k in level]]

    f_got = swap(ffn_send, "wsh", 1)
    gproj_shape, gval_shape = shaped((rc, PROJ), BF16), shaped((rc, VALUE_WIDTH), BF16)
    p_shape = shaped((half, part, PROJ), BF16)
    grad_qk, p_keep, p_send, gproj, gval = pl.pallas_call(
        functools.partial(back_kernel, blocks, size_w),
        out_shape=(shaped((8, Z)),) + held(p_shape, p_shape, gproj_shape, gval_shape),
        in_specs=[SM] + [VM] * 13,
        scratch_shapes=held(gval_shape, shaped((D, rc), BF16)),
        cost_estimate=cost(9),
        compiler_params=room(20),
        name="back",
    )(
        where,
        qk,
        *map(
            resident,
            (
                gcols,
                reset_gate,
                reset_slope,
                values,
                probs,
                keys_low,
                queries,
                shared,
                shared_slope,
                value_slope,
                active_low,
                merge_full,
            ),
        ),
    )
    p_got = swap(p_send, "wsh", 1)
    gproj = tie(p_send, gproj)[1]
    q_shape = shaped((half, part, 2 * D + VALUE_WIDTH), BF16)
    q_keep, q_send, grad_active, grad_normed_value = pl.pallas_call(
        functools.partial(back_rest_kernel, size_w),
        out_shape=held(q_shape, q_shape, shaped((rc, D)), shaped((rc, D))),
        in_specs=[SM] + [VM] * 7,
        scratch_shapes=[pltpu.VMEM((VALUE_WIDTH, rc), BF16)],
        cost_estimate=cost(7),
        compiler_params=room(20),
        name="back_rest",
    )(where, *map(resident, (merged_low, gcols, normed_low, gval, gproj, proj_full, value_full)))

    top = len(cbits)
    pq_rounds = [(("w", k), ("c", 0) if k == 0 else ("w", k - 1)) for k in range(len(wbits) - 1)]
    pq_rounds.append((("c", 0), ("w", len(wbits) - 2)))
    r_order = [0] + list(range(1, top))
    f_steps = [("c", 1)] + [("w", k) for k in range(len(wbits) - 1)]
    f_steps += [("c", k) for k in range(2, top)] + [("c", 0)]
    f_order = list(range(1, top)) + [0]

    def cut(shares, step):
        kind, k = step
        if kind == "w":
            return shares[0::2], rows_of(shares[1::2])
        both = [share.halve(k) for share in shares]
        return [stay for stay, _ in both], rows_of([away for _, away in both])

    def send(value, step):
        kind, k = step
        return swap(value, "wsh", wbits[k + 1]) if kind == "w" else swap(value, "ctx", cbits[k])

    p_shares, f_shares = shares_of(p_keep, p_got), shares_of(ffn_keep, f_got)
    p_shares, p_rows = cut(p_shares, pq_rounds[0][0])
    f_shares, f_rows = cut(f_shares, f_steps[0])
    p_go, f_go = sums(where, p_rows, f_rows)
    p_go, f_go, q_send = tie(p_go, f_go, q_send)
    q_got = swap(q_send, "wsh", 1)
    p_got, f_got = send(p_go, pq_rounds[0][0]), send(f_go, f_steps[0])
    q_shares, q_rows = cut(shares_of(q_keep, q_got), pq_rounds[0][1])
    (q_go,) = sums(where, q_rows)
    q_go, grad_active = tie(q_go, grad_active)
    q_got = send(q_go, pq_rounds[0][1])
    g_mix, gn_local, leads, payload_back, grad_skip = pl.pallas_call(
        functools.partial(adjoint_kernel, run, blocks),
        out_shape=(
            shaped((rc, D)),
            shaped((rc, D)),
            table,
            shaped((1, blocks, STATES, LANES), BF16),
            shaped((1, D)),
        ),
        scratch_shapes=[runs_scratch] * 2 + [table_scratch],
        cost_estimate=cost(ADJOINT),
        compiler_params=room(20),
        name="adjoint",
    )(grad_active, pre_active, normed, par, cont, head)
    b_levels, b_keys = [payload_back], [[0]]
    for bit in reversed(cbits[3:]):
        b_levels, b_keys = widen(b_levels, b_keys, bit)
    block = b_levels[0] if len(b_levels) == 1 else jnp.concatenate(b_levels, axis=0)
    flat = [k for level in b_keys for k in level]
    for bit in (cbits[2], cbits[1], cbits[1] | cbits[2]):
        b_levels.append(swap(block, "ctx", bit))
        b_keys.append([k | bit for k in flat])
    u_part, v_part, v_end = pl.pallas_call(
        functools.partial(slope_kernel, run),
        out_shape=(table, table, table),
        scratch_shapes=[runs_scratch] * 2,
        cost_estimate=cost(SLOPE),
        compiler_params=room(16),
        name="slope",
    )(g_mix, normed, ein, par, cont)

    p_got, q_got, f_got, u_part, *b_levels = tie(p_got, q_got, f_got, u_part, *b_levels)
    p_shares, q_shares, f_shares = plus_all(p_shares, p_got), plus_all(q_shares, q_got), plus_all(f_shares, f_got)
    for number in range(1, len(pq_rounds)):
        p_step, q_step = pq_rounds[number]
        p_shares, p_rows = cut(p_shares, p_step)
        q_shares, q_rows = cut(q_shares, q_step)
        f_shares, f_rows = cut(f_shares, f_steps[number])
        p_go, q_go, f_go = sums(where, p_rows, q_rows, f_rows)
        p_go, q_go, f_go, b_levels[-1] = tie(p_go, q_go, f_go, b_levels[-1])
        p_got, q_got, f_got = send(p_go, p_step), send(q_go, q_step), send(f_go, f_steps[number])
        if number == 1:
            b_levels, b_keys = widen(b_levels, b_keys, 1)
        p_got, q_got, f_got, b_levels[-1] = tie(p_got, q_got, f_got, b_levels[-1])
        p_shares, q_shares, f_shares = plus_all(p_shares, p_got), plus_all(q_shares, q_got), plus_all(f_shares, f_got)
    (p_share,), (q_share,) = p_shares, q_shares

    def finished():
        input_grad, small_share = pl.pallas_call(
            functools.partial(finish_kernel, run, blocks, b_keys),
            out_shape=(shaped((rc, D), BF16), shaped((2, half, SMALL_ROWS + 8, part), BF16)),
            in_specs=[SM, SM] + [VM] * (16 + len(b_keys)),
            scratch_shapes=[
                runs_scratch,
                table_scratch,
                pltpu.SMEM((count,), jnp.int32),
                kept_scratch,
                pltpu.VMEM((size_c, blocks, STATES, LANES), F32),
            ],
            cost_estimate=cost(FINISH),
            compiler_params=room(20),
            name="finish",
        )(
            where,
            deal_order,
            *b_levels,
            got,
            far,
            gn_local,
            grad_normed_value,
            leads,
            u_part,
            v_part,
            v_end,
            tokens[0],
            direct,
            par,
            head,
            tail,
            grad_skip,
            grad_ffn_gain,
            grad_qk,
        )
        return input_grad, small_share

    late = None
    for k in range(1, top):
        f_step = f_steps[len(pq_rounds) + k - 1]
        p_share, p_away = p_share.halve(k)
        q_share, q_away = q_share.halve(k)
        f_shares, f_rows = cut(f_shares, f_step)
        r_go, f_go = sums(where, [[p_away, q_away]], f_rows)
        if k == 1:
            r_go, f_go, b_levels[-1] = tie(r_go, f_go, b_levels[-1])
        else:
            r_go, f_go, late = tie(r_go, f_go, late)
        r_got, f_got = swap(r_go, "ctx", cbits[k]), send(f_go, f_step)
        if k == 1:
            input_grad, late = finished()
            r_got, f_got, late = tie(r_got, f_got, late)
            late = late[0].astype(F32) + swap(late[1], "wsh", 1).astype(F32)
        elif k == 2:
            for wbit in wbits[1:]:
                late = late[0::2] + swap(late[1::2].astype(BF16), "wsh", wbit).astype(F32)
            r_got, f_got, late = tie(r_got, f_got, late)
        p_share, q_share = p_share.plus(r_got, (0,)), q_share.plus(r_got, (0,), PROJ)
        f_shares = plus_all(f_shares, f_got)
    r_own, f_own = sums(where, [[p_share, q_share]], rows_of(f_shares))
    r_own, f_own, late = tie(r_own, f_own, late)
    r_levels, r_keys, f_levels, f_keys = [r_own[0]], [[0]], [f_own[0]], [[0]]
    s_steps = list(range(top))
    s_pieces = late

    def small_step(pieces, level):
        low = pieces.astype(BF16)
        return low.astype(F32) + swap(low, "ctx", cbits[level]).astype(F32)

    depth = merge_weight.shape[0]
    rest_spans = ((0, False), (PROJ, True), (PROJ + 2 * D, False))
    rest_shapes = ((part, PROJ), (depth, D), (part, VALUE_WIDTH))
    in_parts = r_levels[0].shape[1] % 8 == 0
    given = ()
    for number, (r_bit, f_bit) in enumerate(zip(reversed(cbits), [1] + cbits[:0:-1])):
        if r_bit == 1 and in_parts:
            given = place_part(r_levels, r_keys, r_order, where, rest_spans, rest_shapes, (), "place_first")
            head_part, f_levels[-1], s_pieces = tie(given[0], f_levels[-1], s_pieces)
            given = (head_part,) + tuple(given[1:])
        r_levels, r_keys = widen(r_levels, r_keys, r_bit)
        f_levels, f_keys = widen(f_levels, f_keys, f_bit)
        todo = len(s_steps) // (top - number)
        for step in s_steps[:todo]:
            s_pieces = small_step(s_pieces, step)
        s_steps = s_steps[todo:]
        if r_bit > 1:
            r_last, f_last, s_pieces = tie(r_levels[-1], f_levels[-1], s_pieces)
            r_levels, f_levels = r_levels[:-1] + [r_last], f_levels[:-1] + [f_last]
    small_total = s_pieces[0]
    grad_down, grad_up = place(
        f_levels, f_keys, f_order, where, ((0, True), (2 * D, False)), ((depth, D), (part, FF)), "place_ffn"
    )
    if in_parts:
        grad_proj, grad_merge, grad_value = place_part(
            r_levels[-1:], r_keys[-1:], r_order, where, rest_spans, rest_shapes, given, "place_rest"
        )
    else:
        grad_proj, grad_merge, grad_value = place_by_gather(
            r_levels, r_keys, r_order, where, rest_spans, rest_shapes
        )
    return (
        output[None],
        input_grad[None],
        grad_proj,
        grad_value,
        grad_merge,
        grad_up,
        grad_down,
        small_total[48],
        small_total[49],
        small_total[50],
        small_total[0:16].T,
        small_total[16:32].T,
        small_total[32:48].T,
        small_total[56:59, :zpart].T,
    )


def solution(mesh):
    rows, flat = P("wsh", None), P("wsh")
    sequence = P("wsh", "ctx", None)
    placed = (sequence, P("wsh", "ctx"), P(), sequence) + (rows,) * 5 + (flat,) * 3 + (rows,) * 4
    return jax.shard_map(
        body,
        mesh=mesh,
        in_specs=placed,
        out_specs=(sequence, sequence) + (rows,) * 5 + (flat,) * 3 + (rows,) * 4,
        check_vma=False,
    )
```

```python
import functools

import jax
import jax.numpy as jnp
from jax import lax
from jax.experimental import pallas as pl
from jax.experimental.pallas import tpu as pltpu
from jax.sharding import PartitionSpec as P

D = 512
Z = 128
VALUE_WIDTH = 1024
NDIM = 16
BLOCK_TOKENS = 128
FF = 1024
PROJ = 2 * D + Z + VALUE_WIDTH
LANES = 128
GROUPS = D // LANES
STATES = NDIM * GROUPS
PARTS = 8
F32 = jnp.float32
BF16 = jnp.bfloat16
EPS = 1e-05
PACE = 1.0
FRONT = 3
GATE = 4
SCAN = 12
SLOPE = 3.0
ADJOINT = 2.0
FINISH = 1.0
SMALL_ROWS = 56
SCALE = Z ** (-0.5)
VM = pl.BlockSpec(memory_space=pltpu.VMEM)
SM = pl.BlockSpec(memory_space=pltpu.SMEM)
HBM = pl.BlockSpec(memory_space=pltpu.HBM)
ANY = pl.BlockSpec(memory_space=pl.ANY)


sigmoid = jax.nn.sigmoid


def swish_unit(v):
    return v * sigmoid(v)


def swish_slope(v):
    s = sigmoid(v)
    return s * (1.0 + v * (1.0 - s))


def cost(us):
    return pl.CostEstimate(flops=int(us * PACE * 1e9), bytes_accessed=int(us * PACE * 3e6), transcendentals=0)


def room(mib):
    return pltpu.CompilerParams(vmem_limit_bytes=mib * 1024 * 1024)


def in_hbm(array):
    return pltpu.with_memory_space_constraint(array, pltpu.HBM)


def resident(array):
    return pltpu.with_memory_space_constraint(array, pltpu.VMEM)


def shaped(shape, dtype=F32):
    return jax.ShapeDtypeStruct(shape, dtype)


def dot(a, b):
    return jnp.dot(a, b, preferred_element_type=F32)


def dot_nt(a, b):
    return lax.dot_general(a, b, (((1,), (1,)), ((), ())), preferred_element_type=F32)


def tree_sum(terms):
    terms = list(terms)
    while len(terms) > 1:
        terms = [terms[i] + terms[i + 1] if i + 1 < len(terms) else terms[i] for i in range(0, len(terms), 2)]
    return terms[0]


def decay_tables(par_ref):
    decay = par_ref[0:NDIM, :]
    rate = sigmoid(decay)
    width = jnp.sqrt(sigmoid(-decay) * (1.0 + rate))
    return decay, rate, width


def power_of_rate(decay, count):
    return jnp.exp(-count * jnp.log1p(jnp.exp(-decay)))


def spread(table, j, g):
    return jnp.broadcast_to(table[j : j + 1, g * LANES : (g + 1) * LANES], (PARTS, LANES))


def state_rows(j, g):
    return pl.ds((j * GROUPS + g) * PARTS, PARTS)


def put_runs(ref, value, run):
    stride = ref.shape[-2] // PARTS
    if len(ref.shape) == 2:
        for h in range(PARTS):
            ref[h * stride : h * stride + run, :] = value[h * run : (h + 1) * run, :]
    else:
        for g in range(GROUPS):
            for h in range(PARTS):
                ref[g, h * stride : h * stride + run, :] = value[
                    h * run : (h + 1) * run, g * LANES : (g + 1) * LANES
                ]


def get_runs(ref, run):
    stride = ref.shape[-2] // PARTS
    return jnp.concatenate(
        [
            jnp.concatenate([ref[g, h * stride : h * stride + run, :] for h in range(PARTS)], axis=0)
            for g in range(GROUPS)
        ],
        axis=1,
    )


def at_step(ref, t, g=None):
    stride = ref.shape[-2] // PARTS
    if g is None:
        return ref[pl.ds(t, PARTS, stride=stride), :]
    return ref[g, pl.ds(t, PARTS, stride=stride), :]


def set_step(ref, t, g, value):
    stride = ref.shape[-2] // PARTS
    ref[g, pl.ds(t, PARTS, stride=stride), :] = value


def column(ref, i):
    return jnp.broadcast_to(ref[:, i : i + 1], (ref.shape[0], LANES))


class Mover:
    def __init__(self, sems):
        self.sems = sems
        self.used = 0

    def start(self, *pairs):
        copies = []
        for src, dst in pairs:
            copies.append(pltpu.make_async_copy(src, dst, self.sems.at[self.used]))
            self.used += 1
        for copy in copies:
            copy.start()
        return copies


def wait_all(copies):
    for copy in copies:
        copy.wait()


WEIGHTS = (("proj", PROJ, False), ("value", VALUE_WIDTH, False), ("merge", D, True), ("up", FF, False), ("down", D, True))
TRAVEL = ((0, 1), (2, 3, 4))
TRAVEL_LEVEL = (0, None)
WHOLE = 2


def travel_cols(i):
    return WEIGHTS[i][1] * (2 if WEIGHTS[i][2] else 1)


def spans_of(weight, base, count, shard_rows):
    _, cols, tall = WEIGHTS[weight]
    if not tall:
        return [(base, 0, cols)]
    return [(base, 0, cols), (base + shard_rows // 2, cols, 2 * cols)]


def small_kernel(dec_ref, inp_ref, rdo_ref, ng_ref, fg_ref, sg_ref, qk_ref, out_ref):
    part = out_ref.shape[1]
    rows = qk_ref.shape[1]
    out_ref[0:NDIM, :] = dec_ref[...]
    out_ref[NDIM : 2 * NDIM, :] = inp_ref[...]
    out_ref[2 * NDIM : 3 * NDIM, :] = rdo_ref[...]
    gains = jnp.concatenate([ng_ref[...], fg_ref[...], sg_ref[...]], axis=0).astype(F32)
    qk = qk_ref[...].astype(F32)
    if rows < part:
        qk = jnp.concatenate([qk, jnp.zeros((3, part - rows), F32)], axis=1)
    out_ref[3 * NDIM : SMALL_ROWS, :] = jnp.concatenate([gains, qk, jnp.zeros((2, part), F32)], axis=0).astype(BF16)


def pack_kernel(me_ref, *refs):
    shards = refs[:5]
    halves = refs[5 : 5 + len(TRAVEL)]
    move = Mover(refs[-1])
    copies = []
    for group, level, half in zip(TRAVEL, TRAVEL_LEVEL, halves):
        count = half.shape[0]
        side = 0 if level is None else (me_ref[1] >> level) & 1
        at = 0
        for w in group:
            shard_rows = shards[w].shape[0]
            for base, start, stop in spans_of(w, 0 if level is None else pl.multiple_of(side * count, count), count, shard_rows):
                copies += move.start((shards[w].at[pl.ds(base, count), :], half.at[:, at + start : at + stop]))
            at += travel_cols(w)
    wait_all(copies)


def pack_own_kernel(*refs):
    shards, out_ref = refs[:5], refs[5]
    at = 0
    for w, shard in enumerate(shards):
        rows, cols = out_ref.shape[0], shard.shape[1]
        for s in range(shard.shape[0] // rows):
            out_ref[:, at : at + cols] = shard[s * rows : (s + 1) * rows, :]
            at += cols


def gate_kernel(*refs):
    refs[-1][...] = jnp.zeros_like(refs[-1])


def build_masks(seg_ref, run, blocks, cont, head, tail=None, labels=None):
    seg = seg_ref[...].astype(F32)
    rows = [seg[:, b * BLOCK_TOKENS : (b + 1) * BLOCK_TOKENS] for b in range(blocks)]
    turned = jnp.concatenate(rows + [rows[0]] * (8 - blocks), axis=0).T
    per_block = PARTS // blocks
    stride = head.shape[0] // PARTS
    top = lax.broadcasted_iota(jnp.int32, (BLOCK_TOKENS, LANES), 0) == 0
    for b in range(blocks):
        col = jnp.broadcast_to(turned[:, b : b + 1], (BLOCK_TOKENS, LANES))
        if labels is not None:
            labels[b * BLOCK_TOKENS : (b + 1) * BLOCK_TOKENS, :] = col
        joined = jnp.where(top | (col == pltpu.roll(col, 1, 0)), 1.0, 0.0)
        for r in range(per_block):
            first = r * run
            part = col[first : first + run, :]
            entry = col[max(first - 1, 0) : max(first - 1, 0) + 1, :]
            last = col[first + run - 1 : first + run, :]
            at = (b * per_block + r) * stride
            cont[at : at + run, :] = joined[first : first + run, :]
            head[at : at + run, :] = jnp.where(part == entry, 1.0, 0.0)
            if tail is not None:
                tail[at : at + run, :] = jnp.where(part == last, 1.0, 0.0)


def normalise(x, gain):
    centred = x - jnp.mean(x, axis=-1, keepdims=True)
    inv = lax.rsqrt(jnp.mean(centred * centred, axis=-1, keepdims=True) + EPS)
    return centred * inv, inv, centred * inv * gain


def front_kernel(keys, run, blocks, *refs):
    n = len(keys)
    me_ref, tok_ref, seg_ref = refs[:3]
    small_refs = refs[3 : 3 + n]
    par_ref, qk_ref, end_ref, pay_ref, far_ref, nrm_ref, mix_ref, cont, head, tail, lab_ref = refs[3 + n : 14 + n]
    xs, os, sums, small = refs[14 + n :]
    me = me_ref[0]
    size_w = small.shape[0]
    zpart = Z // size_w
    for ref, ks in zip(small_refs, keys):
        for i, k in enumerate(ks):
            small[me ^ k] = ref[i].astype(F32)
    par_ref[...] = jnp.concatenate([small[w] for w in range(size_w)], axis=1)
    qk_ref[0:3, :] = jnp.concatenate(
        [small[w, 3 * NDIM + 3 : 3 * NDIM + 6, 0:zpart] for w in range(size_w)], axis=1
    )
    qk_ref[3:8, :] = jnp.zeros((5, Z), F32)
    normed = normalise(tok_ref[...].astype(F32), par_ref[48:49, :])[2]
    nrm_ref[...] = normed
    put_runs(xs, normed, run)
    for ref in (cont, head, tail):
        ref[...] = jnp.zeros_like(ref)
    build_masks(seg_ref, run, blocks, cont, head, tail, lab_ref)
    decay, rate, width = decay_tables(par_ref)
    gain = par_ref[32:48, :] * width * par_ref[16:32, :]
    far = power_of_rate(decay, BLOCK_TOKENS)
    rate_run = power_of_rate(decay, run)
    head_end = at_step(head, run - 1)
    for g in range(GROUPS):
        rates = [spread(rate, j, g) for j in range(NDIM)]
        gains = [spread(gain, j, g) for j in range(NDIM)]
        for j in range(NDIM):
            far_ref[j * GROUPS + g : j * GROUPS + g + 1, :] = far[j : j + 1, g * LANES : (g + 1) * LANES]

        def step(t, states, g=g, rates=rates, gains=gains):
            x_t = at_step(xs, t, g)
            c_t = at_step(cont, t)
            new = [(c_t * rates[j]) * states[j] + x_t for j in range(NDIM)]
            set_step(os, t, g, tree_sum([gains[j] * new[j] for j in range(NDIM)]))
            return tuple(new)

        zero = tuple(jnp.zeros((PARTS, LANES), F32) for _ in range(NDIM))
        ends = lax.fori_loop(0, run, step, zero, unroll=8)
        for j in range(NDIM):
            end_ref[state_rows(j, g), :] = ends[j]
            sums[state_rows(j, g), :] = ends[j] + head_end * spread(rate_run, j, g) * pltpu.roll(ends[j], 1, 0)
    per_block = PARTS // blocks
    seg = seg_ref[...].astype(F32)
    for b in range(blocks):
        ends = [seg[:, b * BLOCK_TOKENS : b * BLOCK_TOKENS + 1], seg[:, (b + 1) * BLOCK_TOKENS - 1 : (b + 1) * BLOCK_TOKENS]]
        bounds = jnp.concatenate([jnp.broadcast_to(e, (1, LANES)) for e in ends] + [jnp.zeros((6, LANES), F32)], axis=0)
        mine = jnp.concatenate([sums[pl.ds((b + 1) * per_block - 1, STATES, stride=PARTS), :], bounds], axis=0)
        for c in range(pay_ref.shape[0]):
            pay_ref[c, b] = mine.astype(BF16)
    mix_ref[...] = get_runs(os, run)


def scan_kernel(blocks, me_ref, order_ref, got_ref, far_ref, table_ref, place, kept):
    def fetch(pos):
        return got_ref[pos, 0:STATES, :].astype(F32)

    scan_states(me_ref, order_ref, fetch, got_ref, far_ref, table_ref, place, kept, blocks, True)


def scan_states(me_ref, order_ref, fetch, bnd_ref, far_ref, table, place, kept, blocks, forward):
    count = place.shape[0]
    per_block = PARTS // blocks

    def note(p, carry):
        place[order_ref[p]] = p
        return carry

    lax.fori_loop(0, count, note, 0, unroll=8)
    far = far_ref[...]

    def step(i, carry):
        state, label = carry
        pos = place[i if forward else count - 1 - i]
        bnd = bnd_ref[pos, STATES : STATES + 2, :].astype(F32)
        first, last = bnd[0:1, :], bnd[1:2, :]
        state = jnp.where((first if forward else last) == label, state, 0.0)
        kept[pos] = state
        state = jnp.where(first == last, far * state, 0.0) + fetch(pos)
        return state, (last if forward else first)

    lax.fori_loop(0, count, step, (jnp.zeros((STATES, LANES), F32), jnp.full((1, LANES), -1.0, F32)), unroll=8)
    for b in range(blocks):
        state = kept[me_ref[1] * blocks + b]
        for r in range(per_block):
            table[pl.ds(b * per_block + r, STATES, stride=PARTS), :] = state


def weight_copies(move, weight, sources, place, me, target, part):
    _, cols, tall = WEIGHTS[weight]
    level = TRAVEL_LEVEL[next(i for i, g in enumerate(TRAVEL) if weight in g)]
    side = 0 if level is None else (place >> level) & 1
    copies = []
    for ref, column, key, half in sources:
        tall_by = 2 if tall else 1
        base = (me ^ key) * (part * tall_by)
        if half is None:
            copies += move.start((ref, target.at[pl.ds(pl.multiple_of(base, part), part * tall_by), :]))
            continue
        count = part if half == WHOLE else part // 2
        base = base + (0 if half == WHOLE else side if half == 0 else 1 - side) * count
        for s in range(tall_by):
            rows = pl.ds(pl.multiple_of(base + s * part, count), count)
            copies += move.start((ref.at[:, column + s * cols : column + (s + 1) * cols], target.at[rows, :]))
    return copies


def sources_of(weight, own, own_other, travelled, keys):
    group = next(i for i, g in enumerate(TRAVEL) if weight in g)
    column = sum(travel_cols(w) for w in TRAVEL[group] if w < weight)
    out = [(own, 0, 0, None), (own_other, sum(travel_cols(w) for w in range(weight)), 1, WHOLE)]
    if TRAVEL_LEVEL[group] is None:
        near, near_other = travelled[group]
        for i, k in enumerate(keys):
            out += [(near.at[i], column, k, WHOLE), (near_other.at[i], column, k | 1, WHOLE)]
        return out
    near, far, near_other, far_other = travelled[group]
    for i, k in enumerate(keys):
        out += [(near.at[i], column, k, 0), (far.at[i], column, k, 1)]
        out += [(near_other.at[i], column, k | 1, 0), (far_other.at[i], column, k | 1, 1)]
    return out


def shard_transpose(value, me, size_w, target):
    width = value.shape[1] // size_w
    turned = value[...].T
    for shard in range(size_w):
        p = me ^ shard
        at = ((p & 1) * (size_w // 2) + (p >> 1)) * width
        target[pl.ds(pl.multiple_of(at, width), width), :] = turned[shard * width : (shard + 1) * width, :]


def store_shares(res, size_w, keep_ref, send_ref, col, tall=False):
    half = size_w // 2
    width = res.shape[1]
    steps = 2 if tall else 1
    rows = res.shape[0] // (steps * size_w)
    for i in range(size_w):
        target = keep_ref if i < half else send_ref
        for s in range(steps):
            block = res[(steps * i + s) * rows : (steps * i + s + 1) * rows, :]
            target[i % half, :, col + s * width : col + (s + 1) * width] = block.astype(BF16)


def layer_kernel(wkeys, run, blocks, size_w, *refs):
    me_ref, table, end_ref, par_ref, qk_ref, head, lab_ref, seg_ref, _ = refs[:9]
    refs = (None,) + refs
    mix, nrm, tok, cot = refs[10:14]
    own, own_other = refs[14:19], refs[19]
    travelled, at = [], 20
    for level in TRAVEL_LEVEL:
        travelled.append(refs[at : at + (2 if level is None else 4)])
        at += len(travelled[-1])
    refs = refs[at:]
    out_h, ein_ref, fgain_ref, keep, send, pre_s, act, low, mlow, gcol, dir_s, rg, ra, val, vsl, prob, q_s, k_s, ssl, sh, wp, wv, wm = refs[:23]
    (out_s, os, wu, wd, hid, gat, two, inner, ups, turned, sems) = refs[23:]
    move = Mover(sems)
    me = me_ref[0]
    part = D // size_w
    def load(w, target):
        return weight_copies(move, w, sources_of(w, own[w], own_other, travelled, wkeys), me_ref[1], me, target, part)

    loads = [load(0, wp), load(1, wv)]

    decay, rate, width = decay_tables(par_ref)
    gain = par_ref[32:48, :] * width * par_ref[16:32, :]
    rate_run = power_of_rate(decay, run)
    head_end = at_step(head, run - 1)
    head_before = pltpu.roll(head_end, 1, 0)
    per_block = PARTS // blocks
    lead = lax.broadcasted_iota(jnp.int32, (PARTS, LANES), 0) % per_block == 0
    for g in range(GROUPS):
        rates = [spread(rate, j, g) for j in range(NDIM)]
        start = []
        for j in range(NDIM):
            ent = table[state_rows(j, g), :]
            inward = pltpu.roll(end_ref[state_rows(j, g), :], 1, 0) + head_before * spread(rate_run, j, g) * ent
            ent = jnp.where(lead, ent, inward)
            ein_ref[state_rows(j, g), :] = ent
            start.append(ent * spread(gain, j, g))

        def step(t, states, g=g, rates=rates):
            new = [rates[j] * states[j] for j in range(NDIM)]
            set_step(os, t, g, tree_sum(new) * at_step(head, t))
            return tuple(new)

        lax.fori_loop(0, run, step, tuple(start), unroll=8)
    normed = nrm[...]
    pre = mix[...] + get_runs(os, run) + par_ref[50:51, :] * normed
    pre_s[...] = pre
    act[...] = swish_unit(pre).astype(BF16)
    low[...] = normed.astype(BF16)

    wait_all(loads[0])
    loads += [load(2, wm), load(3, wu), load(4, wd)]
    gates = dot(act[...], wp[:, 0 : D + Z])
    gat[...] = sigmoid(gates[:, 0:D])
    shared_in = gates[:, D : D + Z]
    shared = swish_unit(shared_in)
    sh[...] = shared
    ssl[...] = swish_slope(shared_in)
    q_s[...] = (shared * qk_ref[0:1, :] + qk_ref[1:2, :]).astype(BF16)
    k_s[...] = (shared * qk_ref[2:3, :]).astype(BF16)
    hid[...] = dot(act[...], wp[:, D + Z + VALUE_WIDTH :])
    wait_all(loads[1])
    v = dot(low[...], wv[...])
    s = sigmoid(v)
    val[...] = (v * s).astype(BF16)
    vsl[...] = (s * (1.0 + v * (1.0 - s))).astype(BF16)
    causal = lax.broadcasted_iota(jnp.int32, (BLOCK_TOKENS, BLOCK_TOKENS), 0) >= lax.broadcasted_iota(
        jnp.int32, (BLOCK_TOKENS, BLOCK_TOKENS), 1
    )
    seg = seg_ref[...].astype(F32)
    for b in range(blocks):
        rows = slice(b * BLOCK_TOKENS, (b + 1) * BLOCK_TOKENS)
        allowed = causal & (lab_ref[rows, :] == seg[:, rows])
        scores = jnp.where(allowed, dot_nt(q_s[rows, :], k_s[rows, :]) * SCALE, -1e30)
        exps = jnp.exp(scores - jnp.max(scores, axis=-1, keepdims=True))
        prob[rows, :] = exps / jnp.sum(exps, axis=-1, keepdims=True)
    r = dot(act[...], wp[:, D + Z : D + Z + VALUE_WIDTH])
    s = sigmoid(r)
    gate = r * s
    rg[...] = gate.astype(BF16)
    slope = s * (1.0 + r * (1.0 - s))
    att = jnp.concatenate(
        [
            dot(
                prob[b * BLOCK_TOKENS : (b + 1) * BLOCK_TOKENS, :].astype(BF16),
                val[b * BLOCK_TOKENS : (b + 1) * BLOCK_TOKENS, :],
            )
            for b in range(blocks)
        ],
        axis=0,
    )
    ra[...] = (slope * att).astype(BF16)
    mlow[...] = (gate * att).astype(BF16)
    wait_all(loads[2])
    hm = hid[...] + dot(mlow[...], wm[...])
    hid[...] = hm
    x = tok[...].astype(F32)
    residual = x + gat[...] * (swish_unit(hm) - x)
    n, inv, normed_two = normalise(residual, par_ref[49:50, :])
    two[...] = normed_two.astype(BF16)

    wait_all(loads[3])
    u = dot(two[...], wu[...])
    s = sigmoid(u)
    inner[...] = (u * s).astype(BF16)
    slope = s * (1.0 + u * (1.0 - s))
    wait_all(loads[4])
    ups[...] = (dot_nt(cot[...], wd[...]) * slope).astype(BF16)
    shard_transpose(inner, me, size_w, turned)
    store_shares(dot(turned[...], cot[...]), size_w, keep, send, 0, True)
    shard_transpose(two, me, size_w, turned.at[0:D])
    store_shares(dot(turned[0:D, :], ups[...]), size_w, keep, send, 2 * D)
    out_s[...] = (residual + dot(inner[...], wd[...])).astype(BF16)
    written = move.start((out_s, out_h))
    g_two = dot_nt(ups[...], wu[...])
    fgain_ref[...] = jnp.sum(g_two * n, axis=0, keepdims=True)
    h = g_two * par_ref[49:50, :]
    g_res = cot[...].astype(F32) + inv * (
        h - jnp.mean(h, axis=-1, keepdims=True) - n * jnp.mean(h * n, axis=-1, keepdims=True)
    )
    gate = gat[...]
    s = sigmoid(hm)
    gcol[:, 0:D] = (g_res * (hm * s - x) * gate * (1.0 - gate)).astype(BF16)
    gcol[:, D : 2 * D] = (g_res * gate * (s * (1.0 + hm * (1.0 - s)))).astype(BF16)
    dir_s[...] = g_res * (1.0 - gate)
    wait_all(written)


def back_kernel(
    blocks,
    size_w,
    me_ref,
    qk_ref,
    gcol,
    rg,
    ra,
    val,
    prob,
    k_s,
    q_s,
    sh,
    ssl,
    vsl,
    act,
    wm,
    gqk_ref,
    keep,
    send,
    gproj,
    gval,
    gatt,
    turned,
):
    me = me_ref[0]
    gp = dot_nt(gcol[:, D : 2 * D], wm[...])
    gatt[...] = (gp * rg[...].astype(F32)).astype(BF16)
    gproj[:, D + Z : D + Z + VALUE_WIDTH] = (gp * ra[...].astype(F32)).astype(BF16)
    gproj[:, 0:D] = gcol[:, 0:D]
    gproj[:, D + Z + VALUE_WIDTH :] = gcol[:, D : 2 * D]
    sums = [jnp.zeros((1, Z), F32)] * 3
    for b in range(blocks):
        rows = slice(b * BLOCK_TOKENS, (b + 1) * BLOCK_TOKENS)
        p = prob[rows, :]
        g_att = gatt[rows, :]
        g_probs = dot_nt(g_att, val[rows, :])
        g_values = dot(p.T.astype(BF16), g_att)
        gval[rows, :] = (g_values * vsl[rows, :].astype(F32)).astype(BF16)
        g_scores = p * (g_probs - jnp.sum(g_probs * p, axis=-1, keepdims=True))
        g_raw = g_scores * SCALE
        g_q = dot(g_raw.astype(BF16), k_s[rows, :])
        g_k = dot(g_raw.T.astype(BF16), q_s[rows, :])
        shared = sh[rows, :]
        for i, term in enumerate((g_q * shared, g_q, g_k * shared)):
            sums[i] = sums[i] + jnp.sum(term, axis=0, keepdims=True)
        g_shared = g_q * qk_ref[0:1, :] + g_k * qk_ref[2:3, :]
        gproj[rows, D : D + Z] = (g_shared * ssl[rows, :]).astype(BF16)
    gqk_ref[...] = jnp.concatenate(sums + [jnp.zeros((5, Z), F32)], axis=0)
    shard_transpose(act, me, size_w, turned)
    split = D + Z + D
    store_shares(dot(turned[...], gproj[:, 0:split]), size_w, keep, send, 0)
    store_shares(dot(turned[...], gproj[:, split:]), size_w, keep, send, split)


def back_rest_kernel(size_w, me_ref, mlow, gcol, low, gval, gproj, wp, wv, keep, send, gact, gnv, turned):
    me = me_ref[0]
    shard_transpose(mlow, me, size_w, turned)
    store_shares(dot(turned[...], gcol[:, D : 2 * D]), size_w, keep, send, 0, True)
    shard_transpose(low, me, size_w, turned.at[0:D])
    store_shares(dot(turned[0:D, :], gval[...]), size_w, keep, send, 2 * D)
    gact[...] = dot_nt(gproj[...], wp[...])
    gnv[...] = dot_nt(gval[...], wv[...])


def adjoint_kernel(run, blocks, gact_ref, pre_ref, nrm_ref, par_ref, cont, head, gmix_ref, gn_ref, lead_ref, pay_ref, gs_ref, gs, os, sums):
    normed = nrm_ref[...]
    g_mix = gact_ref[...] * swish_slope(pre_ref[...])
    gmix_ref[...] = g_mix
    gs_ref[...] = jnp.sum(g_mix * normed, axis=0, keepdims=True)
    put_runs(gs, g_mix, run)
    decay, rate, width = decay_tables(par_ref)
    gain = par_ref[32:48, :] * width * par_ref[16:32, :]
    rate_run = power_of_rate(decay, run)
    head_end = at_step(head, run - 1)
    zero = jnp.zeros((PARTS, LANES), F32)
    for g in range(GROUPS):
        rates = [spread(rate, j, g) for j in range(NDIM)]
        gains = [spread(gain, j, g) for j in range(NDIM)]

        def back(i, carries, g=g, rates=rates, gains=gains):
            t = run - 1 - i
            g_t = at_step(gs, t, g)
            c_t = at_step(cont, t)
            bs = [g_t + carries[j] for j in range(NDIM)]
            set_step(os, t, g, tree_sum([gains[j] * bs[j] for j in range(NDIM)]))
            return tuple((c_t * rates[j]) * bs[j] for j in range(NDIM))

        ends = lax.fori_loop(0, run, back, (zero,) * NDIM, unroll=8)
        for j in range(NDIM):
            lead_ref[state_rows(j, g), :] = ends[j]
            sums[state_rows(j, g), :] = ends[j] + head_end * spread(rate_run, j, g) * pltpu.roll(ends[j], PARTS - 1, 0)
    gn_ref[...] = get_runs(os, run) + par_ref[50:51, :] * g_mix
    per_block = PARTS // blocks
    for b in range(blocks):
        pay_ref[0, b] = sums[pl.ds(b * per_block, STATES, stride=PARTS), :].astype(BF16)


def slope_kernel(run, gmix_ref, nrm_ref, ein_ref, par_ref, cont, u_ref, v_ref, ve_ref, xs, gs):
    put_runs(xs, nrm_ref[...], run)
    put_runs(gs, gmix_ref[...], run)
    _, rate, _ = decay_tables(par_ref)
    zero = jnp.zeros((PARTS, LANES), F32)
    half = NDIM // 2
    for g in range(GROUPS):
        rates = [spread(rate, j, g) for j in range(NDIM)]
        for first in (0, half):
            picks = range(first, first + half)

            def ahead(t, carry, g=g, picks=picks, rates=rates):
                us, vs, uacc, vacc = carry
                g_t = at_step(gs, t, g)
                x_t = at_step(xs, t, g)
                c_t = at_step(cont, t)
                nu, nv, nua, nva = [], [], [], []
                for i, j in enumerate(picks):
                    r = c_t * rates[j]
                    v = r * vs[i] + c_t * us[i]
                    u = r * us[i] + x_t
                    nu.append(u)
                    nv.append(v)
                    nua.append(uacc[i] + g_t * u)
                    nva.append(vacc[i] + g_t * v)
                return tuple(nu), tuple(nv), tuple(nua), tuple(nva)

            us = tuple(ein_ref[state_rows(j, g), :] for j in picks)
            zeros = (zero,) * half
            us, vs, uacc, vacc = lax.fori_loop(0, run, ahead, (us, zeros, zeros, zeros), unroll=8)
            for i, j in enumerate(picks):
                u_ref[state_rows(j, g), :] = uacc[i]
                v_ref[state_rows(j, g), :] = vacc[i]
                ve_ref[state_rows(j, g), :] = vs[i]


def finish_kernel(run, blocks, keys, me_ref, order_ref, *refs):
    n = len(keys)
    back_refs = refs[:n]
    finish(run, blocks, keys, me_ref, order_ref, back_refs, *refs[n:])


def finish(run, blocks, keys, me_ref, order_ref, back_refs, bnd_ref, far_ref, gn_ref, gnv_ref, lead_ref, u_ref, v_ref, ve_ref, tok_ref, dir_ref, par_ref, head, tail, gs_ref, fg_ref, gqk_ref, ig_ref, small_ref, os, table, place, kept, gathered):
    for ref, ks in zip(back_refs, keys):
        for i, k in enumerate(ks):
            gathered[me_ref[1] ^ k] = ref[i].astype(F32)

    def fetch(pos):
        return gathered[pos // blocks, pos % blocks]

    scan_states(me_ref, order_ref, fetch, bnd_ref, far_ref, table, place, kept, blocks, False)
    decay, rate, width = decay_tables(par_ref)
    drive_in = par_ref[16:32, :]
    readout = par_ref[32:48, :]
    drive = width * drive_in
    gain = readout * drive
    rate_run = power_of_rate(decay, run)
    head_after = pltpu.roll(at_step(head, run - 1), PARTS - 1, 0)
    per_block = PARTS // blocks
    final = lax.broadcasted_iota(jnp.int32, (PARTS, LANES), 0) % per_block == per_block - 1
    u_rows, v_rows = [], []
    for g in range(GROUPS):
        rates = [spread(rate, j, g) for j in range(NDIM)]
        start = []
        u_list, v_list = [], []
        for j in range(NDIM):
            at = state_rows(j, g)
            que = table[at, :]
            inward = pltpu.roll(lead_ref[at, :], PARTS - 1, 0) + head_after * spread(rate_run, j, g) * que
            que = jnp.where(final, que, inward)
            start.append(que * spread(gain, j, g))
            u_list.append(jnp.sum(u_ref[at, :], axis=0, keepdims=True))
            v_list.append(jnp.sum(v_ref[at, :] + que * ve_ref[at, :], axis=0, keepdims=True))
        u_rows.append(jnp.concatenate(u_list, axis=0))
        v_rows.append(jnp.concatenate(v_list, axis=0))

        def step(i, states, g=g, rates=rates):
            t = run - 1 - i
            set_step(os, t, g, tree_sum(states) * at_step(tail, t))
            return tuple(rates[j] * states[j] for j in range(NDIM))

        lax.fori_loop(0, run, step, tuple(start), unroll=8)
    u_all = jnp.concatenate(u_rows, axis=1)
    v_all = jnp.concatenate(v_rows, axis=1)
    g_normed = gn_ref[...] + gnv_ref[...] + get_runs(os, run)
    x = tok_ref[...].astype(F32)
    centred = x - jnp.mean(x, axis=-1, keepdims=True)
    var = jnp.mean(centred * centred, axis=-1, keepdims=True)
    inv = lax.rsqrt(var + EPS)
    n = centred * inv
    h = g_normed * par_ref[48:49, :]
    back = inv * (h - jnp.mean(h, axis=-1, keepdims=True) - n * jnp.mean(h * n, axis=-1, keepdims=True))
    ig_ref[...] = (dir_ref[...] + back).astype(BF16)
    size_w = 2 * small_ref.shape[1]
    half = size_w // 2
    part = small_ref.shape[3]
    zpart = Z // size_w
    me = me_ref[0]
    grads = jnp.concatenate(
        [
            readout * drive * v_all * rate * (1.0 - rate)
            - readout * u_all * drive_in * rate * rate * (1.0 - rate) / width,
            readout * u_all * width,
            drive * u_all,
            jnp.sum(g_normed * n, axis=0, keepdims=True),
            fg_ref[...],
            gs_ref[...],
            jnp.zeros((5, D), F32),
        ],
        axis=0,
    )
    for w in range(size_w):
        p = me ^ w
        qk = gqk_ref[0:8, w * zpart : (w + 1) * zpart]
        if zpart < part:
            qk = jnp.concatenate([qk, jnp.zeros((8, part - zpart), F32)], axis=1)
        both = jnp.concatenate([grads[:, w * part : (w + 1) * part], qk], axis=0)
        small_ref[p & 1, p >> 1] = both.astype(BF16)


def swap(value, axis, bit):
    size = lax.axis_size(axis)
    return lax.ppermute(value, axis, [(i, i ^ bit) for i in range(size)])


def bits_of(size):
    out, bit = [], 1
    while bit < size:
        out.append(bit)
        bit *= 2
    return out


def tie(*values):
    return lax.optimization_barrier(values)


class Share:
    def __init__(self, terms, count, cols):
        self.terms = terms
        self.count = count
        self.cols = cols

    def halve(self, level):
        count = self.count // 2

        def moved(first, other):
            return lambda me: first(me) + (((me >> level) & 1) ^ other) * count

        stay = Share([(a, i, moved(f, 0), c) for a, i, f, c in self.terms], count, self.cols)
        go = Share([(a, i, moved(f, 1), c) for a, i, f, c in self.terms], count, self.cols)
        return stay, go

    def plus(self, array, lead=(), col=0):
        return Share(self.terms + [(array, lead, lambda me: 0, col)], self.count, self.cols)


def plain_sum(share, me):
    total = None
    for array, lead, first, col in share.terms:
        for i in lead:
            array = array[i]
        array = lax.dynamic_slice_in_dim(array, first(me), share.count, 0)[:, :, col : col + share.cols].astype(F32)
        total = array if total is None else total + array
    return total.astype(BF16)


def sum_kernel(plan, n, *refs):
    me = refs[0][1]
    arrays = refs[1 : 1 + n]
    outs = refs[1 + n :]
    for out, stacked in zip(outs, plan):
        for i, row in enumerate(stacked):
            column = 0
            for terms, count, cols in row:
                total = None
                for k, lead, first, col in terms:
                    value = arrays[k][(*lead, pl.ds(first(me), count), slice(None), slice(col, col + cols))].astype(F32)
                    total = value if total is None else total + value
                out[i, :, :, column : column + cols] = total.astype(BF16)
                column += cols


def sums(where, *outputs):
    first = outputs[0][0][0]
    rows = first.terms[0][0].shape[-2]
    if rows % 8:
        return [
            jnp.stack([jnp.concatenate([plain_sum(share, where[1]) for share in row], axis=2) for row in stacked])
            for stacked in outputs
        ]
    arrays, plan, shapes = [], [], []
    for stacked in outputs:
        rows_plan = []
        for row in stacked:
            row_plan = []
            for share in row:
                terms = []
                for array, lead, start, col in share.terms:
                    k = next((k for k, a in enumerate(arrays) if a is array), None)
                    if k is None:
                        k = len(arrays)
                        arrays.append(array)
                    terms.append((k, lead, start, col))
                row_plan.append((terms, share.count, share.cols))
            rows_plan.append(row_plan)
        plan.append(rows_plan)
        shapes.append(pltpu.VMEM((len(stacked), stacked[0][0].count, rows, sum(s.cols for s in stacked[0])), BF16))
    return pl.pallas_call(
        functools.partial(sum_kernel, plan, len(arrays)),
        out_shape=tuple(shapes),
        in_specs=[SM] + [VM] * len(arrays),
        out_specs=(VM,) * len(shapes),
        cost_estimate=cost(1),
        compiler_params=room(12),
        name="sums",
    )(where, *[resident(array) for array in arrays])


def far_keys(size):
    keys = []
    for bit in reversed(bits_of(size)[1:]):
        keys += [k | bit for k in [0] + keys]
    return keys


def position(place, order):
    out = 0
    for i, level in enumerate(order):
        out = out | (((place >> level) & 1) << (len(order) - 1 - i))
    return out


def place_kernel(keys, order, spans, *refs):
    n = len(keys)
    me = refs[0][1]
    pieces = refs[1 : 1 + n]
    outs = refs[1 + n :]
    for ref, ks in zip(pieces, keys):
        rows = ref.shape[1]
        for i, k in enumerate(ks):
            base = position(me ^ k, order) * rows
            for out, (start, tall) in zip(outs, spans):
                width = out.shape[1]
                for s in range(2 if tall else 1):
                    at = pl.ds(pl.multiple_of(base + s * (out.shape[0] // 2), rows), rows)
                    out[at, :] = ref[i, :, start + s * width : start + (s + 1) * width].astype(F32)


def place(levels, keys, order, where, spans, shapes, name):
    rows = levels[0].shape[1]
    if rows % 8:
        return place_by_gather(levels, keys, order, where, spans, shapes)
    return pl.pallas_call(
        functools.partial(place_kernel, keys, order, spans),
        out_shape=tuple(shaped(s) for s in shapes),
        in_specs=[SM] + [VM] * len(levels),
        cost_estimate=cost(0.1),
        compiler_params=room(16),
        name=name,
    )(where, *[resident(level) for level in levels])


def place_part_kernel(keys, order, spans, given, *refs):
    n = len(keys)
    me = refs[0][1]
    pieces = refs[1 : 1 + n]
    outs = refs[1 + n + given : 1 + n + given + len(spans)]
    wide, sems = refs[-2:]
    move = Mover(sems)
    copies, at = [], 0
    for ref, ks in zip(pieces, keys):
        rows = ref.shape[1]
        for i, k in enumerate(ks):
            wide[at] = ref[i].astype(F32)
            base = position(me ^ k, order) * rows
            for out, (start, tall) in zip(outs, spans):
                width = out.shape[1]
                for s in range(2 if tall else 1):
                    where = pl.ds(pl.multiple_of(base + s * (out.shape[0] // 2), rows), rows)
                    source = wide.at[at, :, start + s * width : start + (s + 1) * width]
                    copies += move.start((source, out.at[where, :]))
            at += 1
    wait_all(copies)


def place_part(levels, keys, order, where, spans, shapes, given, name):
    count = sum(map(len, keys))
    rows, cols = levels[0].shape[1:]
    return pl.pallas_call(
        functools.partial(place_part_kernel, keys, order, spans, len(given)),
        out_shape=tuple(pltpu.HBM(s, F32) for s in shapes),
        in_specs=[SM] + [VM] * len(levels) + [HBM] * len(given),
        out_specs=(HBM,) * len(shapes),
        input_output_aliases={1 + len(levels) + i: i for i in range(len(given))},
        scratch_shapes=[
            pltpu.VMEM((count, rows, cols), F32),
            pltpu.SemaphoreType.DMA((count * sum(2 if tall else 1 for _, tall in spans),)),
        ],
        cost_estimate=cost(0.1 if given else 4.0),
        compiler_params=room(16),
        name=name,
    )(where, *[resident(level) for level in levels], *given)


def place_by_gather(levels, keys, order, where, spans, shapes):
    flat = [k for level in keys for k in level]
    index = jnp.array([flat.index(k) for k in range(len(flat))], jnp.int32)
    holder = {position(device, order): device for device in range(len(flat))}
    picks = index[where[1] ^ jnp.array([holder[i] for i in range(len(flat))], jnp.int32)]
    block = jnp.concatenate(levels, axis=0)[picks].astype(F32)
    block = block.reshape(-1, block.shape[-1])
    outs = []
    for (start, tall), (rows, width) in zip(spans, shapes):
        columns = [block[:, start + s * width : start + (s + 1) * width] for s in range(2 if tall else 1)]
        outs.append(jnp.concatenate(columns, axis=0))
    return tuple(outs)


def body(
    tokens,
    segments,
    deal_order,
    cotangent,
    proj_weight,
    value_weight,
    merge_weight,
    ffn_up,
    ffn_down,
    norm_gain,
    ffn_gain,
    skip_gain,
    ema_decay,
    ema_input,
    ema_output,
    query_key,
):
    size_w, size_c = lax.axis_size("wsh"), lax.axis_size("ctx")
    me_w, me_c = lax.axis_index("wsh"), lax.axis_index("ctx")
    where = jnp.stack([me_w, me_c]).astype(jnp.int32)
    wbits, cbits = bits_of(size_w), bits_of(size_c)
    part = D // size_w
    zpart = Z // size_w
    half = size_w // 2
    rc = tokens.shape[1]
    blocks = rc // BLOCK_TOKENS
    run = rc // PARTS
    count = deal_order.shape[0]
    shards = (proj_weight, value_weight, merge_weight, ffn_up, ffn_down)
    group_cols = [sum(travel_cols(w) for w in group) for group in TRAVEL]

    small = pl.pallas_call(small_kernel, out_shape=shaped((SMALL_ROWS, part), BF16), cost_estimate=cost(1), compiler_params=room(60), name="small")(
        ema_decay.T,
        ema_input.T,
        ema_output.T,
        norm_gain[None],
        ffn_gain[None],
        skip_gain[None],
        query_key.T,
    )
    travel = pl.pallas_call(
        pack_kernel,
        out_shape=tuple(
            shaped((part if level is None else part // 2, c), BF16) for c, level in zip(group_cols, TRAVEL_LEVEL)
        ),
        in_specs=[SM] + [HBM] * 5,
        scratch_shapes=[pltpu.SemaphoreType.DMA((16,))],
        cost_estimate=cost(3),
        compiler_params=room(8),
        name="pack",
    )(where, *shards)

    def far_pieces(block):
        have = []
        for bit in reversed(wbits[1:]):
            sent = jnp.concatenate([block[None]] + have, axis=0) if have else block[None]
            have.append(swap(sent, "wsh", bit))
        return have[0] if len(have) == 1 else jnp.concatenate(have, axis=0)

    wkeys = far_keys(size_w)
    small_near = swap(small[None], "wsh", 1)
    small_far = far_pieces(small)
    small_far, *travel = tie(small_far, *travel)
    near = [far_pieces(block) for block in travel]
    small_last = swap(small_far, "wsh", 1)
    skeys = [[0], [1], wkeys, [k | 1 for k in wkeys]]

    pad_run = run + 1
    runs_scratch = pltpu.VMEM((GROUPS, PARTS * pad_run, LANES), F32)
    mask_shape = shaped((PARTS * pad_run, LANES))
    kept_scratch = pltpu.VMEM((count, STATES, LANES), F32)
    table_scratch = pltpu.VMEM((STATES * PARTS, LANES), F32)
    table = shaped((STATES * PARTS, LANES))
    par, qk, ends, payload, far, normed, mix_local, cont, head, tail, label_cols = pl.pallas_call(
        functools.partial(front_kernel, skeys, run, blocks),
        out_shape=(
            shaped((SMALL_ROWS, D)),
            shaped((8, Z)),
            table,
            shaped((size_c, blocks, STATES + 8, LANES), BF16),
            shaped((STATES, LANES)),
            shaped((rc, D)),
            shaped((rc, D)),
            mask_shape,
            mask_shape,
            mask_shape,
            shaped((rc, LANES)),
        ),
        in_specs=[SM] + [VM] * 6,
        scratch_shapes=[
            runs_scratch,
            runs_scratch,
            table_scratch,
            pltpu.VMEM((size_w, SMALL_ROWS, part), F32),
        ],
        cost_estimate=cost(FRONT),
        compiler_params=room(60),
        name="front",
    )(where, tokens[0], segments, small[None], small_near, small_far, small_last)
    got = lax.all_to_all(payload, "ctx", 0, 0, tiled=True).reshape(count, STATES + 8, LANES)

    for i in range(len(TRAVEL)):
        near[i] = tie(payload, near[i])[1]
    across = [
        None if level is None else swap(piece, "ctx", 1 << level) for piece, level in zip(near, TRAVEL_LEVEL)
    ]
    for i, level in enumerate(TRAVEL_LEVEL):
        if level is None:
            _, near[i] = tie(across[0], near[i])
    near_other = [swap(piece, "wsh", 1) for piece in near]
    gate = pl.pallas_call(
        gate_kernel,
        out_shape=shaped((8, LANES)),
        in_specs=[ANY] * sum(b is not None for b in across),
        cost_estimate=cost(GATE),
        compiler_params=room(1),
        name="gate",
    )(*[b for b in across if b is not None])
    tied = tie(payload, *shards)
    packed_own = pl.pallas_call(
        pack_own_kernel,
        out_shape=shaped((part, sum(travel_cols(w) for w in range(len(WEIGHTS)))), BF16),
        cost_estimate=cost(2),
        compiler_params=room(60),
        name="pack_own",
    )(*tied[1:])
    own_other = swap(packed_own, "wsh", 1)
    travelled = [
        (a, c) if b is None else (a, b, c, swap(b, "wsh", 1)) for a, b, c in zip(near, across, near_other)
    ]

    entered = pl.pallas_call(
        functools.partial(scan_kernel, blocks),
        out_shape=table,
        in_specs=[SM, SM, VM, VM],
        scratch_shapes=[pltpu.SMEM((count,), jnp.int32), kept_scratch],
        cost_estimate=cost(SCAN),
        compiler_params=room(8),
        name="scan",
    )(where, deal_order, got, far)

    saved = (
        shaped((half, part, 2 * D + FF), BF16),
        shaped((half, part, 2 * D + FF), BF16),
        shaped((rc, D)),
        shaped((rc, D), BF16),
        shaped((rc, D), BF16),
        shaped((rc, VALUE_WIDTH), BF16),
        shaped((rc, 2 * D), BF16),
        shaped((rc, D)),
        shaped((rc, VALUE_WIDTH), BF16),
        shaped((rc, VALUE_WIDTH), BF16),
        shaped((rc, VALUE_WIDTH), BF16),
        shaped((rc, VALUE_WIDTH), BF16),
        shaped((rc, BLOCK_TOKENS)),
        shaped((rc, Z), BF16),
        shaped((rc, Z), BF16),
        shaped((rc, Z)),
        shaped((rc, Z)),
        shaped((D, PROJ), BF16),
        shaped((D, VALUE_WIDTH), BF16),
        shaped((VALUE_WIDTH, D), BF16),
    )

    def held(*shapes):
        return tuple(pltpu.VMEM(s.shape, s.dtype) for s in shapes)

    copies_each = 2 + 4 * len(wkeys)
    results = pl.pallas_call(
        functools.partial(layer_kernel, wkeys, run, blocks, size_w),
        out_shape=(pltpu.HBM((rc, D), BF16), table, shaped((1, D))) + held(*saved),
        in_specs=[SM] + [VM] * 12 + [HBM] * 5 + [ANY] * (1 + sum(map(len, travelled))),
        out_specs=(HBM, VM, VM) + (VM,) * len(saved),
        scratch_shapes=[
            pltpu.VMEM((rc, D), BF16),
            runs_scratch,
            pltpu.VMEM((D, FF), BF16),
            pltpu.VMEM((FF, D), BF16),
            pltpu.VMEM((rc, D), F32),
            pltpu.VMEM((rc, D), F32),
            pltpu.VMEM((rc, D), BF16),
            pltpu.VMEM((rc, FF), BF16),
            pltpu.VMEM((rc, FF), BF16),
            pltpu.VMEM((FF, rc), BF16),
            pltpu.SemaphoreType.DMA((1 + 7 * (copies_each + 1),)),
        ],
        cost_estimate=cost(17),
        compiler_params=room(32),
        name="layer",
    )(
        where,
        entered,
        ends,
        par,
        qk,
        head,
        label_cols,
        segments,
        gate,
        *map(resident, (mix_local, normed, tokens[0], cotangent[0])),
        *map(in_hbm, shards),
        own_other,
        *[piece for group in travelled for piece in group],
    )
    output, ein, grad_ffn_gain = results[:3]
    (
        ffn_keep,
        ffn_send,
        pre_active,
        active_low,
        normed_low,
        merged_low,
        gcols,
        direct,
        reset_gate,
        reset_slope,
        values,
        value_slope,
        probs,
        queries,
        keys_low,
        shared_slope,
        shared,
        proj_full,
        value_full,
        merge_full,
    ) = results[3:]

    def shares_of(keep, got):
        cut = (half, size_c, keep.shape[1] // size_c, keep.shape[2])
        keep, got = keep.reshape(cut), got.reshape(cut)
        return [
            Share([(keep, (i,), lambda me: 0, 0), (got, (i,), lambda me: 0, 0)], size_c, cut[3]) for i in range(half)
        ]

    def plus_all(shares, got, first=0):
        return [share.plus(got, (first + i,)) for i, share in enumerate(shares)]

    def rows_of(shares):
        return [[share] for share in shares]

    def widen(levels, keys, bit):
        block = levels[0] if len(levels) == 1 else jnp.concatenate(levels, axis=0)
        return levels + [swap(block, "ctx", bit)], keys + [[k | bit for level in keys for k in level]]

    f_got = swap(ffn_send, "wsh", 1)
    gproj_shape, gval_shape = shaped((rc, PROJ), BF16), shaped((rc, VALUE_WIDTH), BF16)
    p_shape = shaped((half, part, PROJ), BF16)
    grad_qk, p_keep, p_send, gproj, gval = pl.pallas_call(
        functools.partial(back_kernel, blocks, size_w),
        out_shape=(shaped((8, Z)),) + held(p_shape, p_shape, gproj_shape, gval_shape),
        in_specs=[SM] + [VM] * 13,
        scratch_shapes=held(gval_shape, shaped((D, rc), BF16)),
        cost_estimate=cost(9),
        compiler_params=room(20),
        name="back",
    )(
        where,
        qk,
        *map(
            resident,
            (
                gcols,
                reset_gate,
                reset_slope,
                values,
                probs,
                keys_low,
                queries,
                shared,
                shared_slope,
                value_slope,
                active_low,
                merge_full,
            ),
        ),
    )
    p_got = swap(p_send, "wsh", 1)
    gproj = tie(p_send, gproj)[1]
    q_shape = shaped((half, part, 2 * D + VALUE_WIDTH), BF16)
    q_keep, q_send, grad_active, grad_normed_value = pl.pallas_call(
        functools.partial(back_rest_kernel, size_w),
        out_shape=held(q_shape, q_shape, shaped((rc, D)), shaped((rc, D))),
        in_specs=[SM] + [VM] * 7,
        scratch_shapes=[pltpu.VMEM((VALUE_WIDTH, rc), BF16)],
        cost_estimate=cost(7),
        compiler_params=room(20),
        name="back_rest",
    )(where, *map(resident, (merged_low, gcols, normed_low, gval, gproj, proj_full, value_full)))

    top = len(cbits)
    pq_rounds = [(("w", k), ("c", 0) if k == 0 else ("w", k - 1)) for k in range(len(wbits) - 1)]
    pq_rounds.append((("c", 0), ("w", len(wbits) - 2)))
    r_order = [0] + list(range(1, top))
    f_steps = [("c", 1)] + [("w", k) for k in range(len(wbits) - 1)]
    f_steps += [("c", k) for k in range(2, top)] + [("c", 0)]
    f_order = list(range(1, top)) + [0]

    def cut(shares, step):
        kind, k = step
        if kind == "w":
            return shares[0::2], rows_of(shares[1::2])
        both = [share.halve(k) for share in shares]
        return [stay for stay, _ in both], rows_of([away for _, away in both])

    def send(value, step):
        kind, k = step
        return swap(value, "wsh", wbits[k + 1]) if kind == "w" else swap(value, "ctx", cbits[k])

    p_shares, f_shares = shares_of(p_keep, p_got), shares_of(ffn_keep, f_got)
    p_shares, p_rows = cut(p_shares, pq_rounds[0][0])
    f_shares, f_rows = cut(f_shares, f_steps[0])
    p_go, f_go = sums(where, p_rows, f_rows)
    p_go, f_go, q_send = tie(p_go, f_go, q_send)
    q_got = swap(q_send, "wsh", 1)
    p_got, f_got = send(p_go, pq_rounds[0][0]), send(f_go, f_steps[0])
    q_shares, q_rows = cut(shares_of(q_keep, q_got), pq_rounds[0][1])
    (q_go,) = sums(where, q_rows)
    q_go, grad_active = tie(q_go, grad_active)
    q_got = send(q_go, pq_rounds[0][1])
    g_mix, gn_local, leads, payload_back, grad_skip = pl.pallas_call(
        functools.partial(adjoint_kernel, run, blocks),
        out_shape=(
            shaped((rc, D)),
            shaped((rc, D)),
            table,
            shaped((1, blocks, STATES, LANES), BF16),
            shaped((1, D)),
        ),
        scratch_shapes=[runs_scratch] * 2 + [table_scratch],
        cost_estimate=cost(ADJOINT),
        compiler_params=room(20),
        name="adjoint",
    )(grad_active, pre_active, normed, par, cont, head)
    b_levels, b_keys = [payload_back], [[0]]
    for bit in reversed(cbits[3:]):
        b_levels, b_keys = widen(b_levels, b_keys, bit)
    block = b_levels[0] if len(b_levels) == 1 else jnp.concatenate(b_levels, axis=0)
    flat = [k for level in b_keys for k in level]
    b_keys += [[k | bit for k in flat] for bit in (cbits[1] | cbits[2], cbits[2], cbits[1])]
    b_levels += [swap(block, "ctx", bit) for bit in (cbits[1] | cbits[2], cbits[2])]
    u_part, v_part, v_end = pl.pallas_call(
        functools.partial(slope_kernel, run),
        out_shape=(table, table, table),
        scratch_shapes=[runs_scratch] * 2,
        cost_estimate=cost(SLOPE),
        compiler_params=room(16),
        name="slope",
    )(g_mix, normed, ein, par, cont)
    block, u_part = tie(block, u_part)
    b_last = swap(block, "ctx", cbits[1])

    p_got, q_got, f_got, u_part, *b_levels = tie(p_got, q_got, f_got, u_part, *b_levels)
    b_levels.append(b_last)
    p_shares, q_shares, f_shares = plus_all(p_shares, p_got), plus_all(q_shares, q_got), plus_all(f_shares, f_got)
    for number in range(1, len(pq_rounds)):
        p_step, q_step = pq_rounds[number]
        f_step = f_steps[number]
        p_shares, p_rows = cut(p_shares, p_step)
        q_shares, q_rows = cut(q_shares, q_step)
        f_shares, f_rows = cut(f_shares, f_step)
        together = q_step == f_step
        if together:
            p_go, q_go = sums(where, p_rows, q_rows + f_rows)
            p_go, q_go, b_levels[-2] = tie(p_go, q_go, b_levels[-2])
            p_got, q_got = send(p_go, p_step), send(q_go, q_step)
            f_got = q_got
        else:
            p_go, q_go, f_go = sums(where, p_rows, q_rows, f_rows)
            p_go, q_go, f_go, b_levels[-2] = tie(p_go, q_go, f_go, b_levels[-2])
            p_got, q_got, f_got = send(p_go, p_step), send(q_go, q_step), send(f_go, f_step)
        if number == 1:
            b_levels, b_keys = widen(b_levels, b_keys, 1)
        p_got, q_got, f_got, b_levels[-1] = tie(p_got, q_got, f_got, b_levels[-1])
        if together:
            f_got = q_got
        p_shares, q_shares = plus_all(p_shares, p_got), plus_all(q_shares, q_got)
        f_shares = plus_all(f_shares, f_got, len(q_rows) if together else 0)
    (p_share,), (q_share,) = p_shares, q_shares

    def finished():
        input_grad, small_share = pl.pallas_call(
            functools.partial(finish_kernel, run, blocks, b_keys),
            out_shape=(shaped((rc, D), BF16), shaped((2, half, SMALL_ROWS + 8, part), BF16)),
            in_specs=[SM, SM] + [VM] * (16 + len(b_keys)),
            scratch_shapes=[
                runs_scratch,
                table_scratch,
                pltpu.SMEM((count,), jnp.int32),
                kept_scratch,
                pltpu.VMEM((size_c, blocks, STATES, LANES), F32),
            ],
            cost_estimate=cost(FINISH),
            compiler_params=room(20),
            name="finish",
        )(
            where,
            deal_order,
            *b_levels,
            got,
            far,
            gn_local,
            grad_normed_value,
            leads,
            u_part,
            v_part,
            v_end,
            tokens[0],
            direct,
            par,
            head,
            tail,
            grad_skip,
            grad_ffn_gain,
            grad_qk,
        )
        return input_grad, small_share

    late = None
    for k in range(1, top):
        f_step = f_steps[len(pq_rounds) + k - 1]
        p_share, p_away = p_share.halve(k)
        q_share, q_away = q_share.halve(k)
        f_shares, f_rows = cut(f_shares, f_step)
        r_go, f_go = sums(where, [[p_away, q_away]], f_rows)
        if k == 1:
            r_go, f_go, b_levels[-1] = tie(r_go, f_go, b_levels[-1])
        else:
            r_go, f_go, late = tie(r_go, f_go, late)
        r_got, f_got = swap(r_go, "ctx", cbits[k]), send(f_go, f_step)
        if k == 1:
            input_grad, late = finished()
            r_got, f_got, late = tie(r_got, f_got, late)
            late = late[0].astype(F32) + swap(late[1], "wsh", 1).astype(F32)
        elif k == 2:
            for wbit in wbits[1:]:
                late = late[0::2] + swap(late[1::2].astype(BF16), "wsh", wbit).astype(F32)
            r_got, f_got, late = tie(r_got, f_got, late)
        p_share, q_share = p_share.plus(r_got, (0,)), q_share.plus(r_got, (0,), PROJ)
        f_shares = plus_all(f_shares, f_got)
    r_own, f_own = sums(where, [[p_share, q_share]], rows_of(f_shares))
    r_own, f_own, late = tie(r_own, f_own, late)
    r_levels, r_keys, f_levels, f_keys = [r_own[0]], [[0]], [f_own[0]], [[0]]
    s_steps = list(range(top))
    s_pieces = late

    def small_step(pieces, level):
        low = pieces.astype(BF16)
        return low.astype(F32) + swap(low, "ctx", cbits[level]).astype(F32)

    depth = merge_weight.shape[0]
    rest_spans = ((0, False), (PROJ, True), (PROJ + 2 * D, False))
    rest_shapes = ((part, PROJ), (depth, D), (part, VALUE_WIDTH))
    in_parts = r_levels[0].shape[1] % 8 == 0
    given = ()
    for number, (r_bit, f_bit) in enumerate(zip(reversed(cbits), [1] + cbits[:0:-1])):
        if r_bit == 1 and in_parts:
            given = place_part(r_levels, r_keys, r_order, where, rest_spans, rest_shapes, (), "place_first")
            head_part, f_levels[-1], s_pieces = tie(given[0], f_levels[-1], s_pieces)
            given = (head_part,) + tuple(given[1:])
        r_levels, r_keys = widen(r_levels, r_keys, r_bit)
        f_levels, f_keys = widen(f_levels, f_keys, f_bit)
        todo = len(s_steps) // (top - number)
        for step in s_steps[:todo]:
            s_pieces = small_step(s_pieces, step)
        s_steps = s_steps[todo:]
        if r_bit > 1:
            r_last, f_last, s_pieces = tie(r_levels[-1], f_levels[-1], s_pieces)
            r_levels, f_levels = r_levels[:-1] + [r_last], f_levels[:-1] + [f_last]
    small_total = s_pieces[0]
    grad_down, grad_up = place(
        f_levels, f_keys, f_order, where, ((0, True), (2 * D, False)), ((depth, D), (part, FF)), "place_ffn"
    )
    if in_parts:
        grad_proj, grad_merge, grad_value = place_part(
            r_levels[-1:], r_keys[-1:], r_order, where, rest_spans, rest_shapes, given, "place_rest"
        )
    else:
        grad_proj, grad_merge, grad_value = place_by_gather(
            r_levels, r_keys, r_order, where, rest_spans, rest_shapes
        )
    return (
        output[None],
        input_grad[None],
        grad_proj,
        grad_value,
        grad_merge,
        grad_up,
        grad_down,
        small_total[48],
        small_total[49],
        small_total[50],
        small_total[0:16].T,
        small_total[16:32].T,
        small_total[32:48].T,
        small_total[56:59, :zpart].T,
    )


def solution(mesh):
    rows, flat = P("wsh", None), P("wsh")
    sequence = P("wsh", "ctx", None)
    placed = (sequence, P("wsh", "ctx"), P(), sequence) + (rows,) * 5 + (flat,) * 3 + (rows,) * 4
    return jax.shard_map(
        body,
        mesh=mesh,
        in_specs=placed,
        out_specs=(sequence, sequence) + (rows,) * 5 + (flat,) * 3 + (rows,) * 4,
        check_vma=False,
    )
```

```python
import functools

import jax
import jax.numpy as jnp
from jax import lax
from jax.experimental import pallas as pl
from jax.experimental.pallas import tpu as pltpu
from jax.sharding import PartitionSpec as P

D = 512
Z = 128
VALUE_WIDTH = 1024
NDIM = 16
BLOCK_TOKENS = 128
FF = 1024
PROJ = 2 * D + Z + VALUE_WIDTH
LANES = 128
GROUPS = D // LANES
STATES = NDIM * GROUPS
PARTS = 8
F32 = jnp.float32
BF16 = jnp.bfloat16
EPS = 1e-05
PACE = 1.0
FRONT = 3
GATE = 4
SCAN = 12
SLOPE = 3.0
ADJOINT = 2.0
FINISH = 1.0
SMALL_ROWS = 56
SCALE = Z ** (-0.5)
VM = pl.BlockSpec(memory_space=pltpu.VMEM)
SM = pl.BlockSpec(memory_space=pltpu.SMEM)
HBM = pl.BlockSpec(memory_space=pltpu.HBM)
ANY = pl.BlockSpec(memory_space=pl.ANY)


sigmoid = jax.nn.sigmoid


def swish_unit(v):
    return v * sigmoid(v)


def swish_slope(v):
    s = sigmoid(v)
    return s * (1.0 + v * (1.0 - s))


def cost(us):
    return pl.CostEstimate(flops=int(us * PACE * 1e9), bytes_accessed=int(us * PACE * 3e6), transcendentals=0)


def room(mib):
    return pltpu.CompilerParams(vmem_limit_bytes=mib * 1024 * 1024)


def in_hbm(array):
    return pltpu.with_memory_space_constraint(array, pltpu.HBM)


def resident(array):
    return pltpu.with_memory_space_constraint(array, pltpu.VMEM)


def shaped(shape, dtype=F32):
    return jax.ShapeDtypeStruct(shape, dtype)


def dot(a, b):
    return jnp.dot(a, b, preferred_element_type=F32)


def dot_nt(a, b):
    return lax.dot_general(a, b, (((1,), (1,)), ((), ())), preferred_element_type=F32)


def tree_sum(terms):
    terms = list(terms)
    while len(terms) > 1:
        terms = [terms[i] + terms[i + 1] if i + 1 < len(terms) else terms[i] for i in range(0, len(terms), 2)]
    return terms[0]


def decay_tables(par_ref):
    decay = par_ref[0:NDIM, :]
    rate = sigmoid(decay)
    width = jnp.sqrt(sigmoid(-decay) * (1.0 + rate))
    return decay, rate, width


def power_of_rate(decay, count):
    return jnp.exp(-count * jnp.log1p(jnp.exp(-decay)))


def spread(table, j, g):
    return jnp.broadcast_to(table[j : j + 1, g * LANES : (g + 1) * LANES], (PARTS, LANES))


def state_rows(j, g):
    return pl.ds((j * GROUPS + g) * PARTS, PARTS)


def put_runs(ref, value, run):
    stride = ref.shape[-2] // PARTS
    if len(ref.shape) == 2:
        for h in range(PARTS):
            ref[h * stride : h * stride + run, :] = value[h * run : (h + 1) * run, :]
    else:
        for g in range(GROUPS):
            for h in range(PARTS):
                ref[g, h * stride : h * stride + run, :] = value[
                    h * run : (h + 1) * run, g * LANES : (g + 1) * LANES
                ]


def get_runs(ref, run):
    stride = ref.shape[-2] // PARTS
    return jnp.concatenate(
        [
            jnp.concatenate([ref[g, h * stride : h * stride + run, :] for h in range(PARTS)], axis=0)
            for g in range(GROUPS)
        ],
        axis=1,
    )


def at_step(ref, t, g=None):
    stride = ref.shape[-2] // PARTS
    if g is None:
        return ref[pl.ds(t, PARTS, stride=stride), :]
    return ref[g, pl.ds(t, PARTS, stride=stride), :]


def set_step(ref, t, g, value):
    stride = ref.shape[-2] // PARTS
    ref[g, pl.ds(t, PARTS, stride=stride), :] = value


def column(ref, i):
    return jnp.broadcast_to(ref[:, i : i + 1], (ref.shape[0], LANES))


class Mover:
    def __init__(self, sems):
        self.sems = sems
        self.used = 0

    def start(self, *pairs):
        copies = []
        for src, dst in pairs:
            copies.append(pltpu.make_async_copy(src, dst, self.sems.at[self.used]))
            self.used += 1
        for copy in copies:
            copy.start()
        return copies


def wait_all(copies):
    for copy in copies:
        copy.wait()


WEIGHTS = (("proj", PROJ, False), ("value", VALUE_WIDTH, False), ("merge", D, True), ("up", FF, False), ("down", D, True))
TRAVEL = ((0, 1), (2, 3, 4))
TRAVEL_LEVEL = (0, None)
WHOLE = 2


def travel_cols(i):
    return WEIGHTS[i][1] * (2 if WEIGHTS[i][2] else 1)


def spans_of(weight, base, count, shard_rows):
    _, cols, tall = WEIGHTS[weight]
    if not tall:
        return [(base, 0, cols)]
    return [(base, 0, cols), (base + shard_rows // 2, cols, 2 * cols)]


def small_kernel(dec_ref, inp_ref, rdo_ref, ng_ref, fg_ref, sg_ref, qk_ref, out_ref):
    part = out_ref.shape[1]
    rows = qk_ref.shape[1]
    out_ref[0:NDIM, :] = dec_ref[...]
    out_ref[NDIM : 2 * NDIM, :] = inp_ref[...]
    out_ref[2 * NDIM : 3 * NDIM, :] = rdo_ref[...]
    gains = jnp.concatenate([ng_ref[...], fg_ref[...], sg_ref[...]], axis=0).astype(F32)
    qk = qk_ref[...].astype(F32)
    if rows < part:
        qk = jnp.concatenate([qk, jnp.zeros((3, part - rows), F32)], axis=1)
    out_ref[3 * NDIM : SMALL_ROWS, :] = jnp.concatenate([gains, qk, jnp.zeros((2, part), F32)], axis=0).astype(BF16)


def pack_kernel(me_ref, *refs):
    shards = refs[:5]
    halves = refs[5 : 5 + len(TRAVEL)]
    move = Mover(refs[-1])
    copies = []
    for group, level, half in zip(TRAVEL, TRAVEL_LEVEL, halves):
        count = half.shape[0]
        side = 0 if level is None else (me_ref[1] >> level) & 1
        at = 0
        for w in group:
            shard_rows = shards[w].shape[0]
            for base, start, stop in spans_of(w, 0 if level is None else pl.multiple_of(side * count, count), count, shard_rows):
                copies += move.start((shards[w].at[pl.ds(base, count), :], half.at[:, at + start : at + stop]))
            at += travel_cols(w)
    wait_all(copies)


def pack_own_kernel(*refs):
    shards, out_ref = refs[:5], refs[5]
    at = 0
    for w, shard in enumerate(shards):
        rows, cols = out_ref.shape[0], shard.shape[1]
        for s in range(shard.shape[0] // rows):
            out_ref[:, at : at + cols] = shard[s * rows : (s + 1) * rows, :]
            at += cols


def gate_kernel(*refs):
    refs[-1][...] = jnp.zeros_like(refs[-1])


def build_masks(seg_ref, run, blocks, cont, head, tail=None, labels=None):
    seg = seg_ref[...].astype(F32)
    rows = [seg[:, b * BLOCK_TOKENS : (b + 1) * BLOCK_TOKENS] for b in range(blocks)]
    turned = jnp.concatenate(rows + [rows[0]] * (8 - blocks), axis=0).T
    per_block = PARTS // blocks
    stride = head.shape[0] // PARTS
    top = lax.broadcasted_iota(jnp.int32, (BLOCK_TOKENS, LANES), 0) == 0
    for b in range(blocks):
        col = jnp.broadcast_to(turned[:, b : b + 1], (BLOCK_TOKENS, LANES))
        if labels is not None:
            labels[b * BLOCK_TOKENS : (b + 1) * BLOCK_TOKENS, :] = col
        joined = jnp.where(top | (col == pltpu.roll(col, 1, 0)), 1.0, 0.0)
        for r in range(per_block):
            first = r * run
            part = col[first : first + run, :]
            entry = col[max(first - 1, 0) : max(first - 1, 0) + 1, :]
            last = col[first + run - 1 : first + run, :]
            at = (b * per_block + r) * stride
            cont[at : at + run, :] = joined[first : first + run, :]
            head[at : at + run, :] = jnp.where(part == entry, 1.0, 0.0)
            if tail is not None:
                tail[at : at + run, :] = jnp.where(part == last, 1.0, 0.0)


def normalise(x, gain):
    centred = x - jnp.mean(x, axis=-1, keepdims=True)
    inv = lax.rsqrt(jnp.mean(centred * centred, axis=-1, keepdims=True) + EPS)
    return centred * inv, inv, centred * inv * gain


def front_kernel(keys, run, blocks, *refs):
    n = len(keys)
    me_ref, tok_ref, seg_ref = refs[:3]
    small_refs = refs[3 : 3 + n]
    par_ref, qk_ref, end_ref, pay_ref, far_ref, nrm_ref, mix_ref, cont, head, tail, lab_ref = refs[3 + n : 14 + n]
    xs, os, sums, small = refs[14 + n :]
    me = me_ref[0]
    size_w = small.shape[0]
    zpart = Z // size_w
    for ref, ks in zip(small_refs, keys):
        for i, k in enumerate(ks):
            small[me ^ k] = ref[i].astype(F32)
    par_ref[...] = jnp.concatenate([small[w] for w in range(size_w)], axis=1)
    qk_ref[0:3, :] = jnp.concatenate(
        [small[w, 3 * NDIM + 3 : 3 * NDIM + 6, 0:zpart] for w in range(size_w)], axis=1
    )
    qk_ref[3:8, :] = jnp.zeros((5, Z), F32)
    normed = normalise(tok_ref[...].astype(F32), par_ref[48:49, :])[2]
    nrm_ref[...] = normed
    put_runs(xs, normed, run)
    for ref in (cont, head, tail):
        ref[...] = jnp.zeros_like(ref)
    build_masks(seg_ref, run, blocks, cont, head, tail, lab_ref)
    decay, rate, width = decay_tables(par_ref)
    gain = par_ref[32:48, :] * width * par_ref[16:32, :]
    far = power_of_rate(decay, BLOCK_TOKENS)
    rate_run = power_of_rate(decay, run)
    head_end = at_step(head, run - 1)
    for g in range(GROUPS):
        rates = [spread(rate, j, g) for j in range(NDIM)]
        gains = [spread(gain, j, g) for j in range(NDIM)]
        for j in range(NDIM):
            far_ref[j * GROUPS + g : j * GROUPS + g + 1, :] = far[j : j + 1, g * LANES : (g + 1) * LANES]

        def step(t, states, g=g, rates=rates, gains=gains):
            x_t = at_step(xs, t, g)
            c_t = at_step(cont, t)
            new = [(c_t * rates[j]) * states[j] + x_t for j in range(NDIM)]
            set_step(os, t, g, tree_sum([gains[j] * new[j] for j in range(NDIM)]))
            return tuple(new)

        zero = tuple(jnp.zeros((PARTS, LANES), F32) for _ in range(NDIM))
        ends = lax.fori_loop(0, run, step, zero, unroll=16)
        for j in range(NDIM):
            end_ref[state_rows(j, g), :] = ends[j]
            sums[state_rows(j, g), :] = ends[j] + head_end * spread(rate_run, j, g) * pltpu.roll(ends[j], 1, 0)
    per_block = PARTS // blocks
    seg = seg_ref[...].astype(F32)
    for b in range(blocks):
        ends = [seg[:, b * BLOCK_TOKENS : b * BLOCK_TOKENS + 1], seg[:, (b + 1) * BLOCK_TOKENS - 1 : (b + 1) * BLOCK_TOKENS]]
        bounds = jnp.concatenate([jnp.broadcast_to(e, (1, LANES)) for e in ends] + [jnp.zeros((6, LANES), F32)], axis=0)
        mine = jnp.concatenate([sums[pl.ds((b + 1) * per_block - 1, STATES, stride=PARTS), :], bounds], axis=0)
        for c in range(pay_ref.shape[0]):
            pay_ref[c, b] = mine.astype(BF16)
    mix_ref[...] = get_runs(os, run)


def scan_kernel(blocks, me_ref, order_ref, got_ref, far_ref, table_ref, place, kept):
    def fetch(pos):
        return got_ref[pos, 0:STATES, :].astype(F32)

    scan_states(me_ref, order_ref, fetch, got_ref, far_ref, table_ref, place, kept, blocks, True)


def scan_states(me_ref, order_ref, fetch, bnd_ref, far_ref, table, place, kept, blocks, forward):
    count = place.shape[0]
    per_block = PARTS // blocks

    def note(p, carry):
        place[order_ref[p]] = p
        return carry

    lax.fori_loop(0, count, note, 0, unroll=16)
    far = far_ref[...]

    def step(i, carry):
        state, label = carry
        pos = place[i if forward else count - 1 - i]
        bnd = bnd_ref[pos, STATES : STATES + 2, :].astype(F32)
        first, last = bnd[0:1, :], bnd[1:2, :]
        state = jnp.where((first if forward else last) == label, state, 0.0)
        kept[pos] = state
        state = jnp.where(first == last, far * state, 0.0) + fetch(pos)
        return state, (last if forward else first)

    lax.fori_loop(0, count, step, (jnp.zeros((STATES, LANES), F32), jnp.full((1, LANES), -1.0, F32)), unroll=16)
    for b in range(blocks):
        state = kept[me_ref[1] * blocks + b]
        for r in range(per_block):
            table[pl.ds(b * per_block + r, STATES, stride=PARTS), :] = state


def weight_copies(move, weight, sources, place, me, target, part):
    _, cols, tall = WEIGHTS[weight]
    level = TRAVEL_LEVEL[next(i for i, g in enumerate(TRAVEL) if weight in g)]
    side = 0 if level is None else (place >> level) & 1
    copies = []
    for ref, column, key, half in sources:
        tall_by = 2 if tall else 1
        base = (me ^ key) * (part * tall_by)
        if half is None:
            copies += move.start((ref, target.at[pl.ds(pl.multiple_of(base, part), part * tall_by), :]))
            continue
        count = part if half == WHOLE else part // 2
        base = base + (0 if half == WHOLE else side if half == 0 else 1 - side) * count
        for s in range(tall_by):
            rows = pl.ds(pl.multiple_of(base + s * part, count), count)
            copies += move.start((ref.at[:, column + s * cols : column + (s + 1) * cols], target.at[rows, :]))
    return copies


def sources_of(weight, own, own_other, travelled, keys):
    group = next(i for i, g in enumerate(TRAVEL) if weight in g)
    column = sum(travel_cols(w) for w in TRAVEL[group] if w < weight)
    out = [(own, 0, 0, None), (own_other, sum(travel_cols(w) for w in range(weight)), 1, WHOLE)]
    if TRAVEL_LEVEL[group] is None:
        near, near_other = travelled[group]
        for i, k in enumerate(keys):
            out += [(near.at[i], column, k, WHOLE), (near_other.at[i], column, k | 1, WHOLE)]
        return out
    near, far, near_other, far_other = travelled[group]
    for i, k in enumerate(keys):
        out += [(near.at[i], column, k, 0), (far.at[i], column, k, 1)]
        out += [(near_other.at[i], column, k | 1, 0), (far_other.at[i], column, k | 1, 1)]
    return out


def shard_transpose(value, me, size_w, target):
    width = value.shape[1] // size_w
    turned = value[...].T
    for shard in range(size_w):
        p = me ^ shard
        at = ((p & 1) * (size_w // 2) + (p >> 1)) * width
        target[pl.ds(pl.multiple_of(at, width), width), :] = turned[shard * width : (shard + 1) * width, :]


def store_shares(res, size_w, keep_ref, send_ref, col, tall=False):
    half = size_w // 2
    width = res.shape[1]
    steps = 2 if tall else 1
    rows = res.shape[0] // (steps * size_w)
    for i in range(size_w):
        target = keep_ref if i < half else send_ref
        for s in range(steps):
            block = res[(steps * i + s) * rows : (steps * i + s + 1) * rows, :]
            target[i % half, :, col + s * width : col + (s + 1) * width] = block.astype(BF16)


def layer_kernel(wkeys, run, blocks, size_w, *refs):
    me_ref, table, end_ref, par_ref, qk_ref, head, lab_ref, seg_ref, _ = refs[:9]
    refs = (None,) + refs
    mix, nrm, tok, cot = refs[10:14]
    own, own_other = refs[14:19], refs[19]
    travelled, at = [], 20
    for level in TRAVEL_LEVEL:
        travelled.append(refs[at : at + (2 if level is None else 4)])
        at += len(travelled[-1])
    refs = refs[at:]
    out_h, ein_ref, fgain_ref, keep, send, pre_s, act, low, mlow, gcol, dir_s, rg, ra, val, vsl, prob, q_s, k_s, ssl, sh, wp, wv, wm = refs[:23]
    (out_s, os, wu, wd, hid, gat, two, inner, ups, turned, sems) = refs[23:]
    move = Mover(sems)
    me = me_ref[0]
    part = D // size_w
    def load(w, target):
        return weight_copies(move, w, sources_of(w, own[w], own_other, travelled, wkeys), me_ref[1], me, target, part)

    loads = [load(0, wp), load(1, wv)]

    decay, rate, width = decay_tables(par_ref)
    gain = par_ref[32:48, :] * width * par_ref[16:32, :]
    rate_run = power_of_rate(decay, run)
    head_end = at_step(head, run - 1)
    head_before = pltpu.roll(head_end, 1, 0)
    per_block = PARTS // blocks
    lead = lax.broadcasted_iota(jnp.int32, (PARTS, LANES), 0) % per_block == 0
    for g in range(GROUPS):
        rates = [spread(rate, j, g) for j in range(NDIM)]
        start = []
        for j in range(NDIM):
            ent = table[state_rows(j, g), :]
            inward = pltpu.roll(end_ref[state_rows(j, g), :], 1, 0) + head_before * spread(rate_run, j, g) * ent
            ent = jnp.where(lead, ent, inward)
            ein_ref[state_rows(j, g), :] = ent
            start.append(ent * spread(gain, j, g))

        def step(t, states, g=g, rates=rates):
            new = [rates[j] * states[j] for j in range(NDIM)]
            set_step(os, t, g, tree_sum(new) * at_step(head, t))
            return tuple(new)

        lax.fori_loop(0, run, step, tuple(start), unroll=16)
    normed = nrm[...]
    pre = mix[...] + get_runs(os, run) + par_ref[50:51, :] * normed
    pre_s[...] = pre
    act[...] = swish_unit(pre).astype(BF16)
    low[...] = normed.astype(BF16)

    wait_all(loads[0])
    loads += [load(2, wm), load(3, wu), load(4, wd)]
    gates = dot(act[...], wp[:, 0 : D + Z])
    gat[...] = sigmoid(gates[:, 0:D])
    shared_in = gates[:, D : D + Z]
    shared = swish_unit(shared_in)
    sh[...] = shared
    ssl[...] = swish_slope(shared_in)
    q_s[...] = (shared * qk_ref[0:1, :] + qk_ref[1:2, :]).astype(BF16)
    k_s[...] = (shared * qk_ref[2:3, :]).astype(BF16)
    hid[...] = dot(act[...], wp[:, D + Z + VALUE_WIDTH :])
    wait_all(loads[1])
    v = dot(low[...], wv[...])
    s = sigmoid(v)
    val[...] = (v * s).astype(BF16)
    vsl[...] = (s * (1.0 + v * (1.0 - s))).astype(BF16)
    causal = lax.broadcasted_iota(jnp.int32, (BLOCK_TOKENS, BLOCK_TOKENS), 0) >= lax.broadcasted_iota(
        jnp.int32, (BLOCK_TOKENS, BLOCK_TOKENS), 1
    )
    seg = seg_ref[...].astype(F32)
    for b in range(blocks):
        rows = slice(b * BLOCK_TOKENS, (b + 1) * BLOCK_TOKENS)
        allowed = causal & (lab_ref[rows, :] == seg[:, rows])
        scores = jnp.where(allowed, dot_nt(q_s[rows, :], k_s[rows, :]) * SCALE, -1e30)
        exps = jnp.exp(scores - jnp.max(scores, axis=-1, keepdims=True))
        prob[rows, :] = exps / jnp.sum(exps, axis=-1, keepdims=True)
    r = dot(act[...], wp[:, D + Z : D + Z + VALUE_WIDTH])
    s = sigmoid(r)
    gate = r * s
    rg[...] = gate.astype(BF16)
    slope = s * (1.0 + r * (1.0 - s))
    att = jnp.concatenate(
        [
            dot(
                prob[b * BLOCK_TOKENS : (b + 1) * BLOCK_TOKENS, :].astype(BF16),
                val[b * BLOCK_TOKENS : (b + 1) * BLOCK_TOKENS, :],
            )
            for b in range(blocks)
        ],
        axis=0,
    )
    ra[...] = (slope * att).astype(BF16)
    mlow[...] = (gate * att).astype(BF16)
    wait_all(loads[2])
    hm = hid[...] + dot(mlow[...], wm[...])
    hid[...] = hm
    x = tok[...].astype(F32)
    residual = x + gat[...] * (swish_unit(hm) - x)
    n, inv, normed_two = normalise(residual, par_ref[49:50, :])
    two[...] = normed_two.astype(BF16)

    wait_all(loads[3])
    u = dot(two[...], wu[...])
    s = sigmoid(u)
    inner[...] = (u * s).astype(BF16)
    slope = s * (1.0 + u * (1.0 - s))
    wait_all(loads[4])
    ups[...] = (dot_nt(cot[...], wd[...]) * slope).astype(BF16)
    shard_transpose(inner, me, size_w, turned)
    store_shares(dot(turned[...], cot[...]), size_w, keep, send, 0, True)
    shard_transpose(two, me, size_w, turned.at[0:D])
    store_shares(dot(turned[0:D, :], ups[...]), size_w, keep, send, 2 * D)
    out_s[...] = (residual + dot(inner[...], wd[...])).astype(BF16)
    written = move.start((out_s, out_h))
    g_two = dot_nt(ups[...], wu[...])
    fgain_ref[...] = jnp.sum(g_two * n, axis=0, keepdims=True)
    h = g_two * par_ref[49:50, :]
    g_res = cot[...].astype(F32) + inv * (
        h - jnp.mean(h, axis=-1, keepdims=True) - n * jnp.mean(h * n, axis=-1, keepdims=True)
    )
    gate = gat[...]
    s = sigmoid(hm)
    gcol[:, 0:D] = (g_res * (hm * s - x) * gate * (1.0 - gate)).astype(BF16)
    gcol[:, D : 2 * D] = (g_res * gate * (s * (1.0 + hm * (1.0 - s)))).astype(BF16)
    dir_s[...] = g_res * (1.0 - gate)
    wait_all(written)


def back_kernel(
    blocks,
    size_w,
    me_ref,
    qk_ref,
    gcol,
    rg,
    ra,
    val,
    prob,
    k_s,
    q_s,
    sh,
    ssl,
    vsl,
    act,
    wm,
    gqk_ref,
    keep,
    send,
    gproj,
    gval,
    gatt,
    turned,
):
    me = me_ref[0]
    gp = dot_nt(gcol[:, D : 2 * D], wm[...])
    gatt[...] = (gp * rg[...].astype(F32)).astype(BF16)
    gproj[:, D + Z : D + Z + VALUE_WIDTH] = (gp * ra[...].astype(F32)).astype(BF16)
    gproj[:, 0:D] = gcol[:, 0:D]
    gproj[:, D + Z + VALUE_WIDTH :] = gcol[:, D : 2 * D]
    sums = [jnp.zeros((1, Z), F32)] * 3
    for b in range(blocks):
        rows = slice(b * BLOCK_TOKENS, (b + 1) * BLOCK_TOKENS)
        p = prob[rows, :]
        g_att = gatt[rows, :]
        g_probs = dot_nt(g_att, val[rows, :])
        g_values = dot(p.T.astype(BF16), g_att)
        gval[rows, :] = (g_values * vsl[rows, :].astype(F32)).astype(BF16)
        g_scores = p * (g_probs - jnp.sum(g_probs * p, axis=-1, keepdims=True))
        g_raw = g_scores * SCALE
        g_q = dot(g_raw.astype(BF16), k_s[rows, :])
        g_k = dot(g_raw.T.astype(BF16), q_s[rows, :])
        shared = sh[rows, :]
        for i, term in enumerate((g_q * shared, g_q, g_k * shared)):
            sums[i] = sums[i] + jnp.sum(term, axis=0, keepdims=True)
        g_shared = g_q * qk_ref[0:1, :] + g_k * qk_ref[2:3, :]
        gproj[rows, D : D + Z] = (g_shared * ssl[rows, :]).astype(BF16)
    gqk_ref[...] = jnp.concatenate(sums + [jnp.zeros((5, Z), F32)], axis=0)
    shard_transpose(act, me, size_w, turned)
    split = D + Z + D
    store_shares(dot(turned[...], gproj[:, 0:split]), size_w, keep, send, 0)
    store_shares(dot(turned[...], gproj[:, split:]), size_w, keep, send, split)


def back_rest_kernel(size_w, me_ref, mlow, gcol, low, gval, gproj, wp, wv, keep, send, gact, gnv, turned):
    me = me_ref[0]
    shard_transpose(mlow, me, size_w, turned)
    store_shares(dot(turned[...], gcol[:, D : 2 * D]), size_w, keep, send, 0, True)
    shard_transpose(low, me, size_w, turned.at[0:D])
    store_shares(dot(turned[0:D, :], gval[...]), size_w, keep, send, 2 * D)
    gact[...] = dot_nt(gproj[...], wp[...])
    gnv[...] = dot_nt(gval[...], wv[...])


def adjoint_kernel(run, blocks, gact_ref, pre_ref, nrm_ref, par_ref, cont, head, gmix_ref, gn_ref, lead_ref, pay_ref, gs_ref, gs, os, sums):
    normed = nrm_ref[...]
    g_mix = gact_ref[...] * swish_slope(pre_ref[...])
    gmix_ref[...] = g_mix
    gs_ref[...] = jnp.sum(g_mix * normed, axis=0, keepdims=True)
    put_runs(gs, g_mix, run)
    decay, rate, width = decay_tables(par_ref)
    gain = par_ref[32:48, :] * width * par_ref[16:32, :]
    rate_run = power_of_rate(decay, run)
    head_end = at_step(head, run - 1)
    zero = jnp.zeros((PARTS, LANES), F32)
    for g in range(GROUPS):
        rates = [spread(rate, j, g) for j in range(NDIM)]
        gains = [spread(gain, j, g) for j in range(NDIM)]

        def back(i, carries, g=g, rates=rates, gains=gains):
            t = run - 1 - i
            g_t = at_step(gs, t, g)
            c_t = at_step(cont, t)
            bs = [g_t + carries[j] for j in range(NDIM)]
            set_step(os, t, g, tree_sum([gains[j] * bs[j] for j in range(NDIM)]))
            return tuple((c_t * rates[j]) * bs[j] for j in range(NDIM))

        ends = lax.fori_loop(0, run, back, (zero,) * NDIM, unroll=16)
        for j in range(NDIM):
            lead_ref[state_rows(j, g), :] = ends[j]
            sums[state_rows(j, g), :] = ends[j] + head_end * spread(rate_run, j, g) * pltpu.roll(ends[j], PARTS - 1, 0)
    gn_ref[...] = get_runs(os, run) + par_ref[50:51, :] * g_mix
    per_block = PARTS // blocks
    for b in range(blocks):
        pay_ref[0, b] = sums[pl.ds(b * per_block, STATES, stride=PARTS), :].astype(BF16)


def slope_kernel(run, gmix_ref, nrm_ref, ein_ref, par_ref, cont, u_ref, v_ref, ve_ref, xs, gs):
    put_runs(xs, nrm_ref[...], run)
    put_runs(gs, gmix_ref[...], run)
    _, rate, _ = decay_tables(par_ref)
    zero = jnp.zeros((PARTS, LANES), F32)
    half = NDIM // 2
    for g in range(GROUPS):
        rates = [spread(rate, j, g) for j in range(NDIM)]
        for first in (0, half):
            picks = range(first, first + half)

            def ahead(t, carry, g=g, picks=picks, rates=rates):
                us, vs, uacc, vacc = carry
                g_t = at_step(gs, t, g)
                x_t = at_step(xs, t, g)
                c_t = at_step(cont, t)
                nu, nv, nua, nva = [], [], [], []
                for i, j in enumerate(picks):
                    r = c_t * rates[j]
                    v = r * vs[i] + c_t * us[i]
                    u = r * us[i] + x_t
                    nu.append(u)
                    nv.append(v)
                    nua.append(uacc[i] + g_t * u)
                    nva.append(vacc[i] + g_t * v)
                return tuple(nu), tuple(nv), tuple(nua), tuple(nva)

            us = tuple(ein_ref[state_rows(j, g), :] for j in picks)
            zeros = (zero,) * half
            us, vs, uacc, vacc = lax.fori_loop(0, run, ahead, (us, zeros, zeros, zeros), unroll=16)
            for i, j in enumerate(picks):
                u_ref[state_rows(j, g), :] = uacc[i]
                v_ref[state_rows(j, g), :] = vacc[i]
                ve_ref[state_rows(j, g), :] = vs[i]


def finish_kernel(run, blocks, keys, me_ref, order_ref, *refs):
    n = len(keys)
    back_refs = refs[:n]
    finish(run, blocks, keys, me_ref, order_ref, back_refs, *refs[n:])


def finish(run, blocks, keys, me_ref, order_ref, back_refs, bnd_ref, far_ref, gn_ref, gnv_ref, lead_ref, u_ref, v_ref, ve_ref, tok_ref, dir_ref, par_ref, head, tail, gs_ref, fg_ref, gqk_ref, ig_ref, small_ref, os, table, place, kept, gathered):
    for ref, ks in zip(back_refs, keys):
        for i, k in enumerate(ks):
            gathered[me_ref[1] ^ k] = ref[i].astype(F32)

    def fetch(pos):
        return gathered[pos // blocks, pos % blocks]

    scan_states(me_ref, order_ref, fetch, bnd_ref, far_ref, table, place, kept, blocks, False)
    decay, rate, width = decay_tables(par_ref)
    drive_in = par_ref[16:32, :]
    readout = par_ref[32:48, :]
    drive = width * drive_in
    gain = readout * drive
    rate_run = power_of_rate(decay, run)
    head_after = pltpu.roll(at_step(head, run - 1), PARTS - 1, 0)
    per_block = PARTS // blocks
    final = lax.broadcasted_iota(jnp.int32, (PARTS, LANES), 0) % per_block == per_block - 1
    u_rows, v_rows = [], []
    for g in range(GROUPS):
        rates = [spread(rate, j, g) for j in range(NDIM)]
        start = []
        u_list, v_list = [], []
        for j in range(NDIM):
            at = state_rows(j, g)
            que = table[at, :]
            inward = pltpu.roll(lead_ref[at, :], PARTS - 1, 0) + head_after * spread(rate_run, j, g) * que
            que = jnp.where(final, que, inward)
            start.append(que * spread(gain, j, g))
            u_list.append(jnp.sum(u_ref[at, :], axis=0, keepdims=True))
            v_list.append(jnp.sum(v_ref[at, :] + que * ve_ref[at, :], axis=0, keepdims=True))
        u_rows.append(jnp.concatenate(u_list, axis=0))
        v_rows.append(jnp.concatenate(v_list, axis=0))

        def step(i, states, g=g, rates=rates):
            t = run - 1 - i
            set_step(os, t, g, tree_sum(states) * at_step(tail, t))
            return tuple(rates[j] * states[j] for j in range(NDIM))

        lax.fori_loop(0, run, step, tuple(start), unroll=16)
    u_all = jnp.concatenate(u_rows, axis=1)
    v_all = jnp.concatenate(v_rows, axis=1)
    g_normed = gn_ref[...] + gnv_ref[...] + get_runs(os, run)
    x = tok_ref[...].astype(F32)
    centred = x - jnp.mean(x, axis=-1, keepdims=True)
    var = jnp.mean(centred * centred, axis=-1, keepdims=True)
    inv = lax.rsqrt(var + EPS)
    n = centred * inv
    h = g_normed * par_ref[48:49, :]
    back = inv * (h - jnp.mean(h, axis=-1, keepdims=True) - n * jnp.mean(h * n, axis=-1, keepdims=True))
    ig_ref[...] = (dir_ref[...] + back).astype(BF16)
    size_w = 2 * small_ref.shape[1]
    half = size_w // 2
    part = small_ref.shape[3]
    zpart = Z // size_w
    me = me_ref[0]
    grads = jnp.concatenate(
        [
            readout * drive * v_all * rate * (1.0 - rate)
            - readout * u_all * drive_in * rate * rate * (1.0 - rate) / width,
            readout * u_all * width,
            drive * u_all,
            jnp.sum(g_normed * n, axis=0, keepdims=True),
            fg_ref[...],
            gs_ref[...],
            jnp.zeros((5, D), F32),
        ],
        axis=0,
    )
    for w in range(size_w):
        p = me ^ w
        qk = gqk_ref[0:8, w * zpart : (w + 1) * zpart]
        if zpart < part:
            qk = jnp.concatenate([qk, jnp.zeros((8, part - zpart), F32)], axis=1)
        both = jnp.concatenate([grads[:, w * part : (w + 1) * part], qk], axis=0)
        small_ref[p & 1, p >> 1] = both.astype(BF16)


def swap(value, axis, bit):
    size = lax.axis_size(axis)
    return lax.ppermute(value, axis, [(i, i ^ bit) for i in range(size)])


def bits_of(size):
    out, bit = [], 1
    while bit < size:
        out.append(bit)
        bit *= 2
    return out


def tie(*values):
    return lax.optimization_barrier(values)


class Share:
    def __init__(self, terms, count, cols):
        self.terms = terms
        self.count = count
        self.cols = cols

    def halve(self, level):
        count = self.count // 2

        def moved(first, other):
            return lambda me: first(me) + (((me >> level) & 1) ^ other) * count

        stay = Share([(a, i, moved(f, 0), c) for a, i, f, c in self.terms], count, self.cols)
        go = Share([(a, i, moved(f, 1), c) for a, i, f, c in self.terms], count, self.cols)
        return stay, go

    def plus(self, array, lead=(), col=0):
        return Share(self.terms + [(array, lead, lambda me: 0, col)], self.count, self.cols)


def plain_sum(share, me):
    total = None
    for array, lead, first, col in share.terms:
        for i in lead:
            array = array[i]
        array = lax.dynamic_slice_in_dim(array, first(me), share.count, 0)[:, :, col : col + share.cols].astype(F32)
        total = array if total is None else total + array
    return total.astype(BF16)


def sum_kernel(plan, n, *refs):
    me = refs[0][1]
    arrays = refs[1 : 1 + n]
    outs = refs[1 + n :]
    for out, stacked in zip(outs, plan):
        for i, row in enumerate(stacked):
            column = 0
            for terms, count, cols in row:
                total = None
                for k, lead, first, col in terms:
                    value = arrays[k][(*lead, pl.ds(first(me), count), slice(None), slice(col, col + cols))].astype(F32)
                    total = value if total is None else total + value
                out[i, :, :, column : column + cols] = total.astype(BF16)
                column += cols


def sums(where, *outputs):
    first = outputs[0][0][0]
    rows = first.terms[0][0].shape[-2]
    if rows % 8:
        return [
            jnp.stack([jnp.concatenate([plain_sum(share, where[1]) for share in row], axis=2) for row in stacked])
            for stacked in outputs
        ]
    arrays, plan, shapes = [], [], []
    for stacked in outputs:
        rows_plan = []
        for row in stacked:
            row_plan = []
            for share in row:
                terms = []
                for array, lead, start, col in share.terms:
                    k = next((k for k, a in enumerate(arrays) if a is array), None)
                    if k is None:
                        k = len(arrays)
                        arrays.append(array)
                    terms.append((k, lead, start, col))
                row_plan.append((terms, share.count, share.cols))
            rows_plan.append(row_plan)
        plan.append(rows_plan)
        shapes.append(pltpu.VMEM((len(stacked), stacked[0][0].count, rows, sum(s.cols for s in stacked[0])), BF16))
    return pl.pallas_call(
        functools.partial(sum_kernel, plan, len(arrays)),
        out_shape=tuple(shapes),
        in_specs=[SM] + [VM] * len(arrays),
        out_specs=(VM,) * len(shapes),
        cost_estimate=cost(1),
        compiler_params=room(12),
        name="sums",
    )(where, *[resident(array) for array in arrays])


def far_keys(size):
    keys = []
    for bit in reversed(bits_of(size)[1:]):
        keys += [k | bit for k in [0] + keys]
    return keys


def position(place, order):
    out = 0
    for i, level in enumerate(order):
        out = out | (((place >> level) & 1) << (len(order) - 1 - i))
    return out


def place_kernel(keys, order, spans, *refs):
    n = len(keys)
    me = refs[0][1]
    pieces = refs[1 : 1 + n]
    outs = refs[1 + n :]
    for ref, ks in zip(pieces, keys):
        rows = ref.shape[1]
        for i, k in enumerate(ks):
            base = position(me ^ k, order) * rows
            for out, (start, tall) in zip(outs, spans):
                width = out.shape[1]
                for s in range(2 if tall else 1):
                    at = pl.ds(pl.multiple_of(base + s * (out.shape[0] // 2), rows), rows)
                    out[at, :] = ref[i, :, start + s * width : start + (s + 1) * width].astype(F32)


def place(levels, keys, order, where, spans, shapes, name):
    rows = levels[0].shape[1]
    if rows % 8:
        return place_by_gather(levels, keys, order, where, spans, shapes)
    return pl.pallas_call(
        functools.partial(place_kernel, keys, order, spans),
        out_shape=tuple(shaped(s) for s in shapes),
        in_specs=[SM] + [VM] * len(levels),
        cost_estimate=cost(0.1),
        compiler_params=room(16),
        name=name,
    )(where, *[resident(level) for level in levels])


def place_part_kernel(keys, order, spans, given, *refs):
    n = len(keys)
    me = refs[0][1]
    pieces = refs[1 : 1 + n]
    outs = refs[1 + n + given : 1 + n + given + len(spans)]
    wide, sems = refs[-2:]
    move = Mover(sems)
    copies, at = [], 0
    for ref, ks in zip(pieces, keys):
        rows = ref.shape[1]
        for i, k in enumerate(ks):
            wide[at] = ref[i].astype(F32)
            base = position(me ^ k, order) * rows
            for out, (start, tall) in zip(outs, spans):
                width = out.shape[1]
                for s in range(2 if tall else 1):
                    where = pl.ds(pl.multiple_of(base + s * (out.shape[0] // 2), rows), rows)
                    source = wide.at[at, :, start + s * width : start + (s + 1) * width]
                    copies += move.start((source, out.at[where, :]))
            at += 1
    wait_all(copies)


def place_part(levels, keys, order, where, spans, shapes, given, name):
    count = sum(map(len, keys))
    rows, cols = levels[0].shape[1:]
    return pl.pallas_call(
        functools.partial(place_part_kernel, keys, order, spans, len(given)),
        out_shape=tuple(pltpu.HBM(s, F32) for s in shapes),
        in_specs=[SM] + [VM] * len(levels) + [HBM] * len(given),
        out_specs=(HBM,) * len(shapes),
        input_output_aliases={1 + len(levels) + i: i for i in range(len(given))},
        scratch_shapes=[
            pltpu.VMEM((count, rows, cols), F32),
            pltpu.SemaphoreType.DMA((count * sum(2 if tall else 1 for _, tall in spans),)),
        ],
        cost_estimate=cost(0.1 if given else 4.0),
        compiler_params=room(16),
        name=name,
    )(where, *[resident(level) for level in levels], *given)


def place_by_gather(levels, keys, order, where, spans, shapes):
    flat = [k for level in keys for k in level]
    index = jnp.array([flat.index(k) for k in range(len(flat))], jnp.int32)
    holder = {position(device, order): device for device in range(len(flat))}
    picks = index[where[1] ^ jnp.array([holder[i] for i in range(len(flat))], jnp.int32)]
    block = jnp.concatenate(levels, axis=0)[picks].astype(F32)
    block = block.reshape(-1, block.shape[-1])
    outs = []
    for (start, tall), (rows, width) in zip(spans, shapes):
        columns = [block[:, start + s * width : start + (s + 1) * width] for s in range(2 if tall else 1)]
        outs.append(jnp.concatenate(columns, axis=0))
    return tuple(outs)


def body(
    tokens,
    segments,
    deal_order,
    cotangent,
    proj_weight,
    value_weight,
    merge_weight,
    ffn_up,
    ffn_down,
    norm_gain,
    ffn_gain,
    skip_gain,
    ema_decay,
    ema_input,
    ema_output,
    query_key,
):
    size_w, size_c = lax.axis_size("wsh"), lax.axis_size("ctx")
    me_w, me_c = lax.axis_index("wsh"), lax.axis_index("ctx")
    where = jnp.stack([me_w, me_c]).astype(jnp.int32)
    wbits, cbits = bits_of(size_w), bits_of(size_c)
    part = D // size_w
    zpart = Z // size_w
    half = size_w // 2
    rc = tokens.shape[1]
    blocks = rc // BLOCK_TOKENS
    run = rc // PARTS
    count = deal_order.shape[0]
    shards = (proj_weight, value_weight, merge_weight, ffn_up, ffn_down)
    group_cols = [sum(travel_cols(w) for w in group) for group in TRAVEL]

    small = pl.pallas_call(small_kernel, out_shape=shaped((SMALL_ROWS, part), BF16), cost_estimate=cost(1), compiler_params=room(60), name="small")(
        ema_decay.T,
        ema_input.T,
        ema_output.T,
        norm_gain[None],
        ffn_gain[None],
        skip_gain[None],
        query_key.T,
    )
    travel = pl.pallas_call(
        pack_kernel,
        out_shape=tuple(
            shaped((part if level is None else part // 2, c), BF16) for c, level in zip(group_cols, TRAVEL_LEVEL)
        ),
        in_specs=[SM] + [HBM] * 5,
        scratch_shapes=[pltpu.SemaphoreType.DMA((16,))],
        cost_estimate=cost(3),
        compiler_params=room(8),
        name="pack",
    )(where, *shards)

    def far_pieces(block):
        have = []
        for bit in reversed(wbits[1:]):
            sent = jnp.concatenate([block[None]] + have, axis=0) if have else block[None]
            have.append(swap(sent, "wsh", bit))
        return have[0] if len(have) == 1 else jnp.concatenate(have, axis=0)

    wkeys = far_keys(size_w)
    small_near = swap(small[None], "wsh", 1)
    small_far = far_pieces(small)
    small_far, *travel = tie(small_far, *travel)
    near = [far_pieces(block) for block in travel]
    small_last = swap(small_far, "wsh", 1)
    skeys = [[0], [1], wkeys, [k | 1 for k in wkeys]]

    pad_run = run + 1
    runs_scratch = pltpu.VMEM((GROUPS, PARTS * pad_run, LANES), F32)
    mask_shape = shaped((PARTS * pad_run, LANES))
    kept_scratch = pltpu.VMEM((count, STATES, LANES), F32)
    table_scratch = pltpu.VMEM((STATES * PARTS, LANES), F32)
    table = shaped((STATES * PARTS, LANES))
    par, qk, ends, payload, far, normed, mix_local, cont, head, tail, label_cols = pl.pallas_call(
        functools.partial(front_kernel, skeys, run, blocks),
        out_shape=(
            shaped((SMALL_ROWS, D)),
            shaped((8, Z)),
            table,
            shaped((size_c, blocks, STATES + 8, LANES), BF16),
            shaped((STATES, LANES)),
            shaped((rc, D)),
            shaped((rc, D)),
            mask_shape,
            mask_shape,
            mask_shape,
            shaped((rc, LANES)),
        ),
        in_specs=[SM] + [VM] * 6,
        scratch_shapes=[
            runs_scratch,
            runs_scratch,
            table_scratch,
            pltpu.VMEM((size_w, SMALL_ROWS, part), F32),
        ],
        cost_estimate=cost(FRONT),
        compiler_params=room(60),
        name="front",
    )(where, tokens[0], segments, small[None], small_near, small_far, small_last)
    got = lax.all_to_all(payload, "ctx", 0, 0, tiled=True).reshape(count, STATES + 8, LANES)

    for i in range(len(TRAVEL)):
        near[i] = tie(payload, near[i])[1]
    across = [
        None if level is None else swap(piece, "ctx", 1 << level) for piece, level in zip(near, TRAVEL_LEVEL)
    ]
    for i, level in enumerate(TRAVEL_LEVEL):
        if level is None:
            _, near[i] = tie(across[0], near[i])
    near_other = [swap(piece, "wsh", 1) for piece in near]
    gate = pl.pallas_call(
        gate_kernel,
        out_shape=shaped((8, LANES)),
        in_specs=[ANY] * sum(b is not None for b in across),
        cost_estimate=cost(GATE),
        compiler_params=room(1),
        name="gate",
    )(*[b for b in across if b is not None])
    tied = tie(payload, *shards)
    packed_own = pl.pallas_call(
        pack_own_kernel,
        out_shape=shaped((part, sum(travel_cols(w) for w in range(len(WEIGHTS)))), BF16),
        cost_estimate=cost(2),
        compiler_params=room(60),
        name="pack_own",
    )(*tied[1:])
    own_other = swap(packed_own, "wsh", 1)
    travelled = [
        (a, c) if b is None else (a, b, c, swap(b, "wsh", 1)) for a, b, c in zip(near, across, near_other)
    ]

    entered = pl.pallas_call(
        functools.partial(scan_kernel, blocks),
        out_shape=table,
        in_specs=[SM, SM, VM, VM],
        scratch_shapes=[pltpu.SMEM((count,), jnp.int32), kept_scratch],
        cost_estimate=cost(SCAN),
        compiler_params=room(8),
        name="scan",
    )(where, deal_order, got, far)

    saved = (
        shaped((half, part, 2 * D + FF), BF16),
        shaped((half, part, 2 * D + FF), BF16),
        shaped((rc, D)),
        shaped((rc, D), BF16),
        shaped((rc, D), BF16),
        shaped((rc, VALUE_WIDTH), BF16),
        shaped((rc, 2 * D), BF16),
        shaped((rc, D)),
        shaped((rc, VALUE_WIDTH), BF16),
        shaped((rc, VALUE_WIDTH), BF16),
        shaped((rc, VALUE_WIDTH), BF16),
        shaped((rc, VALUE_WIDTH), BF16),
        shaped((rc, BLOCK_TOKENS)),
        shaped((rc, Z), BF16),
        shaped((rc, Z), BF16),
        shaped((rc, Z)),
        shaped((rc, Z)),
        shaped((D, PROJ), BF16),
        shaped((D, VALUE_WIDTH), BF16),
        shaped((VALUE_WIDTH, D), BF16),
    )

    def held(*shapes):
        return tuple(pltpu.VMEM(s.shape, s.dtype) for s in shapes)

    copies_each = 2 + 4 * len(wkeys)
    results = pl.pallas_call(
        functools.partial(layer_kernel, wkeys, run, blocks, size_w),
        out_shape=(pltpu.HBM((rc, D), BF16), table, shaped((1, D))) + held(*saved),
        in_specs=[SM] + [VM] * 12 + [HBM] * 5 + [ANY] * (1 + sum(map(len, travelled))),
        out_specs=(HBM, VM, VM) + (VM,) * len(saved),
        scratch_shapes=[
            pltpu.VMEM((rc, D), BF16),
            runs_scratch,
            pltpu.VMEM((D, FF), BF16),
            pltpu.VMEM((FF, D), BF16),
            pltpu.VMEM((rc, D), F32),
            pltpu.VMEM((rc, D), F32),
            pltpu.VMEM((rc, D), BF16),
            pltpu.VMEM((rc, FF), BF16),
            pltpu.VMEM((rc, FF), BF16),
            pltpu.VMEM((FF, rc), BF16),
            pltpu.SemaphoreType.DMA((1 + 7 * (copies_each + 1),)),
        ],
        cost_estimate=cost(17),
        compiler_params=room(32),
        name="layer",
    )(
        where,
        entered,
        ends,
        par,
        qk,
        head,
        label_cols,
        segments,
        gate,
        *map(resident, (mix_local, normed, tokens[0], cotangent[0])),
        *map(in_hbm, shards),
        own_other,
        *[piece for group in travelled for piece in group],
    )
    output, ein, grad_ffn_gain = results[:3]
    (
        ffn_keep,
        ffn_send,
        pre_active,
        active_low,
        normed_low,
        merged_low,
        gcols,
        direct,
        reset_gate,
        reset_slope,
        values,
        value_slope,
        probs,
        queries,
        keys_low,
        shared_slope,
        shared,
        proj_full,
        value_full,
        merge_full,
    ) = results[3:]

    def shares_of(keep, got):
        cut = (half, size_c, keep.shape[1] // size_c, keep.shape[2])
        keep, got = keep.reshape(cut), got.reshape(cut)
        return [
            Share([(keep, (i,), lambda me: 0, 0), (got, (i,), lambda me: 0, 0)], size_c, cut[3]) for i in range(half)
        ]

    def plus_all(shares, got, first=0):
        return [share.plus(got, (first + i,)) for i, share in enumerate(shares)]

    def rows_of(shares):
        return [[share] for share in shares]

    def widen(levels, keys, bit):
        block = levels[0] if len(levels) == 1 else jnp.concatenate(levels, axis=0)
        return levels + [swap(block, "ctx", bit)], keys + [[k | bit for level in keys for k in level]]

    f_got = swap(ffn_send, "wsh", 1)
    gproj_shape, gval_shape = shaped((rc, PROJ), BF16), shaped((rc, VALUE_WIDTH), BF16)
    p_shape = shaped((half, part, PROJ), BF16)
    grad_qk, p_keep, p_send, gproj, gval = pl.pallas_call(
        functools.partial(back_kernel, blocks, size_w),
        out_shape=(shaped((8, Z)),) + held(p_shape, p_shape, gproj_shape, gval_shape),
        in_specs=[SM] + [VM] * 13,
        scratch_shapes=held(gval_shape, shaped((D, rc), BF16)),
        cost_estimate=cost(9),
        compiler_params=room(20),
        name="back",
    )(
        where,
        qk,
        *map(
            resident,
            (
                gcols,
                reset_gate,
                reset_slope,
                values,
                probs,
                keys_low,
                queries,
                shared,
                shared_slope,
                value_slope,
                active_low,
                merge_full,
            ),
        ),
    )
    p_got = swap(p_send, "wsh", 1)
    gproj = tie(p_send, gproj)[1]
    q_shape = shaped((half, part, 2 * D + VALUE_WIDTH), BF16)
    q_keep, q_send, grad_active, grad_normed_value = pl.pallas_call(
        functools.partial(back_rest_kernel, size_w),
        out_shape=held(q_shape, q_shape, shaped((rc, D)), shaped((rc, D))),
        in_specs=[SM] + [VM] * 7,
        scratch_shapes=[pltpu.VMEM((VALUE_WIDTH, rc), BF16)],
        cost_estimate=cost(7),
        compiler_params=room(20),
        name="back_rest",
    )(where, *map(resident, (merged_low, gcols, normed_low, gval, gproj, proj_full, value_full)))

    top = len(cbits)
    pq_rounds = [(("w", k), ("c", 0) if k == 0 else ("w", k - 1)) for k in range(len(wbits) - 1)]
    pq_rounds.append((("c", 0), ("w", len(wbits) - 2)))
    r_order = [0] + list(range(1, top))
    f_steps = [("c", 1)] + [("w", k) for k in range(len(wbits) - 1)]
    f_steps += [("c", k) for k in range(2, top)] + [("c", 0)]
    f_order = list(range(1, top)) + [0]

    def cut(shares, step):
        kind, k = step
        if kind == "w":
            return shares[0::2], rows_of(shares[1::2])
        both = [share.halve(k) for share in shares]
        return [stay for stay, _ in both], rows_of([away for _, away in both])

    def send(value, step):
        kind, k = step
        return swap(value, "wsh", wbits[k + 1]) if kind == "w" else swap(value, "ctx", cbits[k])

    p_shares, f_shares = shares_of(p_keep, p_got), shares_of(ffn_keep, f_got)
    p_shares, p_rows = cut(p_shares, pq_rounds[0][0])
    f_shares, f_rows = cut(f_shares, f_steps[0])
    p_go, f_go = sums(where, p_rows, f_rows)
    p_go, f_go, q_send = tie(p_go, f_go, q_send)
    q_got = swap(q_send, "wsh", 1)
    p_got, f_got = send(p_go, pq_rounds[0][0]), send(f_go, f_steps[0])
    q_shares, q_rows = cut(shares_of(q_keep, q_got), pq_rounds[0][1])
    (q_go,) = sums(where, q_rows)
    q_go, grad_active = tie(q_go, grad_active)
    q_got = send(q_go, pq_rounds[0][1])
    g_mix, gn_local, leads, payload_back, grad_skip = pl.pallas_call(
        functools.partial(adjoint_kernel, run, blocks),
        out_shape=(
            shaped((rc, D)),
            shaped((rc, D)),
            table,
            shaped((1, blocks, STATES, LANES), BF16),
            shaped((1, D)),
        ),
        scratch_shapes=[runs_scratch] * 2 + [table_scratch],
        cost_estimate=cost(ADJOINT),
        compiler_params=room(20),
        name="adjoint",
    )(grad_active, pre_active, normed, par, cont, head)
    b_levels, b_keys = [payload_back], [[0]]
    for bit in reversed(cbits[3:]):
        b_levels, b_keys = widen(b_levels, b_keys, bit)
    block = b_levels[0] if len(b_levels) == 1 else jnp.concatenate(b_levels, axis=0)
    flat = [k for level in b_keys for k in level]
    b_keys += [[k | bit for k in flat] for bit in (cbits[1] | cbits[2], cbits[2], cbits[1])]
    b_levels += [swap(block, "ctx", bit) for bit in (cbits[1] | cbits[2], cbits[2])]
    u_part, v_part, v_end = pl.pallas_call(
        functools.partial(slope_kernel, run),
        out_shape=(table, table, table),
        scratch_shapes=[runs_scratch] * 2,
        cost_estimate=cost(SLOPE),
        compiler_params=room(16),
        name="slope",
    )(g_mix, normed, ein, par, cont)
    block, u_part = tie(block, u_part)
    b_last = swap(block, "ctx", cbits[1])

    p_got, q_got, f_got, u_part, *b_levels = tie(p_got, q_got, f_got, u_part, *b_levels)
    b_levels.append(b_last)
    p_shares, q_shares, f_shares = plus_all(p_shares, p_got), plus_all(q_shares, q_got), plus_all(f_shares, f_got)
    for number in range(1, len(pq_rounds)):
        p_step, q_step = pq_rounds[number]
        f_step = f_steps[number]
        p_shares, p_rows = cut(p_shares, p_step)
        q_shares, q_rows = cut(q_shares, q_step)
        f_shares, f_rows = cut(f_shares, f_step)
        together = q_step == f_step
        if together:
            p_go, q_go = sums(where, p_rows, q_rows + f_rows)
            p_go, q_go, b_levels[-2] = tie(p_go, q_go, b_levels[-2])
            p_got, q_got = send(p_go, p_step), send(q_go, q_step)
            f_got = q_got
        else:
            p_go, q_go, f_go = sums(where, p_rows, q_rows, f_rows)
            p_go, q_go, f_go, b_levels[-2] = tie(p_go, q_go, f_go, b_levels[-2])
            p_got, q_got, f_got = send(p_go, p_step), send(q_go, q_step), send(f_go, f_step)
        if number == 1:
            b_levels, b_keys = widen(b_levels, b_keys, 1)
        p_got, q_got, f_got, b_levels[-1] = tie(p_got, q_got, f_got, b_levels[-1])
        if together:
            f_got = q_got
        p_shares, q_shares = plus_all(p_shares, p_got), plus_all(q_shares, q_got)
        f_shares = plus_all(f_shares, f_got, len(q_rows) if together else 0)
    (p_share,), (q_share,) = p_shares, q_shares

    def finished():
        input_grad, small_share = pl.pallas_call(
            functools.partial(finish_kernel, run, blocks, b_keys),
            out_shape=(shaped((rc, D), BF16), shaped((2, half, SMALL_ROWS + 8, part), BF16)),
            in_specs=[SM, SM] + [VM] * (16 + len(b_keys)),
            scratch_shapes=[
                runs_scratch,
                table_scratch,
                pltpu.SMEM((count,), jnp.int32),
                kept_scratch,
                pltpu.VMEM((size_c, blocks, STATES, LANES), F32),
            ],
            cost_estimate=cost(FINISH),
            compiler_params=room(20),
            name="finish",
        )(
            where,
            deal_order,
            *b_levels,
            got,
            far,
            gn_local,
            grad_normed_value,
            leads,
            u_part,
            v_part,
            v_end,
            tokens[0],
            direct,
            par,
            head,
            tail,
            grad_skip,
            grad_ffn_gain,
            grad_qk,
        )
        return input_grad, small_share

    late = None
    for k in range(1, top):
        f_step = f_steps[len(pq_rounds) + k - 1]
        p_share, p_away = p_share.halve(k)
        q_share, q_away = q_share.halve(k)
        f_shares, f_rows = cut(f_shares, f_step)
        r_go, f_go = sums(where, [[p_away, q_away]], f_rows)
        if k == 1:
            r_go, f_go, b_levels[-1] = tie(r_go, f_go, b_levels[-1])
        else:
            r_go, f_go, late = tie(r_go, f_go, late)
        r_got, f_got = swap(r_go, "ctx", cbits[k]), send(f_go, f_step)
        if k == 1:
            input_grad, late = finished()
            r_got, f_got, late = tie(r_got, f_got, late)
            late = late[0].astype(F32) + swap(late[1], "wsh", 1).astype(F32)
        elif k == 2:
            for wbit in wbits[1:]:
                late = late[0::2] + swap(late[1::2].astype(BF16), "wsh", wbit).astype(F32)
            r_got, f_got, late = tie(r_got, f_got, late)
        p_share, q_share = p_share.plus(r_got, (0,)), q_share.plus(r_got, (0,), PROJ)
        f_shares = plus_all(f_shares, f_got)
    r_own, f_own = sums(where, [[p_share, q_share]], rows_of(f_shares))
    r_own, f_own, late = tie(r_own, f_own, late)
    r_levels, r_keys, f_levels, f_keys = [r_own[0]], [[0]], [f_own[0]], [[0]]
    s_steps = list(range(top))
    s_pieces = late

    def small_step(pieces, level):
        low = pieces.astype(BF16)
        return low.astype(F32) + swap(low, "ctx", cbits[level]).astype(F32)

    depth = merge_weight.shape[0]
    rest_spans = ((0, False), (PROJ, True), (PROJ + 2 * D, False))
    rest_shapes = ((part, PROJ), (depth, D), (part, VALUE_WIDTH))
    in_parts = r_levels[0].shape[1] % 8 == 0
    given = ()
    for number, (r_bit, f_bit) in enumerate(zip(reversed(cbits), [1] + cbits[:0:-1])):
        if r_bit == 1 and in_parts:
            given = place_part(r_levels, r_keys, r_order, where, rest_spans, rest_shapes, (), "place_first")
            head_part, f_levels[-1], s_pieces = tie(given[0], f_levels[-1], s_pieces)
            given = (head_part,) + tuple(given[1:])
        r_levels, r_keys = widen(r_levels, r_keys, r_bit)
        f_levels, f_keys = widen(f_levels, f_keys, f_bit)
        todo = len(s_steps) // (top - number)
        for step in s_steps[:todo]:
            s_pieces = small_step(s_pieces, step)
        s_steps = s_steps[todo:]
        if r_bit > 1:
            r_last, f_last, s_pieces = tie(r_levels[-1], f_levels[-1], s_pieces)
            r_levels, f_levels = r_levels[:-1] + [r_last], f_levels[:-1] + [f_last]
    small_total = s_pieces[0]
    grad_down, grad_up = place(
        f_levels, f_keys, f_order, where, ((0, True), (2 * D, False)), ((depth, D), (part, FF)), "place_ffn"
    )
    if in_parts:
        grad_proj, grad_merge, grad_value = place_part(
            r_levels[-1:], r_keys[-1:], r_order, where, rest_spans, rest_shapes, given, "place_rest"
        )
    else:
        grad_proj, grad_merge, grad_value = place_by_gather(
            r_levels, r_keys, r_order, where, rest_spans, rest_shapes
        )
    return (
        output[None],
        input_grad[None],
        grad_proj,
        grad_value,
        grad_merge,
        grad_up,
        grad_down,
        small_total[48],
        small_total[49],
        small_total[50],
        small_total[0:16].T,
        small_total[16:32].T,
        small_total[32:48].T,
        small_total[56:59, :zpart].T,
    )


def solution(mesh):
    rows, flat = P("wsh", None), P("wsh")
    sequence = P("wsh", "ctx", None)
    placed = (sequence, P("wsh", "ctx"), P(), sequence) + (rows,) * 5 + (flat,) * 3 + (rows,) * 4
    return jax.shard_map(
        body,
        mesh=mesh,
        in_specs=placed,
        out_specs=(sequence, sequence) + (rows,) * 5 + (flat,) * 3 + (rows,) * 4,
        check_vma=False,
    )
```
